32 devices in a mesh: ctx: 16 (over z, y, x), fsdp: 2 (over core).
Axes of the slice: x: 2, y: 2, z: 4, core: 2. Of those that a mesh axis runs over, the one named last changes fastest.
Arguments:
- block_input: bfloat16 [2, 2048, 768], P('fsdp', 'ctx'), may hold values from -6 to 6
- out_cotangent: float32 [2, 2048, 768], P('fsdp', 'ctx'), may hold values from -6 to 6
- block_position: int32 [2, 16], P('fsdp'), may hold values from 0 to 15, each once within a row
- first_gain: bfloat16 [768], P('fsdp'), may hold values from 0.25 to 1.75
- first_shift: bfloat16 [768], P('fsdp'), may hold values from -3 to 3
- qkv_weight: bfloat16 [768, 2304], P('fsdp'), may hold values from -1 to 1
- query_bias: bfloat16 [768], P('fsdp'), may hold values from -6 to 6
- value_bias: bfloat16 [768], P('fsdp'), may hold values from -3 to 3
- output_weight: bfloat16 [768, 768], P('fsdp'), may hold values from -1.25 to 1.25
- output_bias: bfloat16 [768], P('fsdp'), may hold values from -3 to 3
- second_gain: bfloat16 [768], P('fsdp'), may hold values from 0.25 to 1.75
- second_shift: bfloat16 [768], P('fsdp'), may hold values from -3 to 3
- expand_weight: bfloat16 [768, 3072], P('fsdp'), may hold values from -0.21875 to 0.21875
- expand_bias: bfloat16 [3072], P('fsdp'), may hold values from -3 to 3
- shrink_weight: bfloat16 [3072, 768], P('fsdp'), may hold values from -0.109375 to 0.109375
- shrink_bias: bfloat16 [768], P('fsdp'), may hold values from -3 to 3
Outputs:
- block_output: bfloat16 [2, 2048, 768], P('fsdp', 'ctx')
- input_grad: float32 [2, 2048, 768], P('fsdp', 'ctx')
- first_gain_grad: float32 [768], P('fsdp')
- first_shift_grad: float32 [768], P('fsdp')
- qkv_weight_grad: float32 [768, 2304], P('fsdp')
- query_bias_grad: float32 [768], P('fsdp')
- value_bias_grad: float32 [768], P('fsdp')
- output_weight_grad: float32 [768, 768], P('fsdp')
- output_bias_grad: float32 [768], P('fsdp')
- second_gain_grad: float32 [768], P('fsdp')
- second_shift_grad: float32 [768], P('fsdp')
- expand_weight_grad: float32 [768, 3072], P('fsdp')
- expand_bias_grad: float32 [3072], P('fsdp')
- shrink_weight_grad: float32 [3072, 768], P('fsdp')
- shrink_bias_grad: float32 [768], P('fsdp')
The draws below stay inside these ranges and needn't reach their ends.
Inputs may be any that keep to these rules, and one draw needn't show every extreme that they name: Each row of block_position names every block once: the device at index c along ctx holds tokens block_position[s, c] * 128 to block_position[s, c] * 128 + 127 of sequence s.
All inputs are finite; a program needn't handle non-finite values.
Results may differ from the reference program's by a relative error of at most 0.019.
Values may be sent and summed in bfloat16 or wider, within the bound.
No kernel may reach another device: no remote copies, remote signals or barrier semaphores. Data moves between devices by JAX's collectives and lax.ppermute only.
A program may use at most 192 MiB of HBM per device.

```python
import math
import jax
import jax.numpy as jnp
from jax import lax

D = 768
H = 12
HD = 64
FF = 3072
BLK = 128
SEQ_LEN = 2048
SEQS = 2
N_CTX = 16


def draw_qkv_weight(key, part):
    first_key = jax.random.fold_in(key, 0)
    base = jax.random.normal(first_key, (D, 3 * D), jnp.float32) / math.sqrt(D)
    return jnp.clip(base, -1.0, 1.0).astype(jnp.bfloat16)


def shard_levels(own_key, shape, cuts, low, high):
    factor_of, own = 1.0, jax.random.fold_in(own_key, 6)
    for position, parts in cuts:
        heights = jnp.exp(jax.random.uniform(jax.random.fold_in(own, position), (parts,), jnp.float32, low / len(cuts), high / len(cuts)))
        factor_of = factor_of * jnp.repeat(heights, shape[position] // parts).reshape([-1 if axis == position else 1 for axis in range(len(shape))])
    return factor_of


def scatter_about(rng, extent, scale, reach, pieces=(), kind=jnp.bfloat16):
    gain = shard_levels(rng, extent, pieces, -0.22, 0.18) if pieces else 1.0
    entries = jax.random.normal(rng, extent, jnp.float32) * scale * gain
    return jnp.minimum(jnp.maximum(entries, -reach), reach).astype(kind)


def setup_inputs(seed: int = 0) -> dict:
    seeds = jax.random.split(jax.random.key(seed), 17)
    return {
        "block_input": scatter_about(seeds[0], (SEQS, SEQ_LEN, D), 1.0, 6.0, ((0, 2), (1, 16))),
        "out_cotangent": scatter_about(seeds[1], (SEQS, SEQ_LEN, D), 1.0, 6.0, ((0, 2), (1, 16)), jnp.float32),
        "block_position": jax.vmap(lambda own: jax.random.permutation(own, N_CTX))(jax.random.split(seeds[2], SEQS)).reshape((SEQS, N_CTX)).astype(jnp.int32),
        "first_gain": jnp.clip(1.0 + 0.15 * jax.random.normal(seeds[3], (D,), jnp.float32), 0.25, 1.75).astype(jnp.bfloat16),
        "first_shift": scatter_about(seeds[4], (D,), 0.5, 3.0, ((0, 2),)),
        "qkv_weight": draw_qkv_weight(jax.random.fold_in(seeds[16], 71), 0),
        "query_bias": scatter_about(seeds[6], (D,), 1.5, 6.0, ((0, 2),)),
        "value_bias": scatter_about(seeds[7], (D,), 0.5, 3.0, ((0, 2),)),
        "output_weight": scatter_about(seeds[8], (D, D), (D // 32) ** -0.5, 1.25, ((0, 2),)),
        "output_bias": scatter_about(seeds[9], (D,), 0.5, 3.0, ((0, 2),)),
        "second_gain": jnp.clip(1.0 + 0.15 * jax.random.normal(seeds[10], (D,), jnp.float32), 0.25, 1.75).astype(jnp.bfloat16),
        "second_shift": scatter_about(seeds[11], (D,), 0.5, 3.0, ((0, 2),)),
        "expand_weight": scatter_about(seeds[12], (D, FF), D ** -0.5, 0.21875, ((0, 2),)),
        "expand_bias": scatter_about(seeds[13], (FF,), 0.5, 3.0, ((0, 2),)),
        "shrink_weight": scatter_about(seeds[14], (FF, D), FF ** -0.5, 0.109375, ((0, 2),)),
        "shrink_bias": scatter_about(seeds[15], (D,), 0.5, 3.0, ((0, 2),)),
    }


NORM_EPS = 1e-05
MASK_FLOOR = -1e+30
GELU_COEF = 0.7978845608028654
GELU_CUBE = 0.044715

def rounded(inputs):
    return lax.optimization_barrier(inputs.astype(jnp.bfloat16)).astype(jnp.float32)

def layer_norm(inputs, norm_gain, norm_shift):
    middle = lax.optimization_barrier(jnp.mean(inputs, axis=-1, keepdims=True))
    centred = inputs - middle
    inv_std = lax.rsqrt(lax.optimization_barrier(jnp.mean(centred * centred, axis=-1, keepdims=True)) + NORM_EPS)
    normed = centred * inv_std
    return (normed * norm_gain.astype(jnp.float32) + norm_shift.astype(jnp.float32), normed, inv_std)

def norm_back(upstream, normed, inv_std, norm_gain):
    scaled = upstream * norm_gain.astype(jnp.float32)
    return inv_std * (scaled - lax.optimization_barrier(jnp.mean(scaled, axis=-1, keepdims=True)) - normed * lax.optimization_barrier(jnp.mean(scaled * normed, axis=-1, keepdims=True)))

def gelu_value(inputs):
    tanh_part = jnp.tanh(GELU_COEF * (inputs + GELU_CUBE * inputs * inputs * inputs))
    return 0.5 * inputs * (1.0 + tanh_part)

def gelu_slope(inputs):
    tanh_part = jnp.tanh(GELU_COEF * (inputs + GELU_CUBE * inputs * inputs * inputs))
    return 0.5 * (1.0 + tanh_part) + 0.5 * inputs * (1.0 - tanh_part * tanh_part) * GELU_COEF * (1.0 + 3.0 * GELU_CUBE * inputs * inputs)

def attend(queries, key_rows, values, positions):
    length = queries.shape[0]
    block_span = math.gcd(512, length)
    score_scale = HD ** (-0.5)
    key_heads = key_rows.astype(jnp.float32).reshape(length, H, HD)
    value_heads = values.astype(jnp.float32).reshape(length, H, HD)

    def one_block(unused, block_index):
        first_row = block_index * block_span
        query_part = lax.dynamic_slice_in_dim(queries, first_row, block_span, 0).astype(jnp.float32).reshape(block_span, H, HD)
        query_pos = lax.dynamic_slice_in_dim(positions, first_row, block_span, 0)
        visible = positions[None, None, :] <= query_pos[None, :, None]
        scores = jnp.where(visible, jnp.einsum('qhd,khd->hqk', query_part, key_heads) * score_scale, MASK_FLOOR)
        row_max = lax.optimization_barrier(jnp.max(scores, axis=2))
        weights = jnp.where(visible, jnp.exp(scores - row_max[:, :, None]), 0.0)
        row_total = lax.optimization_barrier(jnp.sum(weights, axis=2))
        mixed_sum = jnp.einsum('hqk,khd->qhd', rounded(weights), value_heads)
        output = (mixed_sum / row_total.T[:, :, None]).reshape(block_span, H * HD).astype(jnp.bfloat16)
        return (unused, (output, (row_max + jnp.log(row_total)).T))
    unused, (outputs, totals) = lax.scan(one_block, None, jnp.arange(length // block_span, dtype=jnp.int32))
    return (outputs.reshape(length, H * HD), totals.reshape(length, H))

def attend_back(queries, key_rows, values, positions, attended, log_total, grad_attended):
    length = queries.shape[0]
    block_span = math.gcd(512, length)
    score_scale = HD ** (-0.5)
    key_heads = key_rows.astype(jnp.float32).reshape(length, H, HD)
    value_heads = values.astype(jnp.float32).reshape(length, H, HD)
    delta = lax.optimization_barrier(jnp.sum((grad_attended.astype(jnp.float32) * attended.astype(jnp.float32)).reshape(length, H, HD), axis=2))

    def one_block(sums, block_index):
        key_sum, value_sum = sums
        first_row = block_index * block_span
        query_part = lax.dynamic_slice_in_dim(queries, first_row, block_span, 0).astype(jnp.float32).reshape(block_span, H, HD)
        grad_part = lax.dynamic_slice_in_dim(grad_attended, first_row, block_span, 0).astype(jnp.float32).reshape(block_span, H, HD)
        total_part = lax.dynamic_slice_in_dim(log_total, first_row, block_span, 0)
        delta_part = lax.dynamic_slice_in_dim(delta, first_row, block_span, 0)
        query_pos = lax.dynamic_slice_in_dim(positions, first_row, block_span, 0)
        visible = positions[None, None, :] <= query_pos[None, :, None]
        scores = jnp.where(visible, jnp.einsum('qhd,khd->hqk', query_part, key_heads) * score_scale, MASK_FLOOR)
        probs = jnp.where(visible, jnp.exp(scores - total_part.T[:, :, None]), 0.0)
        prob_grad = jnp.einsum('qhd,khd->hqk', grad_part, value_heads)
        score_grad = probs * (prob_grad - delta_part.T[:, :, None])
        value_sum = value_sum + jnp.einsum('hqk,qhd->khd', rounded(probs), grad_part)
        scaled_grad = rounded(score_grad * score_scale)
        query_grad = jnp.einsum('hqk,khd->qhd', scaled_grad, key_heads).reshape(block_span, H * HD)
        key_sum = key_sum + jnp.einsum('hqk,qhd->khd', scaled_grad, query_part)
        return ((key_sum, value_sum), query_grad)
    start_sums = (jnp.zeros((length, H, HD), jnp.float32), jnp.zeros((length, H, HD), jnp.float32))
    (key_sum, value_sum), query_grads = lax.scan(one_block, start_sums, jnp.arange(length // block_span, dtype=jnp.int32))
    return (query_grads.reshape(length, H * HD), key_sum.reshape(length, H * HD), value_sum.reshape(length, H * HD))

def sequence_pass(seq_input, seq_grad, table, params):
    first_gain, first_shift, qkv_weight, query_bias, value_bias, output_weight, output_bias, second_gain, second_shift, expand_weight, expand_bias, shrink_weight, shrink_bias = params
    width = seq_input.shape[1]
    length = seq_input.shape[0]
    row_ids = jnp.arange(length, dtype=jnp.int32)
    positions = (table[row_ids // BLK] * BLK + row_ids % BLK).astype(jnp.int32)
    inputs_f = seq_input.astype(jnp.float32)
    normed_a, unit_a, inv_a = layer_norm(inputs_f, first_gain, first_shift)
    hidden_a = normed_a.astype(jnp.bfloat16)
    joint = jnp.dot(hidden_a, qkv_weight, preferred_element_type=jnp.float32)
    queries = (joint[:, :width] + query_bias.astype(jnp.float32)).astype(jnp.bfloat16)
    key_rows = joint[:, width:2 * width].astype(jnp.bfloat16)
    values = (joint[:, 2 * width:] + value_bias.astype(jnp.float32)).astype(jnp.bfloat16)
    attended, log_total = attend(queries, key_rows, values, positions)
    middle = inputs_f + jnp.dot(attended, output_weight, preferred_element_type=jnp.float32) + output_bias.astype(jnp.float32)
    normed_b, unit_b, inv_b = layer_norm(middle, second_gain, second_shift)
    hidden_b = normed_b.astype(jnp.bfloat16)
    expanded = jnp.dot(hidden_b, expand_weight, preferred_element_type=jnp.float32) + expand_bias.astype(jnp.float32)
    active = gelu_value(expanded).astype(jnp.bfloat16)
    result = middle + jnp.dot(active, shrink_weight, preferred_element_type=jnp.float32) + shrink_bias.astype(jnp.float32)
    cot_b = seq_grad.astype(jnp.bfloat16)
    grad_shrink = jnp.dot(active.T, cot_b, preferred_element_type=jnp.float32)
    grad_shrink_add = lax.optimization_barrier(jnp.sum(seq_grad, axis=0))
    grad_expanded = jnp.dot(cot_b, shrink_weight.T, preferred_element_type=jnp.float32) * gelu_slope(expanded)
    grad_expanded_b = grad_expanded.astype(jnp.bfloat16)
    grad_expand = jnp.dot(hidden_b.T, grad_expanded_b, preferred_element_type=jnp.float32)
    grad_expand_add = lax.optimization_barrier(jnp.sum(grad_expanded, axis=0))
    grad_hidden_b = jnp.dot(grad_expanded_b, expand_weight.T, preferred_element_type=jnp.float32)
    grad_gain_two = lax.optimization_barrier(jnp.sum(grad_hidden_b * unit_b, axis=0))
    grad_shift_two = lax.optimization_barrier(jnp.sum(grad_hidden_b, axis=0))
    grad_middle = seq_grad + norm_back(grad_hidden_b, unit_b, inv_b, second_gain)
    grad_middle_b = grad_middle.astype(jnp.bfloat16)
    grad_mix = jnp.dot(attended.T, grad_middle_b, preferred_element_type=jnp.float32)
    grad_mix_add = lax.optimization_barrier(jnp.sum(grad_middle, axis=0))
    grad_attended = jnp.dot(grad_middle_b, output_weight.T, preferred_element_type=jnp.float32).astype(jnp.bfloat16)
    query_grad, key_grad, value_grad = attend_back(queries, key_rows, values, positions, attended, log_total, grad_attended)
    grad_joint = jnp.concatenate([query_grad, key_grad, value_grad], axis=1).astype(jnp.bfloat16)
    grad_qkv = jnp.dot(hidden_a.T, grad_joint, preferred_element_type=jnp.float32)
    grad_query_add = lax.optimization_barrier(jnp.sum(query_grad, axis=0))
    grad_value_add = lax.optimization_barrier(jnp.sum(value_grad, axis=0))
    grad_hidden_a = jnp.dot(grad_joint, qkv_weight.T, preferred_element_type=jnp.float32)
    grad_gain_one = lax.optimization_barrier(jnp.sum(grad_hidden_a * unit_a, axis=0))
    grad_shift_one = lax.optimization_barrier(jnp.sum(grad_hidden_a, axis=0))
    input_grad = grad_middle + norm_back(grad_hidden_a, unit_a, inv_a, first_gain)
    grads = (grad_gain_one, grad_shift_one, grad_qkv, grad_query_add, grad_value_add, grad_mix, grad_mix_add, grad_gain_two, grad_shift_two, grad_expand, grad_expand_add, grad_shrink, grad_shrink_add)
    return ((result.astype(jnp.bfloat16), input_grad), grads)

def reference(block_input, out_cotangent, block_position, first_gain, first_shift, qkv_weight, query_bias, value_bias, output_weight, output_bias, second_gain, second_shift, expand_weight, expand_bias, shrink_weight, shrink_bias):
    params = (first_gain, first_shift, qkv_weight, query_bias, value_bias, output_weight, output_bias, second_gain, second_shift, expand_weight, expand_bias, shrink_weight, shrink_bias)

    def one_sequence(sums, inputs):
        seq_input, seq_grad, table = inputs
        results, grads = sequence_pass(seq_input, seq_grad, table, params)
        return (tuple((left + right for left, right in zip(sums, grads))), results)
    start_sums = tuple((jnp.zeros(param.shape, jnp.float32) for param in params))
    sums, (outputs, input_grads) = lax.scan(one_sequence, start_sums, (block_input, out_cotangent, block_position))
    return (outputs, input_grads, sums[0], sums[1], sums[2], sums[3], sums[4], sums[5], sums[6], sums[7], sums[8], sums[9], sums[10], sums[11], sums[12])
```

```python
import functools

import jax
import jax.numpy as jnp
from jax import lax
from jax.experimental import pallas as pl
from jax.experimental.pallas import tpu as pltpu
from jax.sharding import PartitionSpec as P

H = 12
HD = 64
NORM_EPS = 1e-05
MASK_FLOOR = -1e30
GELU_COEF = 0.7978845608028654
GELU_CUBE = 0.044715
SCALE = HD ** (-0.5)
F32 = jnp.float32
BF16 = jnp.bfloat16
VMEM_LIMIT = 56 * 1024 * 1024


def dot_nn(left, right):
    return lax.dot_general(left, right, (((1,), (0,)), ((), ())), preferred_element_type=F32)


def dot_nt(left, right):
    return lax.dot_general(left, right, (((1,), (1,)), ((), ())), preferred_element_type=F32)


def dot_tn(left, right):
    return lax.dot_general(left, right, (((0,), (0,)), ((), ())), preferred_element_type=F32)


def normalise(inputs):
    centred = inputs - jnp.mean(inputs, axis=-1, keepdims=True)
    inv_std = lax.rsqrt(jnp.mean(centred * centred, axis=-1, keepdims=True) + NORM_EPS)
    return centred * inv_std, inv_std


def norm_back(scaled, unit, inv_std):
    return inv_std * (
        scaled
        - jnp.mean(scaled, axis=-1, keepdims=True)
        - unit * jnp.mean(scaled * unit, axis=-1, keepdims=True)
    )


def halves(side_ref, size):
    side = side_ref[0]
    own = pl.ds(pl.multiple_of(side * size, 128), size)
    other = pl.ds(pl.multiple_of((1 - side) * size, 128), size)
    return own, other


def call(kernel, outs, scratch, name, flops, *args, smem=1):
    specs = [pl.BlockSpec(memory_space=pltpu.SMEM)] * smem
    specs += [pl.BlockSpec(memory_space=pltpu.VMEM)] * (len(args) - smem)
    moved = sum(a.size * a.dtype.itemsize for a in args)
    return pl.pallas_call(
        kernel,
        out_shape=[jax.ShapeDtypeStruct(s, d) for s, d in outs],
        in_specs=specs,
        out_specs=[pl.BlockSpec(memory_space=pltpu.VMEM)] * len(outs),
        scratch_shapes=[pltpu.VMEM(s, d) for s, d in scratch],
        compiler_params=pltpu.CompilerParams(vmem_limit_bytes=VMEM_LIMIT),
        cost_estimate=pl.CostEstimate(flops=flops, bytes_accessed=moved, transcendentals=0),
        name=name,
    )(*args)


def project_kernel(side_ref, x_ref, vec_ref, own_ref, other_ref, hid_ref, send_ref):
    rows, width = x_ref.shape
    own, other = halves(side_ref, width // 2)
    unit, _ = normalise(x_ref[...].astype(F32))
    vec = vec_ref[...].astype(F32)
    hid_ref[...] = (unit * vec[0:1] + vec[1:2]).astype(BF16)
    joint = dot_nn(hid_ref[:, own], own_ref[...]) + dot_nn(hid_ref[:, other], other_ref[...])
    three = (
        (joint[:, :width] + vec[2:3]).astype(BF16),
        joint[:, width : 2 * width].astype(BF16),
        (joint[:, 2 * width :] + vec[3:4]).astype(BF16),
    )
    for k, part in enumerate(three):
        turned = part.T
        for h in range(H):
            send_ref[h, k * HD : (k + 1) * HD, :] = turned[h * HD : (h + 1) * HD]
    for h in range(H, send_ref.shape[0]):
        send_ref[h] = jnp.zeros(send_ref.shape[1:], BF16)


def attend_kernel(slot_ref, in_ref, out_ref, total_ref, q_t, k_n, v_t, o_t):
    count, _, rows = in_ref.shape
    tile = 512
    for p in range(count):
        slot = slot_ref[p]
        where = slice(p * rows, (p + 1) * rows)
        q_t[:, where] = in_ref[slot, 0:HD, :] * jnp.asarray(SCALE, BF16)
        k_n[where, :] = in_ref[slot, HD : 2 * HD, :].T
        v_t[:, where] = in_ref[slot, 2 * HD : 3 * HD, :]
    length = count * rows
    below = lax.broadcasted_iota(jnp.int32, (tile, tile), 0) <= lax.broadcasted_iota(
        jnp.int32, (tile, tile), 1
    )
    for i in range(length // tile):
        here = slice(i * tile, (i + 1) * tile)
        query = q_t[:, here]
        scores = jnp.where(below, dot_nn(k_n[here, :], query), MASK_FLOOR)
        best = jnp.max(scores, axis=0, keepdims=True)
        weights = jnp.exp(scores - best)
        total = jnp.sum(weights, axis=0, keepdims=True)
        mixed = dot_nn(v_t[:, here], weights.astype(BF16))

        def step(j, state, query=query):
            best, total, mixed = state
            span = pl.ds(pl.multiple_of(j * tile, tile), tile)
            scores = dot_nn(k_n[span, :], query)
            new_best = jnp.maximum(best, jnp.max(scores, axis=0, keepdims=True))
            factor = jnp.exp(best - new_best)
            weights = jnp.exp(scores - new_best)
            total = total * factor + jnp.sum(weights, axis=0, keepdims=True)
            mixed = mixed * factor + dot_nn(v_t[:, span], weights.astype(BF16))
            return new_best, total, mixed

        if i:
            best, total, mixed = lax.fori_loop(0, i, step, (best, total, mixed))
        o_t[:, here] = (mixed / total).astype(BF16)
        total_ref[:, here] = best + jnp.log(total)
    for p in range(count):
        out_ref[slot_ref[p]] = o_t[:, p * rows : (p + 1) * rows]


def attend_back_kernel(
    slot_ref, in_ref, att_ref, grad_ref, total_ref, out_ref,
    q_t, q_n, k_t, k_n, v_n, g_t, g_n, delta, dq_t, dk_t, dv_t,
):
    count, _, rows = in_ref.shape
    tile = 512
    for p in range(count):
        slot = slot_ref[p]
        where = slice(p * rows, (p + 1) * rows)
        query = in_ref[slot, 0:HD, :] * jnp.asarray(SCALE, BF16)
        q_t[:, where] = query
        q_n[where, :] = query.T
        key = in_ref[slot, HD : 2 * HD, :]
        k_t[:, where] = key
        k_n[where, :] = key.T
        v_n[where, :] = in_ref[slot, 2 * HD : 3 * HD, :].T
        grad = grad_ref[slot]
        g_t[:, where] = grad
        g_n[where, :] = grad.T
        delta[:, where] = jnp.sum(
            grad.astype(F32) * att_ref[slot].astype(F32), axis=0, keepdims=True
        )
    length = count * rows
    tiles = length // tile
    below = lax.broadcasted_iota(jnp.int32, (tile, tile), 0) <= lax.broadcasted_iota(
        jnp.int32, (tile, tile), 1
    )
    dq_t[...] = jnp.zeros_like(dq_t)
    for j in range(tiles):
        here = slice(j * tile, (j + 1) * tile)

        def step(i, state, masked=False, here=here):
            key_sum, value_sum = state
            span = pl.ds(pl.multiple_of(i * tile, tile), tile)
            scores = dot_nn(k_n[here, :], q_t[:, span])
            probs = jnp.exp(scores - total_ref[:, span])
            if masked:
                probs = jnp.where(below, probs, 0.0)
            prob_grad = dot_nn(v_n[here, :], g_t[:, span])
            score_grad = (probs * (prob_grad - delta[:, span])).astype(BF16)
            value_sum = value_sum + dot_nn(probs.astype(BF16), g_n[span, :])
            key_sum = key_sum + dot_nn(score_grad, q_n[span, :])
            dq_t[:, span] = dq_t[:, span] + dot_nn(k_t[:, here], score_grad)
            return key_sum, value_sum

        zero = jnp.zeros((tile, HD), F32)
        state = step(j, (zero, zero), masked=True)
        if j + 1 < tiles:
            state = lax.fori_loop(j + 1, tiles, step, state)
        dk_t[:, here] = state[0].T
        dv_t[:, here] = state[1].T
    for p in range(count):
        slot = slot_ref[p]
        where = slice(p * rows, (p + 1) * rows)
        out_ref[slot, 0:HD, :] = (dq_t[:, where] * SCALE).astype(BF16)
        out_ref[slot, HD : 2 * HD, :] = dk_t[:, where].astype(BF16)
        out_ref[slot, 2 * HD : 3 * HD, :] = dv_t[:, where].astype(BF16)


def middle_kernel(
    side_ref, att_in, x_ref, cot_ref, vec_ref, ebias_ref,
    mix_own, mix_other, ex_own, ex_other, sh_own, sh_other,
    res_ref, gm_ref, gsend_ref, sums_ref, esum_ref,
    cotb_ref, act_keep, act_send, hid_keep, hid_send, ge_ref, att_keep, att_send, gmb_ref,
    wide, act_s, geb_s, hid_s, att_s, narrow,
):
    rows, width = x_ref.shape
    ff = wide.shape[1]
    own, other = halves(side_ref, width // 2)
    fown, fother = halves(side_ref, ff // 2)
    vec = vec_ref[...].astype(F32)
    att_s[...] = att_in[0:H].reshape(width, rows).T
    att_keep[...] = att_s[:, own]
    att_send[...] = att_s[:, other]
    middle = (
        x_ref[...].astype(F32)
        + (dot_nn(att_keep[...], mix_own[...]) + dot_nn(att_send[...], mix_other[...]))
        + vec[4:5]
    )
    unit, inv_std = normalise(middle)
    hid_s[...] = (unit * vec[5:6] + vec[6:7]).astype(BF16)
    hid_keep[...] = hid_s[:, own]
    hid_send[...] = hid_s[:, other]
    expanded = (
        dot_nn(hid_keep[...], ex_own[...])
        + dot_nn(hid_send[...], ex_other[...])
        + ebias_ref[...].astype(F32)
    )
    square = expanded * expanded
    bend = jnp.tanh(GELU_COEF * (expanded + GELU_CUBE * square * expanded))
    act_s[...] = (0.5 * expanded * (1.0 + bend)).astype(BF16)
    slope = 0.5 * (1.0 + bend) + 0.5 * expanded * (1.0 - bend * bend) * GELU_COEF * (
        1.0 + 3.0 * GELU_CUBE * square
    )
    act_keep[...] = act_s[:, fown]
    act_send[...] = act_s[:, fother]
    result = (
        middle
        + (dot_nn(act_keep[...], sh_own[...]) + dot_nn(act_send[...], sh_other[...]))
        + vec[7:8]
    )
    res_ref[...] = result.astype(BF16)
    upstream = cot_ref[...]
    cotb_ref[...] = upstream.astype(BF16)
    wide[:, fown] = dot_nt(cotb_ref[...], sh_own[...])
    wide[:, fother] = dot_nt(cotb_ref[...], sh_other[...])
    grad_expanded = wide[...] * slope
    esum_ref[...] = jnp.sum(grad_expanded, axis=0, keepdims=True)
    ge_ref[...] = grad_expanded.astype(BF16)
    narrow[:, own] = dot_nt(ge_ref[...], ex_own[...])
    narrow[:, other] = dot_nt(ge_ref[...], ex_other[...])
    grad_hidden = narrow[...]
    sums_ref[1:2] = jnp.sum(grad_hidden * unit, axis=0, keepdims=True)
    sums_ref[2:3] = jnp.sum(grad_hidden, axis=0, keepdims=True)
    grad_middle = upstream + norm_back(grad_hidden * vec[5:6], unit, inv_std)
    gm_ref[...] = grad_middle
    gmb_ref[...] = grad_middle.astype(BF16)
    sums_ref[0:1] = jnp.sum(grad_middle, axis=0, keepdims=True)
    sums_ref[3:4] = jnp.sum(upstream, axis=0, keepdims=True)
    narrow[:, own] = dot_nt(gmb_ref[...], mix_own[...])
    narrow[:, other] = dot_nt(gmb_ref[...], mix_other[...])
    gsend_ref[0:H] = narrow[...].astype(BF16).T.reshape(H, HD, rows)
    for h in range(H, gsend_ref.shape[0]):
        gsend_ref[h] = jnp.zeros(gsend_ref.shape[1:], BF16)


def finish_kernel(
    side_ref, in_ref, x_ref, gm_ref, vec_ref, hid_ref, own_ref, other_ref,
    grad_ref, sums_ref, gj_ref, hid_keep, hid_send, narrow,
):
    rows, width = x_ref.shape
    own, other = halves(side_ref, width // 2)
    vec = vec_ref[...].astype(F32)
    for k in range(3):
        gj_ref[:, k * width : (k + 1) * width] = (
            in_ref[0:H, k * HD : (k + 1) * HD, :].reshape(width, rows).T
        )
    hid_keep[...] = hid_ref[:, own]
    hid_send[...] = hid_ref[:, other]
    unit, inv_std = normalise(x_ref[...].astype(F32))
    narrow[:, own] = dot_nt(gj_ref[...], own_ref[...])
    narrow[:, other] = dot_nt(gj_ref[...], other_ref[...])
    grad_hidden = narrow[...]
    sums_ref[0:1] = jnp.sum(grad_hidden * unit, axis=0, keepdims=True)
    sums_ref[1:2] = jnp.sum(grad_hidden, axis=0, keepdims=True)
    sums_ref[2:3] = jnp.sum(gj_ref[:, :width].astype(F32), axis=0, keepdims=True)
    sums_ref[3:4] = jnp.sum(gj_ref[:, 2 * width :].astype(F32), axis=0, keepdims=True)
    grad_ref[...] = gm_ref[...] + norm_back(grad_hidden * vec[0:1], unit, inv_std)


SWAP = [(0, 1), (1, 0)]


def pieces(weight, group):
    if group == 2:
        return weight, lax.ppermute(weight, "fsdp", SWAP)
    full = lax.all_gather(weight, "fsdp", axis=0, tiled=True)
    half = full.shape[0] // 2
    return full[:half], full[half:]


def join_vector(vector, group, side):
    if group == 2:
        other = lax.ppermute(vector, "fsdp", SWAP)
        return jnp.where(
            side == 0,
            jnp.concatenate([vector, other], axis=1),
            jnp.concatenate([other, vector], axis=1),
        )
    return lax.all_gather(vector, "fsdp", axis=1, tiled=True)


def rows_over_pair(keep, send, right, group):
    if group == 2:
        left = jnp.concatenate([keep, lax.ppermute(send, "fsdp", SWAP)], axis=0)
        right = jnp.concatenate([right, lax.ppermute(right, "fsdp", SWAP)], axis=0)
    else:
        left = jnp.concatenate([keep, send], axis=1)
        left = lax.all_to_all(left, "fsdp", split_axis=1, concat_axis=0, tiled=True)
        right = lax.all_gather(right, "fsdp", axis=0, tiled=True)
    return dot_tn(left, right)


def own_columns(sums, group, side):
    if group == 2:
        half = sums.shape[1] // 2
        keep = lax.dynamic_slice_in_dim(sums, side * half, half, 1)
        send = lax.dynamic_slice_in_dim(sums, (1 - side) * half, half, 1)
        return keep + lax.ppermute(send, "fsdp", SWAP)
    return lax.psum_scatter(sums, "fsdp", scatter_dimension=1, tiled=True)


def vector_total(sums, count):
    spread = jnp.broadcast_to(sums[None], (count,) + sums.shape)
    return jnp.sum(lax.all_to_all(spread, "ctx", 0, 0, tiled=True), axis=0)


def bit_orders(count):
    bits = list(range(count.bit_length() - 1))
    turn, last = bits[:3], bits[3:]
    return [turn[k:] + turn[:k] + last for k in range(3)]


def swap_bit(part, bit, count):
    return lax.ppermute(part, "ctx", [(d, d ^ (1 << bit)) for d in range(count)])


def total_over_ctx(parts, count):
    index = lax.axis_index("ctx")
    orders = bit_orders(count)
    steps = len(orders[0])
    parts = list(parts)
    for s in range(steps):
        for k, part in enumerate(parts):
            bit = orders[k][s]
            high = (index >> bit) & 1
            half = part.shape[0] // 2
            keep = lax.dynamic_slice_in_dim(part, high * half, half, 0)
            send = lax.dynamic_slice_in_dim(part, (1 - high) * half, half, 0)
            came = swap_bit(send, bit, count)
            parts[k] = (keep.astype(F32) + came.astype(F32)).astype(BF16)
    for s in reversed(range(steps)):
        for k, part in enumerate(parts):
            bit = orders[k][s]
            high = (index >> bit) & 1
            came = swap_bit(part, bit, count)
            parts[k] = jnp.where(
                high == 0,
                jnp.concatenate([part, came], axis=0),
                jnp.concatenate([came, part], axis=0),
            )
    return parts


def stack_columns(weights, third, wide):
    blocks = []
    for weight in weights:
        span = weight.shape[1] // 3
        for c in range(span // wide):
            start = third * span + c * wide
            blocks.append(weight[:, start : start + wide])
    return jnp.concatenate(blocks, axis=0).astype(BF16)


def unstack_columns(parts, shapes, wide):
    outs = []
    first = 0
    for rows, cols in shapes:
        blocks = []
        each = cols // 3 // wide
        for part in parts:
            for c in range(each):
                blocks.append(part[first + c * rows : first + (c + 1) * rows])
        first += each * rows
        outs.append(jnp.concatenate(blocks, axis=1).astype(F32))
    return outs


def body(
    block_input, out_cotangent, block_position, first_gain, first_shift, qkv_weight, query_bias,
    value_bias, output_weight, output_bias, second_gain, second_shift, expand_weight, expand_bias,
    shrink_weight, shrink_bias,
):
    count = lax.axis_size("ctx")
    group = lax.axis_size("fsdp")
    rows, width = block_input.shape[1:]
    ff = expand_weight.shape[1]
    length = count * rows
    side = lax.axis_index("fsdp") if group == 2 else jnp.int32(0)
    sides = jnp.reshape(side, (1,)).astype(jnp.int32)
    table = block_position[0]
    places = jnp.arange(count, dtype=jnp.int32)
    slots = jnp.sum(
        jnp.where(table[None, :] == places[:, None], places[None, :], 0), axis=1
    ).astype(jnp.int32)
    x = block_input[0]
    vec = join_vector(
        jnp.stack(
            [first_gain, first_shift, query_bias, value_bias, output_bias, second_gain,
             second_shift, shrink_bias]
        ),
        group, side,
    )
    qkv = pieces(qkv_weight, group)
    ebias = join_vector(expand_bias[None], group, side)
    mix = pieces(output_weight, group)
    expand = pieces(expand_weight, group)
    shrink = pieces(shrink_weight, group)
    size = width * ff

    hidden_a, qkv_send = call(
        project_kernel,
        [((rows, width), BF16), ((count, 3 * HD, rows), BF16)],
        [], "project", 6 * rows * width * width,
        sides, x, vec, *qkv,
    )
    qkv_here = lax.all_to_all(qkv_send, "ctx", 0, 0, tiled=True)
    att_send, log_total = call(
        attend_kernel,
        [((count, HD, rows), BF16), ((1, length), F32)],
        [((HD, length), BF16), ((length, HD), BF16), ((HD, length), BF16), ((HD, length), BF16)],
        "attend", 2 * length * length * HD,
        slots, qkv_here,
    )
    att_here = lax.all_to_all(att_send, "ctx", 0, 0, tiled=True)
    half = width // 2
    (
        result, grad_middle, grad_send, sums, esum, cot_b, act_keep, act_out, hidb_keep, hidb_out,
        ge_b, att_keep, att_out, gm_b,
    ) = call(
        middle_kernel,
        [
            ((rows, width), BF16), ((rows, width), F32), ((count, HD, rows), BF16),
            ((4, width), F32), ((1, ff), F32), ((rows, width), BF16), ((rows, ff // 2), BF16),
            ((rows, ff // 2), BF16), ((rows, half), BF16), ((rows, half), BF16),
            ((rows, ff), BF16), ((rows, half), BF16), ((rows, half), BF16), ((rows, width), BF16),
        ],
        [
            ((rows, ff), F32), ((rows, ff), BF16), ((rows, ff), BF16), ((rows, width), BF16),
            ((rows, width), BF16), ((rows, width), F32),
        ],
        "middle", 8 * rows * size + 4 * rows * width * width,
        sides, att_here, x, out_cotangent[0], vec, ebias, *mix, *expand, *shrink,
    )
    grad_here = lax.all_to_all(grad_send, "ctx", 0, 0, tiled=True)
    (dqkv_send,) = call(
        attend_back_kernel,
        [((count, 3 * HD, rows), BF16)],
        [
            ((HD, length), BF16), ((length, HD), BF16), ((HD, length), BF16),
            ((length, HD), BF16), ((length, HD), BF16), ((HD, length), BF16),
            ((length, HD), BF16), ((1, length), F32), ((HD, length), F32), ((HD, length), F32),
            ((HD, length), F32),
        ],
        "attend_back", 5 * length * length * HD,
        slots, qkv_here, att_send, grad_here, log_total,
    )
    dqkv_here = lax.all_to_all(dqkv_send, "ctx", 0, 0, tiled=True)

    grad_shrink = rows_over_pair(act_keep, act_out, cot_b, group)
    grad_expand = rows_over_pair(hidb_keep, hidb_out, ge_b, group)
    grad_mix = rows_over_pair(att_keep, att_out, gm_b, group)
    early = (grad_shrink, grad_expand, grad_mix)
    early_sums = total_over_ctx([stack_columns(early, k, 256) for k in range(3)], count)
    grad_shrink, grad_expand, grad_mix = unstack_columns(
        early_sums, [g.shape for g in early], 256
    )
    each = width // group
    esum = esum.reshape(group, 4, each).swapaxes(0, 1).reshape(4, width)
    sums = own_columns(jnp.concatenate([sums, esum], axis=0), group, side)
    sums = vector_total(sums, count)

    input_grad, late, gj, hida_keep, hida_out = call(
        finish_kernel,
        [
            ((rows, width), F32), ((4, width), F32), ((rows, 3 * width), BF16),
            ((rows, half), BF16), ((rows, half), BF16),
        ],
        [((rows, width), F32)],
        "finish", 6 * rows * width * width,
        sides, dqkv_here, x, grad_middle, vec, hidden_a, *qkv,
    )
    grad_qkv = rows_over_pair(hida_keep, hida_out, gj, group)
    late_sums = total_over_ctx([stack_columns((grad_qkv,), k, 256) for k in range(3)], count)
    (grad_qkv,) = unstack_columns(late_sums, [grad_qkv.shape], 256)
    late = vector_total(own_columns(late, group, side), count)
    return (
        result[None], input_grad[None], late[0], late[1], grad_qkv, late[2], late[3],
        grad_mix, sums[0], sums[1], sums[2], grad_expand, sums[4:8].reshape(-1), grad_shrink,
        sums[3],
    )


def solution(mesh):
    block = P("fsdp", "ctx", None)
    vector, matrix = P("fsdp"), P("fsdp", None)
    return jax.shard_map(
        body,
        mesh=mesh,
        in_specs=(
            block, block, matrix, vector, vector, matrix, vector, vector, matrix, vector, vector,
            vector, matrix, vector, matrix, vector,
        ),
        out_specs=(
            block, block, vector, vector, matrix, vector, vector, matrix, vector, vector, vector,
            matrix, vector, matrix, vector,
        ),
        check_vma=False,
    )
```

```python
import functools

import jax
import jax.numpy as jnp
from jax import lax
from jax.experimental import pallas as pl
from jax.experimental.pallas import tpu as pltpu
from jax.sharding import PartitionSpec as P

H = 12
HD = 64
NORM_EPS = 1e-05
MASK_FLOOR = -1e30
GELU_COEF = 0.7978845608028654
GELU_CUBE = 0.044715
SCALE = HD ** (-0.5)
F32 = jnp.float32
BF16 = jnp.bfloat16
LANES = 128
MIB = 1024 * 1024


def dot_nn(left, right):
    return lax.dot_general(left, right, (((1,), (0,)), ((), ())), preferred_element_type=F32)


def dot_nt(left, right):
    return lax.dot_general(left, right, (((1,), (1,)), ((), ())), preferred_element_type=F32)


def dot_tn(left, right):
    return lax.dot_general(left, right, (((0,), (0,)), ((), ())), preferred_element_type=F32)


def normalise(inputs):
    centred = inputs - jnp.mean(inputs, axis=-1, keepdims=True)
    inv_std = lax.rsqrt(jnp.mean(centred * centred, axis=-1, keepdims=True) + NORM_EPS)
    return centred * inv_std, inv_std


def norm_back(scaled, unit, inv_std):
    return inv_std * (
        scaled
        - jnp.mean(scaled, axis=-1, keepdims=True)
        - unit * jnp.mean(scaled * unit, axis=-1, keepdims=True)
    )


def halves(side_ref, size):
    side = side_ref[0]
    own = pl.ds(pl.multiple_of(side * size, 128), size)
    other = pl.ds(pl.multiple_of((1 - side) * size, 128), size)
    return own, other


def call(kernel, outs, scratch, name, flops, *args, smem=1, away=0, away_outs=0):
    vmem = pl.BlockSpec(memory_space=pltpu.VMEM)
    anywhere = pl.BlockSpec(memory_space=pl.ANY)
    specs = [pl.BlockSpec(memory_space=pltpu.SMEM)] * smem
    specs += [vmem] * (len(args) - smem - away) + [anywhere] * away
    moved = sum(a.size * a.dtype.itemsize for a in args)
    return pl.pallas_call(
        kernel,
        out_shape=[jax.ShapeDtypeStruct(s, d) for s, d in outs],
        in_specs=specs,
        out_specs=[anywhere] * away_outs + [vmem] * (len(outs) - away_outs),
        scratch_shapes=[pltpu.VMEM(*s) if isinstance(s, tuple) else s for s in scratch],
        compiler_params=pltpu.CompilerParams(vmem_limit_bytes=56 * MIB),
        cost_estimate=pl.CostEstimate(flops=flops, bytes_accessed=moved, transcendentals=0),
        name=name,
    )(*args)


def bits_of(count):
    return list(range(count.bit_length() - 1))


def sum_orders(count):
    turn, last = bits_of(count)[:3], bits_of(count)[3:]
    return [list(reversed(turn[k:] + turn[:k] + last)) for k in range(3)]


def place_of(r, order):
    place = 0
    for s, bit in enumerate(order):
        place = place | (((r >> bit) & 1) << s)
    return place


def relative_at(place, order):
    return sum(((place >> s) & 1) << bit for s, bit in enumerate(order))


def project_kernel(side_ref, x_ref, vec_ref, own_ref, other_ref, hid_ref, send_ref):
    rows, width = x_ref.shape
    own, other = halves(side_ref, width // 2)
    unit, _ = normalise(x_ref[...].astype(F32))
    vec = vec_ref[...].astype(F32)
    hid_ref[...] = (unit * vec[0:1] + vec[1:2]).astype(BF16)
    joint = dot_nn(hid_ref[:, own], own_ref[...]) + dot_nn(hid_ref[:, other], other_ref[...])
    three = (
        (joint[:, :width] + vec[2:3]).astype(BF16),
        joint[:, width : 2 * width].astype(BF16),
        (joint[:, 2 * width :] + vec[3:4]).astype(BF16),
    )
    for k, part in enumerate(three):
        turned = part.T
        for h in range(H):
            send_ref[h, k * HD : (k + 1) * HD, :] = turned[h * HD : (h + 1) * HD]
    for h in range(H, send_ref.shape[0]):
        send_ref[h] = jnp.zeros(send_ref.shape[1:], BF16)


def attend_kernel(slot_ref, in_ref, out_ref, total_ref, q_t, k_n, v_t, o_t):
    count, _, rows = in_ref.shape
    tile = 512
    for p in range(count):
        slot = slot_ref[p]
        where = slice(p * rows, (p + 1) * rows)
        q_t[:, where] = in_ref[slot, 0:HD, :] * jnp.asarray(SCALE, BF16)
        k_n[where, :] = in_ref[slot, HD : 2 * HD, :].T
        v_t[:, where] = in_ref[slot, 2 * HD : 3 * HD, :]
    length = count * rows
    below = lax.broadcasted_iota(jnp.int32, (tile, tile), 0) <= lax.broadcasted_iota(
        jnp.int32, (tile, tile), 1
    )
    for i in range(length // tile):
        here = slice(i * tile, (i + 1) * tile)
        query = q_t[:, here]
        scores = jnp.where(below, dot_nn(k_n[here, :], query), MASK_FLOOR)
        best = jnp.max(scores, axis=0, keepdims=True)
        weights = jnp.exp(scores - best)
        total = jnp.sum(weights, axis=0, keepdims=True)
        mixed = dot_nn(v_t[:, here], weights.astype(BF16))

        def step(j, state, query=query):
            best, total, mixed = state
            span = pl.ds(pl.multiple_of(j * tile, tile), tile)
            scores = dot_nn(k_n[span, :], query)
            new_best = jnp.maximum(best, jnp.max(scores, axis=0, keepdims=True))
            factor = jnp.exp(best - new_best)
            weights = jnp.exp(scores - new_best)
            total = total * factor + jnp.sum(weights, axis=0, keepdims=True)
            mixed = mixed * factor + dot_nn(v_t[:, span], weights.astype(BF16))
            return new_best, total, mixed

        if i:
            best, total, mixed = lax.fori_loop(0, i, step, (best, total, mixed))
        o_t[:, here] = (mixed / total).astype(BF16)
        total_ref[:, here] = best + jnp.log(total)
    for p in range(count):
        out_ref[slot_ref[p]] = o_t[:, p * rows : (p + 1) * rows]


def attend_back_kernel(
    slot_ref, in_ref, att_ref, grad_ref, total_ref, out_ref,
    q_t, q_n, k_t, k_n, v_n, g_t, g_n, delta, dq_t, dk_t, dv_t,
):
    count, _, rows = in_ref.shape
    tile = 512
    for p in range(count):
        slot = slot_ref[p]
        where = slice(p * rows, (p + 1) * rows)
        query = in_ref[slot, 0:HD, :] * jnp.asarray(SCALE, BF16)
        q_t[:, where] = query
        q_n[where, :] = query.T
        key = in_ref[slot, HD : 2 * HD, :]
        k_t[:, where] = key
        k_n[where, :] = key.T
        v_n[where, :] = in_ref[slot, 2 * HD : 3 * HD, :].T
        grad = grad_ref[slot]
        g_t[:, where] = grad
        g_n[where, :] = grad.T
        delta[:, where] = jnp.sum(
            grad.astype(F32) * att_ref[slot].astype(F32), axis=0, keepdims=True
        )
    length = count * rows
    tiles = length // tile
    below = lax.broadcasted_iota(jnp.int32, (tile, tile), 0) <= lax.broadcasted_iota(
        jnp.int32, (tile, tile), 1
    )
    dq_t[...] = jnp.zeros_like(dq_t)
    for j in range(tiles):
        here = slice(j * tile, (j + 1) * tile)

        def step(i, state, masked=False, here=here):
            key_sum, value_sum = state
            span = pl.ds(pl.multiple_of(i * tile, tile), tile)
            scores = dot_nn(k_n[here, :], q_t[:, span])
            probs = jnp.exp(scores - total_ref[:, span])
            if masked:
                probs = jnp.where(below, probs, 0.0)
            prob_grad = dot_nn(v_n[here, :], g_t[:, span])
            score_grad = (probs * (prob_grad - delta[:, span])).astype(BF16)
            value_sum = value_sum + dot_nn(probs.astype(BF16), g_n[span, :])
            key_sum = key_sum + dot_nn(score_grad, q_n[span, :])
            dq_t[:, span] = dq_t[:, span] + dot_nn(k_t[:, here], score_grad)
            return key_sum, value_sum

        zero = jnp.zeros((tile, HD), F32)
        state = step(j, (zero, zero), masked=True)
        if j + 1 < tiles:
            state = lax.fori_loop(j + 1, tiles, step, state)
        dk_t[:, here] = state[0].T
        dv_t[:, here] = state[1].T
    for p in range(count):
        slot = slot_ref[p]
        where = slice(p * rows, (p + 1) * rows)
        out_ref[slot, 0:HD, :] = (dq_t[:, where] * SCALE).astype(BF16)
        out_ref[slot, HD : 2 * HD, :] = dk_t[:, where].astype(BF16)
        out_ref[slot, 2 * HD : 3 * HD, :] = dv_t[:, where].astype(BF16)


def middle_kernel(
    side_ref, att_in, x_ref, cot_ref, vec_ref, ebias_ref,
    mix_own, mix_other, ex_own, ex_other, sh_own, sh_other,
    res_ref, gm_ref, gsend_ref, sums_ref, esum_ref,
    cotb_ref, act_keep, act_send, hid_keep, hid_send, ge_ref, att_keep, att_send, gmb_ref,
    wide, act_s, geb_s, hid_s, att_s, narrow,
):
    rows, width = x_ref.shape
    ff = wide.shape[1]
    own, other = halves(side_ref, width // 2)
    fown, fother = halves(side_ref, ff // 2)
    vec = vec_ref[...].astype(F32)
    att_s[...] = att_in[0:H].reshape(width, rows).T
    att_keep[...] = att_s[:, own]
    att_send[...] = att_s[:, other]
    middle = (
        x_ref[...].astype(F32)
        + (dot_nn(att_keep[...], mix_own[...]) + dot_nn(att_send[...], mix_other[...]))
        + vec[4:5]
    )
    unit, inv_std = normalise(middle)
    hid_s[...] = (unit * vec[5:6] + vec[6:7]).astype(BF16)
    hid_keep[...] = hid_s[:, own]
    hid_send[...] = hid_s[:, other]
    expanded = (
        dot_nn(hid_keep[...], ex_own[...])
        + dot_nn(hid_send[...], ex_other[...])
        + ebias_ref[...].astype(F32)
    )
    square = expanded * expanded
    bend = jnp.tanh(GELU_COEF * (expanded + GELU_CUBE * square * expanded))
    act_s[...] = (0.5 * expanded * (1.0 + bend)).astype(BF16)
    slope = 0.5 * (1.0 + bend) + 0.5 * expanded * (1.0 - bend * bend) * GELU_COEF * (
        1.0 + 3.0 * GELU_CUBE * square
    )
    act_keep[...] = act_s[:, fown]
    act_send[...] = act_s[:, fother]
    result = (
        middle
        + (dot_nn(act_keep[...], sh_own[...]) + dot_nn(act_send[...], sh_other[...]))
        + vec[7:8]
    )
    res_ref[...] = result.astype(BF16)
    upstream = cot_ref[...]
    cotb_ref[...] = upstream.astype(BF16)
    wide[:, fown] = dot_nt(cotb_ref[...], sh_own[...])
    wide[:, fother] = dot_nt(cotb_ref[...], sh_other[...])
    grad_expanded = wide[...] * slope
    esum_ref[...] = jnp.sum(grad_expanded, axis=0, keepdims=True)
    ge_ref[...] = grad_expanded.astype(BF16)
    narrow[:, own] = dot_nt(ge_ref[...], ex_own[...])
    narrow[:, other] = dot_nt(ge_ref[...], ex_other[...])
    grad_hidden = narrow[...]
    sums_ref[1:2] = jnp.sum(grad_hidden * unit, axis=0, keepdims=True)
    sums_ref[2:3] = jnp.sum(grad_hidden, axis=0, keepdims=True)
    grad_middle = upstream + norm_back(grad_hidden * vec[5:6], unit, inv_std)
    gm_ref[...] = grad_middle
    gmb_ref[...] = grad_middle.astype(BF16)
    sums_ref[0:1] = jnp.sum(grad_middle, axis=0, keepdims=True)
    sums_ref[3:4] = jnp.sum(upstream, axis=0, keepdims=True)
    narrow[:, own] = dot_nt(gmb_ref[...], mix_own[...])
    narrow[:, other] = dot_nt(gmb_ref[...], mix_other[...])
    gsend_ref[0:H] = narrow[...].astype(BF16).T.reshape(H, HD, rows)
    for h in range(H, gsend_ref.shape[0]):
        gsend_ref[h] = jnp.zeros(gsend_ref.shape[1:], BF16)


def finish_kernel(
    side_ref, in_ref, x_ref, gm_ref, vec_ref, hid_ref, own_ref, other_ref,
    grad_ref, sums_ref, gj_ref, hid_keep, hid_send, narrow,
):
    rows, width = x_ref.shape
    own, other = halves(side_ref, width // 2)
    vec = vec_ref[...].astype(F32)
    for k in range(3):
        gj_ref[:, k * width : (k + 1) * width] = (
            in_ref[0:H, k * HD : (k + 1) * HD, :].reshape(width, rows).T
        )
    hid_keep[...] = hid_ref[:, own]
    hid_send[...] = hid_ref[:, other]
    unit, inv_std = normalise(x_ref[...].astype(F32))
    narrow[:, own] = dot_nt(gj_ref[...], own_ref[...])
    narrow[:, other] = dot_nt(gj_ref[...], other_ref[...])
    grad_hidden = narrow[...]
    sums_ref[0:1] = jnp.sum(grad_hidden * unit, axis=0, keepdims=True)
    sums_ref[1:2] = jnp.sum(grad_hidden, axis=0, keepdims=True)
    sums_ref[2:3] = jnp.sum(gj_ref[:, :width].astype(F32), axis=0, keepdims=True)
    sums_ref[3:4] = jnp.sum(gj_ref[:, 2 * width :].astype(F32), axis=0, keepdims=True)
    grad_ref[...] = gm_ref[...] + norm_back(grad_hidden * vec[0:1], unit, inv_std)


def block_spans(a, k, rows, cols, paired, count):
    third = cols // 3
    if paired:
        tall, wide = 2 * rows // count, third // 2
        first, start = a // 2 * tall, a % 2 * wide
    else:
        tall, wide = rows // count, third
        first, start = a * tall, 0
    return first, tall, [start + j * LANES for j in range(wide // LANES)]


def pack_kernel(paired, meta_ref, *refs):
    weights = len(paired)
    ins, extra_ref = refs[: 4 * weights], refs[4 * weights]
    outs = refs[4 * weights + 1 : 4 * weights + 7]
    lefts = refs[4 * weights + 7 : -1 : 2]
    rights = refs[4 * weights + 8 : -1 : 2]
    pk = refs[-1]
    count = extra_ref.shape[0]
    for i, (left, right) in enumerate(zip(lefts, rights)):
        rows = left.shape[0] // 2
        for n, dst in enumerate((left, left, right, right)):
            dst[(n % 2) * rows : (n % 2 + 1) * rows] = ins[4 * i + n][...]
    for k, order in enumerate(sum_orders(count)):
        keep_ref, send_ref = outs[2 * k : 2 * k + 2]
        line = 0
        for left, right, pair in zip(lefts, rights, paired):
            third = right.shape[1] // 3
            grad = dot_tn(left[...], right[:, k * third : (k + 1) * third]).astype(BF16)
            for a in range(count):
                first, tall, starts = block_spans(a, k, *grad.shape[:1], 3 * third, pair, count)
                for j, start in enumerate(starts):
                    pk[a, line + j * tall : line + (j + 1) * tall] = grad[
                        first : first + tall, start : start + LANES
                    ]
            line += tall * len(starts)
        for m in range(count):
            dst = keep_ref if m < count // 2 else send_ref
            a = relative_at(m, order) ^ meta_ref[1]
            dst[m % (count // 2), 0:line] = pk[a]
            if k == 0:
                dst[m % (count // 2), line:] = extra_ref[a]


def unpack_kernel(paired, meta_ref, *refs):
    weights = len(paired)
    near_far, outs = refs[:6], refs[6 : 6 + weights]
    extra_ref = refs[6 + weights]
    scratch, sem = refs[7 + weights : -1], refs[-1]
    half = near_far[0].shape[0]
    count = 2 * half
    copies = []
    for k, order in enumerate(sum_orders(count)):
        for m in range(count):
            a = relative_at(m, order) ^ meta_ref[1]
            block = near_far[2 * k + m // half][m % half].astype(F32)
            line = 0
            for dst, pair in zip(scratch, paired):
                rows, third = dst.shape[1:]
                first, tall, starts = block_spans(a, k, rows, 3 * third, pair, count)
                for start in starts:
                    if pair:
                        start = pl.ds(pl.multiple_of(start, LANES), LANES)
                    else:
                        start = slice(start, start + LANES)
                    place = pl.ds(pl.multiple_of(first, 8), tall)
                    dst[k, place, start] = block[line : line + tall]
                    line += tall
            if k == 0:
                extra_ref[a] = block[line:]
        for i, (src, dst) in enumerate(zip(scratch, outs)):
            size = src.shape[2]
            copy = pltpu.make_async_copy(
                src.at[k], dst.at[:, k * size : (k + 1) * size], sem.at[k, i]
            )
            copy.start()
            copies.append(copy)
    for copy in copies:
        copy.wait()


def stack_kernel(*refs):
    out_ref = refs[-1]
    row = 0
    for ref in refs[:-1]:
        line = ref[...].reshape(1, -1)
        for start in range(0, line.shape[1], out_ref.shape[1]):
            out_ref[row : row + 1] = line[:, start : start + out_ref.shape[1]]
            row += 1


SWAP = [(0, 1), (1, 0)]


def pieces(weight, group):
    if group == 2:
        return weight, lax.ppermute(weight, "fsdp", SWAP)
    full = lax.all_gather(weight, "fsdp", axis=0, tiled=True)
    half = full.shape[0] // 2
    return full[:half], full[half:]


def join_vector(vector, group, side):
    if group == 2:
        other = lax.ppermute(vector, "fsdp", SWAP)
        return jnp.where(
            side == 0,
            jnp.concatenate([vector, other], axis=1),
            jnp.concatenate([other, vector], axis=1),
        )
    return lax.all_gather(vector, "fsdp", axis=1, tiled=True)


def swap_side(part):
    return lax.ppermute(part, "fsdp", SWAP)


def rows_over_group(keep, send, right):
    left = jnp.concatenate([keep, send], axis=1)
    left = lax.all_to_all(left, "fsdp", split_axis=1, concat_axis=0, tiled=True)
    return dot_tn(left, lax.all_gather(right, "fsdp", axis=0, tiled=True))


def own_columns(sums, group, side):
    if group == 2:
        half = sums.shape[1] // 2
        keep = lax.dynamic_slice_in_dim(sums, side * half, half, 1)
        send = lax.dynamic_slice_in_dim(sums, (1 - side) * half, half, 1)
        return keep + lax.ppermute(send, "fsdp", SWAP)
    return lax.psum_scatter(sums, "fsdp", scatter_dimension=1, tiled=True)


def swap_bit(part, bit, count):
    return lax.ppermute(part, "ctx", [(d, d ^ (1 << bit)) for d in range(count)])


def add_parts(left, right):
    return (left.astype(F32) + right.astype(F32)).astype(BF16)


class Flow:
    def __init__(self, keeps, sends, count):
        self.keeps, self.sends = list(keeps), list(sends)
        self.orders = sum_orders(count)
        self.bits = len(self.orders[0])
        self.step = 0

    def bit_row(self):
        at = self.bits - 1 - self.step if self.step < self.bits else self.step - self.bits
        return [order[at] for order in self.orders]

    def pending(self):
        parts = self.sends if self.step < self.bits else self.keeps
        row = self.bit_row()
        if len(set(row)) == 1:
            return [(jnp.concatenate(parts, axis=1), row[0])]
        return list(zip(parts, row))

    def accept(self, cames):
        if len(cames) == 1:
            sizes = [part.shape[1] for part in self.keeps]
            ends = [sum(sizes[: k + 1]) for k in range(3)]
            cames = [cames[0][:, end - size : end] for end, size in zip(ends, sizes)]
        half = cames[0].shape[0] // 2
        if self.step < self.bits - 1:
            self.sends = [add_parts(p[half:], c[half:]) for p, c in zip(self.keeps, cames)]
            self.keeps = [add_parts(p[:half], c[:half]) for p, c in zip(self.keeps, cames)]
        elif self.step == self.bits - 1:
            self.keeps = [add_parts(p, c) for p, c in zip(self.keeps, cames)]
        elif self.step == 2 * self.bits - 1:
            self.fars = cames
        else:
            self.keeps = [jnp.concatenate(pair, axis=0) for pair in zip(self.keeps, cames)]
        self.step += 1

    def over(self):
        return self.step == 2 * self.bits


def advance(flows, count):
    flows = [flow for flow in flows if not flow.over()]
    waiting = [flow.pending() for flow in flows]
    cames = lax.optimization_barrier(
        [[swap_bit(part, bit, count) for part, bit in parts] for parts in waiting]
    )
    for flow, came in zip(flows, cames):
        flow.accept(came)


LINES = 16


def pack(pairs, paired, sums, meta, index, group, count):
    extra = sums.reshape(-1, LANES)
    extra = jnp.pad(extra, ((0, LINES * count - extra.shape[0]), (0, 0))).astype(BF16)
    extra = extra.reshape(count, LINES, LANES)
    if group == 2 and count == 16:
        args = []
        for keep, send, right in pairs:
            args += [keep, swap_side(send), right, swap_side(right)]
        size = sum(keep.shape[1] * right.shape[1] for keep, _, right in pairs)
        block = size // 3 // LANES // count
        half = count // 2
        tall = [block + LINES, block, block]
        rows = pairs[0][0].shape[0]
        parts = call(
            functools.partial(pack_kernel, paired),
            [((half, tall[k // 2], LANES), BF16) for k in range(6)],
            [((2 * rows, a.shape[1]), BF16) for a in args[::2]] + [((count, block, LANES), BF16)],
            "pack", 4 * rows * size, meta, *args, extra,
        )
        return Flow(parts[::2], parts[1::2], count)
    weights = [rows_over_group(*pair) for pair in pairs]
    return Flow(*plain_pack(weights, extra, index, count), count)


def unpack(flow, shapes, paired, sums, meta, index, group, count):
    if group == 2 and count == 16:
        near_far = [part for pair in zip(flow.keeps, flow.fars) for part in pair]
        *weights, extra = call(
            functools.partial(unpack_kernel, paired),
            [(s, F32) for s in shapes] + [((count, LINES, LANES), F32)],
            [((3, r, c // 3), F32) for r, c in shapes]
            + [pltpu.SemaphoreType.DMA((3, len(shapes)))],
            "unpack", 0, meta, *near_far, away_outs=len(shapes),
        )
    else:
        weights, extra = plain_unpack(flow.keeps, flow.fars, shapes, LINES, index, count)
    sums = extra.reshape(-1, LANES)[: sums.size // LANES].reshape(sums.shape)
    return weights, sums


def plain_pack(weights, extra, index, count):
    keeps, sends = [], []
    for k, order in enumerate(sum_orders(count)):
        blocks = []
        for weight in weights:
            span = weight.shape[1] // 3
            for start in range(k * span, (k + 1) * span, LANES):
                blocks.append(weight[:, start : start + LANES].astype(BF16))
        flat = jnp.concatenate(blocks, axis=0)
        flat = flat.reshape(count, -1, LANES)
        if k == 0:
            flat = jnp.concatenate([flat, extra], axis=1)
        turn = jnp.array([relative_at(m, order) for m in range(count)], jnp.int32) ^ index
        flat = jnp.take(flat, turn, axis=0)
        keeps.append(flat[: count // 2])
        sends.append(flat[count // 2 :])
    return keeps, sends


def plain_unpack(keeps, fars, shapes, lines, index, count):
    columns = [[] for _ in shapes]
    extra = None
    for k, order in enumerate(sum_orders(count)):
        flat = jnp.concatenate([keeps[k], fars[k]], axis=0)
        turn = place_of(jnp.arange(count, dtype=jnp.int32) ^ index, order)
        flat = jnp.take(flat, turn, axis=0).astype(F32)
        if k == 0:
            extra = flat[:, flat.shape[1] - lines :]
            flat = flat[:, : flat.shape[1] - lines]
        flat = flat.reshape(-1, LANES)
        first = 0
        for i, (rows, cols) in enumerate(shapes):
            for _ in range(cols // 3 // LANES):
                columns[i].append(flat[first : first + rows])
                first += rows
    return [jnp.concatenate(c, axis=1) for c in columns], extra


def body(
    block_input, out_cotangent, block_position, first_gain, first_shift, qkv_weight, query_bias,
    value_bias, output_weight, output_bias, second_gain, second_shift, expand_weight, expand_bias,
    shrink_weight, shrink_bias,
):
    count = lax.axis_size("ctx")
    group = lax.axis_size("fsdp")
    rows, width = block_input.shape[1:]
    ff = expand_weight.shape[1]
    length = count * rows
    side = lax.axis_index("fsdp") if group == 2 else jnp.int32(0)
    index = lax.axis_index("ctx")
    half = width // 2
    three = 3 * HD
    each = width // group
    meta = jnp.stack([side, index]).astype(jnp.int32)
    table = block_position[0]
    places = jnp.arange(count, dtype=jnp.int32)
    slots = jnp.sum(
        jnp.where(table[None, :] == places[:, None], places[None, :], 0), axis=1
    ).astype(jnp.int32)
    x = block_input[0]
    qkv = pieces(qkv_weight, group)
    vectors = (
        first_gain, first_shift, query_bias, value_bias, output_bias, second_gain, second_shift,
        shrink_bias,
    )
    if group == 2:
        (vec,) = call(
            stack_kernel, [((12, each), BF16)], [], "stack", 0, *vectors, expand_bias, smem=0
        )
        vec = join_vector(vec, group, side)
        ebias = vec[8:].reshape(4, group, each).swapaxes(0, 1).reshape(1, ff)
    else:
        vec = join_vector(jnp.stack(vectors), group, side)
        ebias = join_vector(expand_bias[None], group, side)
    qkv, output_weight, expand_weight, shrink_weight = lax.optimization_barrier(
        (qkv, output_weight, expand_weight, shrink_weight)
    )
    mix = pieces(output_weight, group)
    expand = pieces(expand_weight, group)
    shrink = pieces(shrink_weight, group)
    size = width * ff

    hidden_a, qkv_send = call(
        project_kernel,
        [((rows, width), BF16), ((count, three, rows), BF16)],
        [], "project", 6 * rows * width * width,
        meta, x, vec, *qkv,
    )
    qkv_here = lax.all_to_all(qkv_send, "ctx", 0, 0, tiled=True)
    att_send, log_total = call(
        attend_kernel,
        [((count, HD, rows), BF16), ((1, length), F32)],
        [((HD, length), BF16), ((length, HD), BF16), ((HD, length), BF16), ((HD, length), BF16)],
        "attend", 2 * length * length * HD,
        slots, qkv_here,
    )
    att_here = lax.all_to_all(att_send, "ctx", 0, 0, tiled=True)
    (
        result, grad_middle, grad_send, sums, esum, cot_b, act_keep, act_out, hid_keep, hid_out,
        ge_b, att_keep, att_out, gm_b,
    ) = call(
        middle_kernel,
        [
            ((rows, width), BF16), ((rows, width), F32), ((count, HD, rows), BF16),
            ((4, width), F32), ((1, ff), F32), ((rows, width), BF16), ((rows, ff // 2), BF16),
            ((rows, ff // 2), BF16), ((rows, half), BF16), ((rows, half), BF16),
            ((rows, ff), BF16), ((rows, half), BF16), ((rows, half), BF16), ((rows, width), BF16),
        ],
        [
            ((rows, ff), F32), ((rows, ff), BF16), ((rows, ff), BF16), ((rows, width), BF16),
            ((rows, width), BF16), ((rows, width), F32),
        ],
        "middle", 8 * rows * size + 4 * rows * width * width,
        meta, att_here, x, out_cotangent[0], vec, ebias, *mix, *expand, *shrink,
    )
    grad_here = lax.all_to_all(grad_send, "ctx", 0, 0, tiled=True)

    esum = esum.reshape(group, 4, each).swapaxes(0, 1).reshape(4, width)
    sums = own_columns(jnp.concatenate([sums, esum], axis=0), group, side)
    early_kinds = (False, True, True)
    early = pack(
        [(act_keep, act_out, cot_b), (hid_keep, hid_out, ge_b), (att_keep, att_out, gm_b)],
        early_kinds, sums, meta, index, group, count,
    )
    early.keeps, early.sends, grad_here = lax.optimization_barrier(
        (early.keeps, early.sends, grad_here)
    )
    advance([early], count)
    (dqkv_send,) = call(
        attend_back_kernel,
        [((count, three, rows), BF16)],
        [
            ((HD, length), BF16), ((length, HD), BF16), ((HD, length), BF16),
            ((length, HD), BF16), ((length, HD), BF16), ((HD, length), BF16),
            ((length, HD), BF16), ((1, length), F32), ((HD, length), F32), ((HD, length), F32),
            ((HD, length), F32),
        ],
        "attend_back", 5 * length * length * HD,
        slots, qkv_here, att_send, grad_here, log_total,
    )
    early.keeps, early.sends, dqkv_send = lax.optimization_barrier(
        (early.keeps, early.sends, dqkv_send)
    )
    dqkv_here = lax.all_to_all(dqkv_send, "ctx", 0, 0, tiled=True)
    advance([early], count)
    early.keeps, early.sends, dqkv_here = lax.optimization_barrier(
        (early.keeps, early.sends, dqkv_here)
    )
    advance([early], count)
    input_grad, late_sums, gj, hida_keep, hida_out = call(
        finish_kernel,
        [
            ((rows, width), F32), ((4, width), F32), ((rows, 3 * width), BF16),
            ((rows, half), BF16), ((rows, half), BF16),
        ],
        [((rows, width), F32)],
        "finish", 6 * rows * width * width,
        meta, dqkv_here, x, grad_middle, vec, hidden_a, *qkv,
    )
    late_sums = own_columns(late_sums, group, side)
    late = pack([(hida_keep, hida_out, gj)], (True,), late_sums, meta, index, group, count)
    while not early.over():
        advance([early, late], count)
    (grad_shrink, grad_expand, grad_mix), sums = unpack(
        early, ((4 * each, width), (each, ff), (each, width)), early_kinds, sums, meta, index,
        group, count,
    )
    while not late.over():
        advance([late], count)
    (grad_qkv,), late_sums = unpack(
        late, ((each, 3 * width),), (True,), late_sums, meta, index, group, count
    )
    return (
        result[None], input_grad[None], late_sums[0], late_sums[1], grad_qkv, late_sums[2],
        late_sums[3], grad_mix, sums[0], sums[1], sums[2], grad_expand, sums[4:8].reshape(-1),
        grad_shrink, sums[3],
    )


def solution(mesh):
    block = P("fsdp", "ctx", None)
    vector, matrix = P("fsdp"), P("fsdp", None)
    return jax.shard_map(
        body,
        mesh=mesh,
        in_specs=(
            block, block, matrix, vector, vector, matrix, vector, vector, matrix, vector, vector,
            vector, matrix, vector, matrix, vector,
        ),
        out_specs=(
            block, block, vector, vector, matrix, vector, vector, matrix, vector, vector, vector,
            matrix, vector, matrix, vector,
        ),
        check_vma=False,
    )
```

```python
import functools

import jax
import jax.numpy as jnp
from jax import lax
from jax.experimental import pallas as pl
from jax.experimental.pallas import tpu as pltpu
from jax.sharding import PartitionSpec as P

H = 12
HD = 64
NORM_EPS = 1e-05
MASK_FLOOR = -1e30
GELU_COEF = 0.7978845608028654
GELU_CUBE = 0.044715
SCALE = HD ** (-0.5)
F32 = jnp.float32
BF16 = jnp.bfloat16
LANES = 128
LINES = 16
MIB = 1024 * 1024


def dot_nn(left, right):
    return lax.dot_general(left, right, (((1,), (0,)), ((), ())), preferred_element_type=F32)


def dot_nt(left, right):
    return lax.dot_general(left, right, (((1,), (1,)), ((), ())), preferred_element_type=F32)


def dot_tn(left, right):
    return lax.dot_general(left, right, (((0,), (0,)), ((), ())), preferred_element_type=F32)


def normalise(inputs):
    centred = inputs - jnp.mean(inputs, axis=-1, keepdims=True)
    inv_std = lax.rsqrt(jnp.mean(centred * centred, axis=-1, keepdims=True) + NORM_EPS)
    return centred * inv_std, inv_std


def norm_back(scaled, unit, inv_std):
    return inv_std * (
        scaled
        - jnp.mean(scaled, axis=-1, keepdims=True)
        - unit * jnp.mean(scaled * unit, axis=-1, keepdims=True)
    )


def whole_vectors(side_ref, mine_ref, theirs_ref, rows):
    mine, theirs = mine_ref[rows].astype(F32), theirs_ref[rows].astype(F32)
    first = side_ref[0] == 0
    left, right = jnp.where(first, mine, theirs), jnp.where(first, theirs, mine)
    return jnp.concatenate([left, right], axis=1)


def halves(side_ref, size):
    side = side_ref[0]
    own = pl.ds(pl.multiple_of(side * size, 128), size)
    other = pl.ds(pl.multiple_of((1 - side) * size, 128), size)
    return own, other


def call(kernel, outs, scratch, name, flops, *args, smem=1, away=0, away_outs=0):
    vmem = pl.BlockSpec(memory_space=pltpu.VMEM)
    anywhere = pl.BlockSpec(memory_space=pl.ANY)
    specs = [pl.BlockSpec(memory_space=pltpu.SMEM)] * smem
    specs += [vmem] * (len(args) - smem - away) + [anywhere] * away
    moved = sum(a.size * a.dtype.itemsize for a in args)
    return pl.pallas_call(
        kernel,
        out_shape=[jax.ShapeDtypeStruct(s, d) for s, d in outs],
        in_specs=specs,
        out_specs=[anywhere] * away_outs + [vmem] * (len(outs) - away_outs),
        scratch_shapes=[pltpu.VMEM(*s) if isinstance(s, tuple) else s for s in scratch],
        compiler_params=pltpu.CompilerParams(vmem_limit_bytes=56 * MIB),
        cost_estimate=pl.CostEstimate(flops=flops, bytes_accessed=moved, transcendentals=0),
        name=name,
    )(*args)


def bits_of(count):
    return list(range(count.bit_length() - 1))


def sum_orders(count, parts):
    turn, last = bits_of(count)[:parts], bits_of(count)[parts:]
    return [list(reversed(turn[k:] + turn[:k] + last)) for k in range(parts)]


def place_of(r, order):
    place = 0
    for s, bit in enumerate(order):
        place = place | (((r >> bit) & 1) << s)
    return place


def relative_at(place, order):
    return sum(((place >> s) & 1) << bit for s, bit in enumerate(order))


def project_kernel(side_ref, x_ref, mine_ref, theirs_ref, own_ref, other_ref, hid_ref, send_ref):
    rows, width = x_ref.shape
    own, other = halves(side_ref, width // 2)
    unit, _ = normalise(x_ref[...].astype(F32))
    vec = whole_vectors(side_ref, mine_ref, theirs_ref, slice(0, 8))
    hid_ref[...] = (unit * vec[0:1] + vec[1:2]).astype(BF16)
    joint = dot_nn(hid_ref[:, own], own_ref[...]) + dot_nn(hid_ref[:, other], other_ref[...])
    three = (
        (joint[:, :width] + vec[2:3]).astype(BF16),
        joint[:, width : 2 * width].astype(BF16),
        (joint[:, 2 * width :] + vec[3:4]).astype(BF16),
    )
    for k, part in enumerate(three):
        turned = part.T
        for h in range(H):
            send_ref[h, k * HD : (k + 1) * HD, :] = turned[h * HD : (h + 1) * HD]
    for h in range(H, send_ref.shape[0]):
        send_ref[h] = jnp.zeros(send_ref.shape[1:], BF16)


def attend_kernel(slot_ref, in_ref, out_ref, total_ref, q_t, k_n, v_t, o_t):
    count, _, rows = in_ref.shape
    tile = 512
    for p in range(count):
        slot = slot_ref[p]
        where = slice(p * rows, (p + 1) * rows)
        q_t[:, where] = in_ref[slot, 0:HD, :] * jnp.asarray(SCALE, BF16)
        k_n[where, :] = in_ref[slot, HD : 2 * HD, :].T
        v_t[:, where] = in_ref[slot, 2 * HD : 3 * HD, :]
    length = count * rows
    below = lax.broadcasted_iota(jnp.int32, (tile, tile), 0) <= lax.broadcasted_iota(
        jnp.int32, (tile, tile), 1
    )
    for i in range(length // tile):
        here = slice(i * tile, (i + 1) * tile)
        query = q_t[:, here]
        scores = jnp.where(below, dot_nn(k_n[here, :], query), MASK_FLOOR)
        best = jnp.max(scores, axis=0, keepdims=True)
        weights = jnp.exp(scores - best)
        total = jnp.sum(weights, axis=0, keepdims=True)
        mixed = dot_nn(v_t[:, here], weights.astype(BF16))

        def step(j, state, query=query):
            best, total, mixed = state
            span = pl.ds(pl.multiple_of(j * tile, tile), tile)
            scores = dot_nn(k_n[span, :], query)
            new_best = jnp.maximum(best, jnp.max(scores, axis=0, keepdims=True))
            factor = jnp.exp(best - new_best)
            weights = jnp.exp(scores - new_best)
            total = total * factor + jnp.sum(weights, axis=0, keepdims=True)
            mixed = mixed * factor + dot_nn(v_t[:, span], weights.astype(BF16))
            return new_best, total, mixed

        if i:
            best, total, mixed = lax.fori_loop(0, i, step, (best, total, mixed))
        o_t[:, here] = (mixed / total).astype(BF16)
        total_ref[:, here] = best + jnp.log(total)
    for p in range(count):
        out_ref[slot_ref[p]] = o_t[:, p * rows : (p + 1) * rows]


def attend_back_kernel(
    slot_ref, in_ref, att_ref, grad_ref, total_ref, out_ref,
    q_t, q_n, k_t, k_n, v_n, g_t, g_n, delta, dq_t, dk_t, dv_t,
):
    count, _, rows = in_ref.shape
    tile = 512
    for p in range(count):
        slot = slot_ref[p]
        where = slice(p * rows, (p + 1) * rows)
        query = in_ref[slot, 0:HD, :] * jnp.asarray(SCALE, BF16)
        q_t[:, where] = query
        q_n[where, :] = query.T
        key = in_ref[slot, HD : 2 * HD, :]
        k_t[:, where] = key
        k_n[where, :] = key.T
        v_n[where, :] = in_ref[slot, 2 * HD : 3 * HD, :].T
        grad = grad_ref[slot]
        g_t[:, where] = grad
        g_n[where, :] = grad.T
        delta[:, where] = jnp.sum(
            grad.astype(F32) * att_ref[slot].astype(F32), axis=0, keepdims=True
        )
    length = count * rows
    tiles = length // tile
    below = lax.broadcasted_iota(jnp.int32, (tile, tile), 0) <= lax.broadcasted_iota(
        jnp.int32, (tile, tile), 1
    )
    dq_t[...] = jnp.zeros_like(dq_t)
    for j in range(tiles):
        here = slice(j * tile, (j + 1) * tile)

        def step(i, state, masked=False, here=here):
            key_sum, value_sum = state
            span = pl.ds(pl.multiple_of(i * tile, tile), tile)
            scores = dot_nn(k_n[here, :], q_t[:, span])
            probs = jnp.exp(scores - total_ref[:, span])
            if masked:
                probs = jnp.where(below, probs, 0.0)
            prob_grad = dot_nn(v_n[here, :], g_t[:, span])
            score_grad = (probs * (prob_grad - delta[:, span])).astype(BF16)
            value_sum = value_sum + dot_nn(probs.astype(BF16), g_n[span, :])
            key_sum = key_sum + dot_nn(score_grad, q_n[span, :])
            dq_t[:, span] = dq_t[:, span] + dot_nn(k_t[:, here], score_grad)
            return key_sum, value_sum

        zero = jnp.zeros((tile, HD), F32)
        state = step(j, (zero, zero), masked=True)
        if j + 1 < tiles:
            state = lax.fori_loop(j + 1, tiles, step, state)
        dk_t[:, here] = state[0].T
        dv_t[:, here] = state[1].T
    for p in range(count):
        slot = slot_ref[p]
        where = slice(p * rows, (p + 1) * rows)
        out_ref[slot, 0:HD, :] = (dq_t[:, where] * SCALE).astype(BF16)
        out_ref[slot, HD : 2 * HD, :] = dk_t[:, where].astype(BF16)
        out_ref[slot, 2 * HD : 3 * HD, :] = dv_t[:, where].astype(BF16)


def split_sums(first, sums, keep_ref, send_ref):
    for r, line in enumerate(sums):
        half = line.shape[1] // 2
        low, high = line[:, :half], line[:, half:]
        keep_ref[r : r + 1] = jnp.where(first, low, high)
        send_ref[r : r + 1] = jnp.where(first, high, low)


def middle_kernel(
    side_ref, att_in, x_ref, cot_ref, mine_ref, theirs_ref, *refs,
):
    sources, refs = refs[:6], refs[6:]
    (
        res_ref, gm_ref, gsend_ref, sums_keep, sums_send,
        cotb_ref, act_keep, act_send, hid_keep, hid_send, ge_ref, att_keep, att_send, gmb_ref,
        wide, act_s, hid_s, att_s, narrow, *weights, sem,
    ) = refs
    mix_own, mix_other, ex_own, ex_other, sh_own, sh_other = weights
    copies = [
        pltpu.make_async_copy(src, dst, sem.at[i])
        for i, (src, dst) in enumerate(zip(sources, weights))
    ]
    for copy in copies:
        copy.start()
    rows, width = x_ref.shape
    ff = wide.shape[1]
    part = ff // 8
    own, other = halves(side_ref, width // 2)
    fown, fother = halves(side_ref, ff // 2)
    vec = whole_vectors(side_ref, mine_ref, theirs_ref, slice(0, 8))
    first = side_ref[0] == 0
    lines = [
        [ref[8 + r : 9 + r].astype(F32) for r in range(4)] for ref in (mine_ref, theirs_ref)
    ]
    ebias = jnp.concatenate(
        [jnp.where(first, a, b) for a, b in zip(*lines)]
        + [jnp.where(first, b, a) for a, b in zip(*lines)],
        axis=1,
    )
    att_s[...] = att_in[0:H].reshape(width, rows).T
    att_keep[...] = att_s[:, own]
    att_send[...] = att_s[:, other]
    copies[0].wait()
    copies[1].wait()
    middle = (
        x_ref[...].astype(F32)
        + (dot_nn(att_keep[...], mix_own[...]) + dot_nn(att_send[...], mix_other[...]))
        + vec[4:5]
    )
    unit, inv_std = normalise(middle)
    hid_s[...] = (unit * vec[5:6] + vec[6:7]).astype(BF16)
    hid_keep[...] = hid_s[:, own]
    hid_send[...] = hid_s[:, other]
    copies[2].wait()
    copies[3].wait()
    expanded = (
        dot_nn(hid_keep[...], ex_own[...])
        + dot_nn(hid_send[...], ex_other[...])
        + ebias
    )
    square = expanded * expanded
    bend = jnp.tanh(GELU_COEF * (expanded + GELU_CUBE * square * expanded))
    act_s[...] = (0.5 * expanded * (1.0 + bend)).astype(BF16)
    slope = 0.5 * (1.0 + bend) + 0.5 * expanded * (1.0 - bend * bend) * GELU_COEF * (
        1.0 + 3.0 * GELU_CUBE * square
    )
    act_keep[...] = act_s[:, fown]
    act_send[...] = act_s[:, fother]
    copies[4].wait()
    copies[5].wait()
    result = (
        middle
        + (dot_nn(act_keep[...], sh_own[...]) + dot_nn(act_send[...], sh_other[...]))
        + vec[7:8]
    )
    res_ref[...] = result.astype(BF16)
    upstream = cot_ref[...]
    cotb_ref[...] = upstream.astype(BF16)
    wide[:, fown] = dot_nt(cotb_ref[...], sh_own[...])
    wide[:, fother] = dot_nt(cotb_ref[...], sh_other[...])
    grad_expanded = wide[...] * slope
    esum = jnp.sum(grad_expanded, axis=0, keepdims=True)
    for r in range(4):
        low = esum[:, r * part : (r + 1) * part]
        high = esum[:, (4 + r) * part : (5 + r) * part]
        sums_keep[4 + r : 5 + r] = jnp.where(first, low, high)
        sums_send[4 + r : 5 + r] = jnp.where(first, high, low)
    ge_ref[...] = grad_expanded.astype(BF16)
    narrow[:, own] = dot_nt(ge_ref[...], ex_own[...])
    narrow[:, other] = dot_nt(ge_ref[...], ex_other[...])
    grad_hidden = narrow[...]
    sums = [jnp.sum(s, axis=0, keepdims=True) for s in (grad_hidden * unit, grad_hidden)]
    grad_middle = upstream + norm_back(grad_hidden * vec[5:6], unit, inv_std)
    gm_ref[...] = grad_middle
    gmb_ref[...] = grad_middle.astype(BF16)
    sums = [jnp.sum(grad_middle, axis=0, keepdims=True)] + sums
    sums += [jnp.sum(upstream, axis=0, keepdims=True)]
    split_sums(first, sums, sums_keep, sums_send)
    narrow[:, own] = dot_nt(gmb_ref[...], mix_own[...])
    narrow[:, other] = dot_nt(gmb_ref[...], mix_other[...])
    gsend_ref[0:H] = narrow[...].astype(BF16).T.reshape(H, HD, rows)
    for h in range(H, gsend_ref.shape[0]):
        gsend_ref[h] = jnp.zeros(gsend_ref.shape[1:], BF16)


def finish_kernel(
    side_ref, in_ref, x_ref, gm_ref, mine_ref, theirs_ref, hid_ref, own_ref, other_ref,
    grad_ref, sums_keep, sums_send, gj_ref, hid_keep, hid_send, narrow,
):
    rows, width = x_ref.shape
    own, other = halves(side_ref, width // 2)
    gain = whole_vectors(side_ref, mine_ref, theirs_ref, slice(0, 1))
    for k in range(3):
        gj_ref[:, k * width : (k + 1) * width] = (
            in_ref[0:H, k * HD : (k + 1) * HD, :].reshape(width, rows).T
        )
    hid_keep[...] = hid_ref[:, own]
    hid_send[...] = hid_ref[:, other]
    unit, inv_std = normalise(x_ref[...].astype(F32))
    narrow[:, own] = dot_nt(gj_ref[...], own_ref[...])
    narrow[:, other] = dot_nt(gj_ref[...], other_ref[...])
    grad_hidden = narrow[...]
    joint = gj_ref[...].astype(F32)
    sums = (grad_hidden * unit, grad_hidden, joint[:, :width], joint[:, 2 * width :])
    sums = [jnp.sum(s, axis=0, keepdims=True) for s in sums]
    split_sums(side_ref[0] == 0, sums, sums_keep, sums_send)
    grad_ref[...] = gm_ref[...] + norm_back(grad_hidden * gain, unit, inv_std)


def block_spans(a, rows, wide, paired, count):
    if paired:
        tall, wide = 2 * rows // count, wide // 2
        first, start = a // 2 * tall, a % 2 * wide
    else:
        tall = rows // count
        first, start = a * tall, 0
    return first, tall, [start + j * LANES for j in range(wide // LANES)]


def pack_kernel(paired, parts, meta_ref, *refs):
    weights = len(paired)
    ins, (keep_sums, came_sums) = refs[: 4 * weights], refs[4 * weights : 4 * weights + 2]
    outs, refs = refs[4 * weights + 2 :][: 2 * parts], refs[4 * weights + 2 + 2 * parts :]
    lefts, rights, (pk, extra) = refs[:-2:2], refs[1:-2:2], refs[-2:]
    count = pk.shape[0]
    for i, (left, right) in enumerate(zip(lefts, rights)):
        rows = left.shape[0] // 2
        for n, dst in enumerate((left, left, right, right)):
            dst[(n % 2) * rows : (n % 2 + 1) * rows] = ins[4 * i + n][...]
    extra[...] = jnp.zeros_like(extra)
    sums = keep_sums[...] + came_sums[...]
    each = sums.shape[1] // LANES
    for q in range(sums.shape[0] * each):
        extra[q // LINES, q % LINES : q % LINES + 1] = sums[
            q // each : q // each + 1, q % each * LANES : (q % each + 1) * LANES
        ]
    for k, order in enumerate(sum_orders(count, parts)):
        keep_ref, send_ref = outs[2 * k : 2 * k + 2]
        line = 0
        for left, right, pair in zip(lefts, rights, paired):
            wide = right.shape[1] // parts
            grad = dot_tn(left[...], right[:, k * wide : (k + 1) * wide]).astype(pk.dtype)
            for a in range(count):
                first, tall, starts = block_spans(a, grad.shape[0], wide, pair, count)
                for j, start in enumerate(starts):
                    pk[a, line + j * tall : line + (j + 1) * tall] = grad[
                        first : first + tall, start : start + LANES
                    ]
            line += tall * len(starts)
        for m in range(count):
            dst = keep_ref if m < count // 2 else send_ref
            a = relative_at(m, order) ^ meta_ref[1]
            dst[m % (count // 2), 0:line] = pk[a].astype(BF16)
            if k == 0:
                dst[m % (count // 2), line:] = extra[a].astype(BF16)


def unpack_kernel(paired, parts, meta_ref, *refs):
    weights = len(paired)
    near_far, refs = refs[: 2 * parts], refs[2 * parts :]
    outs, sums_ref, scratch, (extra, sem) = (
        refs[:weights], refs[weights], refs[weights + 1 : -2], refs[-2:],
    )
    half = near_far[0].shape[0]
    count = 2 * half
    copies = []
    for k, order in enumerate(sum_orders(count, parts)):
        for m in range(count):
            a = relative_at(m, order) ^ meta_ref[1]
            block = near_far[2 * k + m // half][m % half].astype(F32)
            line = 0
            for dst, pair in zip(scratch, paired):
                rows, wide = dst.shape[1:]
                first, tall, starts = block_spans(a, rows, wide, pair, count)
                for start in starts:
                    if pair:
                        start = pl.ds(pl.multiple_of(start, LANES), LANES)
                    else:
                        start = slice(start, start + LANES)
                    place = pl.ds(pl.multiple_of(first, 8), tall)
                    dst[k, place, start] = block[line : line + tall]
                    line += tall
            if k == 0:
                extra[a] = block[line:]
        for i, (src, dst) in enumerate(zip(scratch, outs)):
            size = src.shape[2]
            copy = pltpu.make_async_copy(
                src.at[k], dst.at[:, k * size : (k + 1) * size], sem.at[k, i]
            )
            copy.start()
            copies.append(copy)
    each = sums_ref.shape[1] // LANES
    for q in range(sums_ref.shape[0] * each):
        sums_ref[q // each : q // each + 1, q % each * LANES : (q % each + 1) * LANES] = extra[
            q // LINES, q % LINES : q % LINES + 1
        ]
    for copy in copies:
        copy.wait()


def stack_kernel(*refs):
    out_ref = refs[-1]
    row = 0
    for ref in refs[:-1]:
        line = ref[...].reshape(1, -1)
        for start in range(0, line.shape[1], out_ref.shape[1]):
            out_ref[row : row + 1] = line[:, start : start + out_ref.shape[1]]
            row += 1


SWAP = [(0, 1), (1, 0)]


def pieces(weight, group):
    if group == 2:
        return weight, lax.ppermute(weight, "fsdp", SWAP)
    full = lax.all_gather(weight, "fsdp", axis=0, tiled=True)
    half = full.shape[0] // 2
    return full[:half], full[half:]


def join_vector(vector, group, side):
    if group == 2:
        other = lax.ppermute(vector, "fsdp", SWAP)
        return jnp.where(
            side == 0,
            jnp.concatenate([vector, other], axis=1),
            jnp.concatenate([other, vector], axis=1),
        )
    return lax.all_gather(vector, "fsdp", axis=1, tiled=True)


def swap_side(part):
    return lax.ppermute(part, "fsdp", SWAP)


def rows_over_group(keep, send, right):
    left = jnp.concatenate([keep, send], axis=1)
    left = lax.all_to_all(left, "fsdp", split_axis=1, concat_axis=0, tiled=True)
    return dot_tn(left, lax.all_gather(right, "fsdp", axis=0, tiled=True))


def sums_over_group(keep, send, group):
    sums = jnp.concatenate([keep[:4], send[:4]], axis=1)
    width = sums.shape[1]
    if keep.shape[0] > 4:
        wide = jnp.concatenate([keep[4:].reshape(-1), send[4:].reshape(-1)])
        wide = wide.reshape(group, 4, width // group).swapaxes(0, 1).reshape(4, width)
        sums = jnp.concatenate([sums, wide], axis=0)
    return lax.psum_scatter(sums, "fsdp", scatter_dimension=1, tiled=True)


def swap_bit(part, bit, count):
    return lax.ppermute(part, "ctx", [(d, d ^ (1 << bit)) for d in range(count)])


def add_parts(left, right):
    return (left.astype(F32) + right.astype(F32)).astype(BF16)


class Flow:
    def __init__(self, keeps, sends, count):
        self.keeps, self.sends = list(keeps), list(sends)
        self.orders = sum_orders(count, len(self.keeps))
        self.bits = len(self.orders[0])
        self.step = 0

    def bit_row(self):
        at = self.bits - 1 - self.step if self.step < self.bits else self.step - self.bits
        return [order[at] for order in self.orders]

    def pending(self):
        parts = self.sends if self.step < self.bits else self.keeps
        row = self.bit_row()
        if len(set(row)) == 1:
            return [(jnp.concatenate(parts, axis=1), row[0])]
        return list(zip(parts, row))

    def accept(self, cames):
        if len(cames) == 1:
            sizes = [part.shape[1] for part in self.keeps]
            ends = [sum(sizes[: k + 1]) for k in range(len(sizes))]
            cames = [cames[0][:, end - size : end] for end, size in zip(ends, sizes)]
        half = cames[0].shape[0] // 2
        if self.step < self.bits - 1:
            self.sends = [add_parts(p[half:], c[half:]) for p, c in zip(self.keeps, cames)]
            self.keeps = [add_parts(p[:half], c[:half]) for p, c in zip(self.keeps, cames)]
        elif self.step == self.bits - 1:
            self.keeps = [add_parts(p, c) for p, c in zip(self.keeps, cames)]
        elif self.step == 2 * self.bits - 1:
            self.fars = cames
        else:
            self.keeps = [jnp.concatenate(pair, axis=0) for pair in zip(self.keeps, cames)]
        self.step += 1

    def over(self):
        return self.step == 2 * self.bits


def advance(flows, count):
    flows = [flow for flow in flows if not flow.over()]
    waiting = [flow.pending() for flow in flows]
    cames = lax.optimization_barrier(
        [[swap_bit(part, bit, count) for part, bit in parts] for parts in waiting]
    )
    for flow, came in zip(flows, cames):
        flow.accept(came)


def pack(pairs, paired, sums, meta, index, group, count):
    extra = sums.reshape(-1, LANES)
    extra = jnp.pad(extra, ((0, LINES * count - extra.shape[0]), (0, 0))).astype(BF16)
    extra = extra.reshape(count, LINES, LANES)
    if group == 2 and count == 16:
        args = []
        for keep, send, right in pairs:
            args += [keep, swap_side(send), right, swap_side(right)]
        size = sum(keep.shape[1] * right.shape[1] for keep, _, right in pairs)
        block = size // 3 // LANES // count
        half = count // 2
        tall = [block + LINES, block, block]
        rows = pairs[0][0].shape[0]
        parts = call(
            functools.partial(pack_kernel, paired),
            [((half, tall[k // 2], LANES), BF16) for k in range(6)],
            [((2 * rows, a.shape[1]), BF16) for a in args[::2]] + [((count, block, LANES), BF16)],
            "pack", 4 * rows * size, meta, *args, extra,
        )
        return Flow(parts[::2], parts[1::2], count)
    weights = [rows_over_group(*pair) for pair in pairs]
    return Flow(*plain_pack(weights, extra, index, count), count)


def unpack(flow, shapes, paired, sums, meta, index, group, count):
    if group == 2 and count == 16:
        near_far = [part for pair in zip(flow.keeps, flow.fars) for part in pair]
        *weights, extra = call(
            functools.partial(unpack_kernel, paired),
            [(s, F32) for s in shapes] + [((count, LINES, LANES), F32)],
            [((3, r, c // 3), F32) for r, c in shapes]
            + [pltpu.SemaphoreType.DMA((3, len(shapes)))],
            "unpack", 0, meta, *near_far, away_outs=len(shapes),
        )
    else:
        weights, extra = plain_unpack(flow.keeps, flow.fars, shapes, LINES, index, count)
    sums = extra.reshape(-1, LANES)[: sums.size // LANES].reshape(sums.shape)
    return weights, sums


def plain_pack(weights, extra, index, count, parts):
    keeps, sends = [], []
    for k, order in enumerate(sum_orders(count, parts)):
        blocks = []
        for weight in weights:
            span = weight.shape[1] // parts
            for start in range(k * span, (k + 1) * span, LANES):
                blocks.append(weight[:, start : start + LANES].astype(BF16))
        flat = jnp.concatenate(blocks, axis=0)
        flat = flat.reshape(count, -1, LANES)
        if k == 0:
            flat = jnp.concatenate([flat, extra], axis=1)
        turn = jnp.array([relative_at(m, order) for m in range(count)], jnp.int32) ^ index
        flat = jnp.take(flat, turn, axis=0)
        keeps.append(flat[: count // 2])
        sends.append(flat[count // 2 :])
    return keeps, sends


def plain_unpack(keeps, fars, shapes, index, count, parts):
    columns = [[] for _ in shapes]
    extra = None
    for k, order in enumerate(sum_orders(count, parts)):
        flat = jnp.concatenate([keeps[k], fars[k]], axis=0)
        turn = place_of(jnp.arange(count, dtype=jnp.int32) ^ index, order)
        flat = jnp.take(flat, turn, axis=0).astype(F32)
        if k == 0:
            extra = flat[:, flat.shape[1] - LINES :]
            flat = flat[:, : flat.shape[1] - LINES]
        flat = flat.reshape(-1, LANES)
        first = 0
        for i, (rows, cols) in enumerate(shapes):
            for _ in range(cols // parts // LANES):
                columns[i].append(flat[first : first + rows])
                first += rows
    return [jnp.concatenate(c, axis=1) for c in columns], extra


def pack(pairs, paired, parts, sums, meta, index, group, count):
    keep_sums, send_sums = sums
    if group == 2 and count == 16:
        args = []
        for keep, send, right in pairs:
            args += [keep, swap_side(send), right, swap_side(right)]
        size = sum(keep.shape[1] * right.shape[1] for keep, _, right in pairs)
        block = size // parts // LANES // count
        half = count // 2
        rows = pairs[0][0].shape[0]
        kind = BF16 if block % 16 == 0 else F32
        outs = [
            ((half, block + (LINES if k // 2 == 0 else 0), LANES), BF16) for k in range(2 * parts)
        ]
        flows = call(
            functools.partial(pack_kernel, paired, parts), outs,
            [((2 * rows, a.shape[1]), BF16) for a in args[::2]]
            + [((count, block, LANES), kind), ((count, LINES, LANES), F32)],
            "pack", 4 * rows * size, meta, *args, keep_sums, swap_side(send_sums),
        )
        return Flow(flows[::2], flows[1::2], count)
    extra = sums_over_group(keep_sums, send_sums, group).reshape(-1, LANES)
    extra = jnp.pad(extra, ((0, LINES * count - extra.shape[0]), (0, 0))).astype(BF16)
    extra = extra.reshape(count, LINES, LANES)
    weights = [rows_over_group(*pair) for pair in pairs]
    return Flow(*plain_pack(weights, extra, index, count, parts), count)


def unpack(flow, shapes, paired, vectors, meta, index, group, count):
    parts = len(flow.keeps)
    each = shapes[-1][0]
    if group == 2 and count == 16:
        near_far = [part for pair in zip(flow.keeps, flow.fars) for part in pair]
        *weights, sums = call(
            functools.partial(unpack_kernel, paired, parts),
            [(s, F32) for s in shapes] + [((vectors, each), F32)],
            [((parts, r, c // parts), F32) for r, c in shapes]
            + [((count, LINES, LANES), F32), pltpu.SemaphoreType.DMA((parts, len(shapes)))],
            "unpack", 0, meta, *near_far, away_outs=len(shapes),
        )
        return weights, sums
    weights, extra = plain_unpack(flow.keeps, flow.fars, shapes, index, count, parts)
    return weights, extra.reshape(-1)[: vectors * each].reshape(vectors, each)


def body(
    block_input, out_cotangent, block_position, first_gain, first_shift, qkv_weight, query_bias,
    value_bias, output_weight, output_bias, second_gain, second_shift, expand_weight, expand_bias,
    shrink_weight, shrink_bias,
):
    count = lax.axis_size("ctx")
    group = lax.axis_size("fsdp")
    rows, width = block_input.shape[1:]
    ff = expand_weight.shape[1]
    length = count * rows
    side = lax.axis_index("fsdp") if group == 2 else jnp.int32(0)
    index = lax.axis_index("ctx")
    half = width // 2
    three = 3 * HD
    each = width // group
    meta = jnp.stack([side, index]).astype(jnp.int32)
    table = block_position[0]
    places = jnp.arange(count, dtype=jnp.int32)
    slots = jnp.sum(
        jnp.where(table[None, :] == places[:, None], places[None, :], 0), axis=1
    ).astype(jnp.int32)
    x = block_input[0]
    vectors = (
        first_gain, first_shift, query_bias, value_bias, output_bias, second_gain, second_shift,
        shrink_bias,
    )
    if group == 2:
        (mine,) = call(
            stack_kernel, [((12, each), BF16)], [], "stack", 0, *vectors, expand_bias, smem=0
        )
        mine, qkv_weight = lax.optimization_barrier((mine, qkv_weight))
        vec = mine, swap_side(mine)
    else:
        lines = lax.all_gather(jnp.stack(vectors), "fsdp", axis=1, tiled=True)
        wide = lax.all_gather(expand_bias, "fsdp", axis=0, tiled=True).reshape(2, 4, half)
        vec = [
            jnp.concatenate([lines[:, i * half : (i + 1) * half], wide[i]], axis=0)
            for i in range(2)
        ]
    qkv = pieces(qkv_weight, group)
    qkv, output_weight, expand_weight, shrink_weight = lax.optimization_barrier(
        (qkv, output_weight, expand_weight, shrink_weight)
    )
    mix = pieces(output_weight, group)
    expand = pieces(expand_weight, group)
    shrink = pieces(shrink_weight, group)
    size = width * ff

    hidden_a, qkv_send = call(
        project_kernel,
        [((rows, width), BF16), ((count, three, rows), BF16)],
        [], "project", 6 * rows * width * width,
        meta, x, *vec, *qkv,
    )
    qkv_here = lax.all_to_all(qkv_send, "ctx", 0, 0, tiled=True)
    att_send, log_total = call(
        attend_kernel,
        [((count, HD, rows), BF16), ((1, length), F32)],
        [((HD, length), BF16), ((length, HD), BF16), ((HD, length), BF16), ((HD, length), BF16)],
        "attend", 2 * length * length * HD,
        slots, qkv_here,
    )
    att_here = lax.all_to_all(att_send, "ctx", 0, 0, tiled=True)
    (
        result, grad_middle, grad_send, keep_sums, send_sums, cot_b, act_keep, act_out, hid_keep,
        hid_out, ge_b, att_keep, att_out, gm_b,
    ) = call(
        middle_kernel,
        [
            ((rows, width), BF16), ((rows, width), F32), ((count, HD, rows), BF16),
            ((8, half), F32), ((8, half), F32), ((rows, width), BF16), ((rows, ff // 2), BF16),
            ((rows, ff // 2), BF16), ((rows, half), BF16), ((rows, half), BF16),
            ((rows, ff), BF16), ((rows, half), BF16), ((rows, half), BF16), ((rows, width), BF16),
        ],
        [
            ((rows, ff), F32), ((rows, ff), BF16), ((rows, width), BF16), ((rows, width), BF16),
            ((rows, width), F32),
        ]
        + [(w.shape, BF16) for w in (*mix, *expand, *shrink)]
        + [pltpu.SemaphoreType.DMA((6,))],
        "middle", 8 * rows * size + 4 * rows * width * width,
        meta, att_here, x, out_cotangent[0], *vec, *mix, *expand, *shrink, away=6,
    )
    grad_here = lax.all_to_all(grad_send, "ctx", 0, 0, tiled=True)

    early_kinds = (False, True, True)
    early = pack(
        [(act_keep, act_out, cot_b), (hid_keep, hid_out, ge_b), (att_keep, att_out, gm_b)],
        early_kinds, 3, (keep_sums, send_sums), meta, index, group, count,
    )
    early.keeps, early.sends, grad_here = lax.optimization_barrier(
        (early.keeps, early.sends, grad_here)
    )
    advance([early], count)
    (dqkv_send,) = call(
        attend_back_kernel,
        [((count, three, rows), BF16)],
        [
            ((HD, length), BF16), ((length, HD), BF16), ((HD, length), BF16),
            ((length, HD), BF16), ((length, HD), BF16), ((HD, length), BF16),
            ((length, HD), BF16), ((1, length), F32), ((HD, length), F32), ((HD, length), F32),
            ((HD, length), F32),
        ],
        "attend_back", 5 * length * length * HD,
        slots, qkv_here, att_send, grad_here, log_total,
    )
    dqkv_here = lax.all_to_all(dqkv_send, "ctx", 0, 0, tiled=True)
    early.keeps, early.sends, _ = lax.optimization_barrier(
        (early.keeps, early.sends, dqkv_send)
    )
    advance([early], count)
    advance([early], count)
    input_grad, keep_sums, send_sums, gj, hida_keep, hida_out = call(
        finish_kernel,
        [
            ((rows, width), F32), ((4, half), F32), ((4, half), F32), ((rows, 3 * width), BF16),
            ((rows, half), BF16), ((rows, half), BF16),
        ],
        [((rows, width), F32)],
        "finish", 6 * rows * width * width,
        meta, dqkv_here, x, grad_middle, *vec, hidden_a, *qkv,
    )
    late = pack(
        [(hida_keep, hida_out, gj)], (False,), 2, (keep_sums, send_sums), meta, index, group,
        count,
    )
    while not early.over():
        advance([early, late], count)
    (grad_shrink, grad_expand, grad_mix), sums = unpack(
        early, ((4 * each, width), (each, ff), (each, width)), early_kinds, 8, meta, index,
        group, count,
    )
    while not late.over():
        advance([late], count)
    (grad_qkv,), late_sums = unpack(
        late, ((each, 3 * width),), (False,), 4, meta, index, group, count
    )
    return (
        result[None], input_grad[None], late_sums[0], late_sums[1], grad_qkv, late_sums[2],
        late_sums[3], grad_mix, sums[0], sums[1], sums[2], grad_expand, sums[4:8].reshape(-1),
        grad_shrink, sums[3],
    )


def solution(mesh):
    block = P("fsdp", "ctx", None)
    vector, matrix = P("fsdp"), P("fsdp", None)
    return jax.shard_map(
        body,
        mesh=mesh,
        in_specs=(
            block, block, matrix, vector, vector, matrix, vector, vector, matrix, vector, vector,
            vector, matrix, vector, matrix, vector,
        ),
        out_specs=(
            block, block, vector, vector, matrix, vector, vector, matrix, vector, vector, vector,
            matrix, vector, matrix, vector,
        ),
        check_vma=False,
    )
```

```python
import functools

import jax
import jax.numpy as jnp
from jax import lax
from jax.experimental import pallas as pl
from jax.experimental.pallas import tpu as pltpu
from jax.sharding import PartitionSpec as P

H = 12
HD = 64
NORM_EPS = 1e-05
MASK_FLOOR = -1e30
GELU_COEF = 0.7978845608028654
GELU_CUBE = 0.044715
SCALE = HD ** (-0.5)
F32 = jnp.float32
BF16 = jnp.bfloat16
LANES = 128
LINES = 16
MIB = 1024 * 1024


def dot_nn(left, right):
    return lax.dot_general(left, right, (((1,), (0,)), ((), ())), preferred_element_type=F32)


def dot_nt(left, right):
    return lax.dot_general(left, right, (((1,), (1,)), ((), ())), preferred_element_type=F32)


def dot_tn(left, right):
    return lax.dot_general(left, right, (((0,), (0,)), ((), ())), preferred_element_type=F32)


def normalise(inputs):
    centred = inputs - jnp.mean(inputs, axis=-1, keepdims=True)
    inv_std = lax.rsqrt(jnp.mean(centred * centred, axis=-1, keepdims=True) + NORM_EPS)
    return centred * inv_std, inv_std


def norm_back(scaled, unit, inv_std):
    return inv_std * (
        scaled
        - jnp.mean(scaled, axis=-1, keepdims=True)
        - unit * jnp.mean(scaled * unit, axis=-1, keepdims=True)
    )


def whole_vectors(side_ref, mine_ref, theirs_ref, rows):
    mine, theirs = mine_ref[rows].astype(F32), theirs_ref[rows].astype(F32)
    first = side_ref[0] == 0
    left, right = jnp.where(first, mine, theirs), jnp.where(first, theirs, mine)
    return jnp.concatenate([left, right], axis=1)


def halves(side_ref, size):
    side = side_ref[0]
    own = pl.ds(pl.multiple_of(side * size, 128), size)
    other = pl.ds(pl.multiple_of((1 - side) * size, 128), size)
    return own, other


def call(kernel, outs, scratch, name, flops, *args, smem=1, away=0, away_outs=0):
    vmem = pl.BlockSpec(memory_space=pltpu.VMEM)
    anywhere = pl.BlockSpec(memory_space=pl.ANY)
    specs = [pl.BlockSpec(memory_space=pltpu.SMEM)] * smem
    specs += [vmem] * (len(args) - smem - away) + [anywhere] * away
    moved = sum(a.size * a.dtype.itemsize for a in args)
    return pl.pallas_call(
        kernel,
        out_shape=[jax.ShapeDtypeStruct(s, d) for s, d in outs],
        in_specs=specs,
        out_specs=[anywhere] * away_outs + [vmem] * (len(outs) - away_outs),
        scratch_shapes=[pltpu.VMEM(*s) if isinstance(s, tuple) else s for s in scratch],
        compiler_params=pltpu.CompilerParams(vmem_limit_bytes=56 * MIB),
        cost_estimate=pl.CostEstimate(flops=flops, bytes_accessed=moved, transcendentals=0),
        name=name,
    )(*args)


def bits_of(count):
    return list(range(count.bit_length() - 1))


def sum_orders(count, parts):
    turn, last = bits_of(count)[:parts], bits_of(count)[parts:]
    return [list(reversed(turn[k:] + turn[:k] + last)) for k in range(parts)]


def place_of(r, order):
    place = 0
    for s, bit in enumerate(order):
        place = place | (((r >> bit) & 1) << s)
    return place


def relative_at(place, order):
    return sum(((place >> s) & 1) << bit for s, bit in enumerate(order))


def fetch(sources, targets, sem):
    copies = [
        pltpu.make_async_copy(src, dst, sem.at[i])
        for i, (src, dst) in enumerate(zip(sources, targets))
    ]
    for copy in copies:
        copy.start()
    return copies


def project_kernel(
    side_ref, x_ref, mine_ref, theirs_ref, own_ref, other_ref, hid_ref, send_ref
):
    rows, width = x_ref.shape
    own, other = halves(side_ref, width // 2)
    unit, _ = normalise(x_ref[...].astype(F32))
    vec = whole_vectors(side_ref, mine_ref, theirs_ref, slice(0, 8))
    hid_ref[...] = (unit * vec[0:1] + vec[1:2]).astype(BF16)
    joint = dot_nn(hid_ref[:, own], own_ref[...]) + dot_nn(hid_ref[:, other], other_ref[...])
    three = (
        (joint[:, :width] + vec[2:3]).astype(BF16),
        joint[:, width : 2 * width].astype(BF16),
        (joint[:, 2 * width :] + vec[3:4]).astype(BF16),
    )
    for k, part in enumerate(three):
        turned = part.T
        for h in range(H):
            send_ref[h, k * HD : (k + 1) * HD, :] = turned[h * HD : (h + 1) * HD]
    for h in range(H, send_ref.shape[0]):
        send_ref[h] = jnp.zeros(send_ref.shape[1:], BF16)


def attend_kernel(slot_ref, in_ref, out_ref, total_ref, q_t, k_n, v_t, o_t):
    count, _, rows = in_ref.shape
    tile = 512
    for p in range(count):
        slot = slot_ref[p]
        where = slice(p * rows, (p + 1) * rows)
        q_t[:, where] = in_ref[slot, 0:HD, :] * jnp.asarray(SCALE, BF16)
        k_n[where, :] = in_ref[slot, HD : 2 * HD, :].T
        v_t[:, where] = in_ref[slot, 2 * HD : 3 * HD, :]
    length = count * rows
    below = lax.broadcasted_iota(jnp.int32, (tile, tile), 0) <= lax.broadcasted_iota(
        jnp.int32, (tile, tile), 1
    )
    for i in range(length // tile):
        front, here = slice(0, i * tile), slice(i * tile, (i + 1) * tile)
        query = q_t[:, here]
        spans = [here] + [front] * (i > 0)
        scores = [dot_nn(k_n[span, :], query) for span in spans]
        scores[0] = jnp.where(below, scores[0], MASK_FLOOR)
        best = jnp.max(scores[0], axis=0, keepdims=True)
        for part in scores[1:]:
            best = jnp.maximum(best, jnp.max(part, axis=0, keepdims=True))
        weights = [jnp.exp(part - best) for part in scores]
        total = sum(jnp.sum(part, axis=0, keepdims=True) for part in weights)
        mixed = sum(dot_nn(v_t[:, s], w.astype(BF16)) for s, w in zip(spans, weights))
        o_t[:, here] = (mixed / total).astype(BF16)
        total_ref[:, here] = best + jnp.log(total)
    for p in range(count):
        out_ref[slot_ref[p]] = o_t[:, p * rows : (p + 1) * rows]


def attend_back_kernel(
    slot_ref, in_ref, att_ref, grad_ref, total_ref, out_ref,
    q_t, q_n, k_t, k_n, v_n, g_t, g_n, delta, dq_t, dk_t, dv_t,
):
    count, _, rows = in_ref.shape
    tile = 512
    for p in range(count):
        slot = slot_ref[p]
        where = slice(p * rows, (p + 1) * rows)
        query = in_ref[slot, 0:HD, :] * jnp.asarray(SCALE, BF16)
        q_t[:, where] = query
        q_n[where, :] = query.T
        key = in_ref[slot, HD : 2 * HD, :]
        k_t[:, where] = key
        k_n[where, :] = key.T
        v_n[where, :] = in_ref[slot, 2 * HD : 3 * HD, :].T
        grad = grad_ref[slot]
        g_t[:, where] = grad
        g_n[where, :] = grad.T
        delta[:, where] = jnp.sum(
            grad.astype(F32) * att_ref[slot].astype(F32), axis=0, keepdims=True
        )
    length = count * rows
    tiles = length // tile
    below = lax.broadcasted_iota(jnp.int32, (tile, tile), 0) <= lax.broadcasted_iota(
        jnp.int32, (tile, tile), 1
    )
    dq_t[...] = jnp.zeros_like(dq_t)
    for j in range(tiles):
        here = slice(j * tile, (j + 1) * tile)

        def step(i, state, masked=False, here=here):
            key_sum, value_sum = state
            span = slice(i * tile, (i + 1) * tile)
            scores = dot_nn(k_n[here, :], q_t[:, span])
            probs = jnp.exp(scores - total_ref[:, span])
            if masked:
                probs = jnp.where(below, probs, 0.0)
            prob_grad = dot_nn(v_n[here, :], g_t[:, span])
            score_grad = (probs * (prob_grad - delta[:, span])).astype(BF16)
            value_sum = value_sum + dot_nn(probs.astype(BF16), g_n[span, :])
            key_sum = key_sum + dot_nn(score_grad, q_n[span, :])
            dq_t[:, span] = dq_t[:, span] + dot_nn(k_t[:, here], score_grad)
            return key_sum, value_sum

        zero = jnp.zeros((tile, HD), F32)
        state = step(j, (zero, zero), masked=True)
        for i in range(j + 1, tiles):
            state = step(i, state)
        dk_t[:, here] = state[0].T
        dv_t[:, here] = state[1].T
    for p in range(count):
        slot = slot_ref[p]
        where = slice(p * rows, (p + 1) * rows)
        out_ref[slot, 0:HD, :] = (dq_t[:, where] * SCALE).astype(BF16)
        out_ref[slot, HD : 2 * HD, :] = dk_t[:, where].astype(BF16)
        out_ref[slot, 2 * HD : 3 * HD, :] = dv_t[:, where].astype(BF16)


def split_sums(first, sums, keep_ref, send_ref):
    for r, line in enumerate(sums):
        half = line.shape[1] // 2
        low, high = line[:, :half], line[:, half:]
        keep_ref[r : r + 1] = jnp.where(first, low, high)
        send_ref[r : r + 1] = jnp.where(first, high, low)


def middle_kernel(
    side_ref, att_in, x_ref, cot_ref, mine_ref, theirs_ref, *refs,
):
    sources, refs = refs[:6], refs[6:]
    (
        res_ref, gm_ref, gsend_ref, sums_keep, sums_send,
        cotb_ref, act_keep, act_send, hid_keep, hid_send, ge_ref, att_keep, att_send, gmb_ref,
        wide, act_s, hid_s, att_s, narrow, *weights, sem,
    ) = refs
    mix_own, mix_other, ex_own, ex_other, sh_own, sh_other = weights
    copies = fetch(sources, weights, sem)
    rows, width = x_ref.shape
    ff = wide.shape[1]
    part = ff // 8
    own, other = halves(side_ref, width // 2)
    fown, fother = halves(side_ref, ff // 2)
    vec = whole_vectors(side_ref, mine_ref, theirs_ref, slice(0, 8))
    first = side_ref[0] == 0
    lines = [
        [ref[8 + r : 9 + r].astype(F32) for r in range(4)] for ref in (mine_ref, theirs_ref)
    ]
    ebias = jnp.concatenate(
        [jnp.where(first, a, b) for a, b in zip(*lines)]
        + [jnp.where(first, b, a) for a, b in zip(*lines)],
        axis=1,
    )
    att_s[...] = att_in[0:H].reshape(width, rows).T
    att_keep[...] = att_s[:, own]
    att_send[...] = att_s[:, other]
    copies[0].wait()
    copies[1].wait()
    middle = (
        x_ref[...].astype(F32)
        + (dot_nn(att_keep[...], mix_own[...]) + dot_nn(att_send[...], mix_other[...]))
        + vec[4:5]
    )
    unit, inv_std = normalise(middle)
    hid_s[...] = (unit * vec[5:6] + vec[6:7]).astype(BF16)
    hid_keep[...] = hid_s[:, own]
    hid_send[...] = hid_s[:, other]
    copies[2].wait()
    copies[3].wait()
    expanded = (
        dot_nn(hid_keep[...], ex_own[...])
        + dot_nn(hid_send[...], ex_other[...])
        + ebias
    )
    square = expanded * expanded
    bend = jnp.tanh(GELU_COEF * (expanded + GELU_CUBE * square * expanded))
    act_s[...] = (0.5 * expanded * (1.0 + bend)).astype(BF16)
    slope = 0.5 * (1.0 + bend) + 0.5 * expanded * (1.0 - bend * bend) * GELU_COEF * (
        1.0 + 3.0 * GELU_CUBE * square
    )
    act_keep[...] = act_s[:, fown]
    act_send[...] = act_s[:, fother]
    copies[4].wait()
    copies[5].wait()
    result = (
        middle
        + (dot_nn(act_keep[...], sh_own[...]) + dot_nn(act_send[...], sh_other[...]))
        + vec[7:8]
    )
    res_ref[...] = result.astype(BF16)
    upstream = cot_ref[...]
    cotb_ref[...] = upstream.astype(BF16)
    wide[:, fown] = dot_nt(cotb_ref[...], sh_own[...])
    wide[:, fother] = dot_nt(cotb_ref[...], sh_other[...])
    grad_expanded = wide[...] * slope
    esum = jnp.sum(grad_expanded, axis=0, keepdims=True)
    for r in range(4):
        low = esum[:, r * part : (r + 1) * part]
        high = esum[:, (4 + r) * part : (5 + r) * part]
        sums_keep[4 + r : 5 + r] = jnp.where(first, low, high)
        sums_send[4 + r : 5 + r] = jnp.where(first, high, low)
    ge_ref[...] = grad_expanded.astype(BF16)
    narrow[:, own] = dot_nt(ge_ref[...], ex_own[...])
    narrow[:, other] = dot_nt(ge_ref[...], ex_other[...])
    grad_hidden = narrow[...]
    sums = [jnp.sum(s, axis=0, keepdims=True) for s in (grad_hidden * unit, grad_hidden)]
    grad_middle = upstream + norm_back(grad_hidden * vec[5:6], unit, inv_std)
    gm_ref[...] = grad_middle
    gmb_ref[...] = grad_middle.astype(BF16)
    sums = [jnp.sum(grad_middle, axis=0, keepdims=True)] + sums
    sums += [jnp.sum(upstream, axis=0, keepdims=True)]
    split_sums(first, sums, sums_keep, sums_send)
    narrow[:, own] = dot_nt(gmb_ref[...], mix_own[...])
    narrow[:, other] = dot_nt(gmb_ref[...], mix_other[...])
    gsend_ref[0:H] = narrow[...].astype(BF16).T.reshape(H, HD, rows)
    for h in range(H, gsend_ref.shape[0]):
        gsend_ref[h] = jnp.zeros(gsend_ref.shape[1:], BF16)


def finish_kernel(
    side_ref, in_ref, x_ref, gm_ref, mine_ref, theirs_ref, hid_ref, own_ref, other_ref,
    grad_ref, sums_keep, sums_send, gj_ref, hid_keep, hid_send, narrow,
):
    rows, width = x_ref.shape
    own, other = halves(side_ref, width // 2)
    gain = whole_vectors(side_ref, mine_ref, theirs_ref, slice(0, 1))
    for k in range(3):
        gj_ref[:, k * width : (k + 1) * width] = (
            in_ref[0:H, k * HD : (k + 1) * HD, :].reshape(width, rows).T
        )
    hid_keep[...] = hid_ref[:, own]
    hid_send[...] = hid_ref[:, other]
    unit, inv_std = normalise(x_ref[...].astype(F32))
    narrow[:, own] = dot_nt(gj_ref[...], own_ref[...])
    narrow[:, other] = dot_nt(gj_ref[...], other_ref[...])
    grad_hidden = narrow[...]
    joint = gj_ref[...].astype(F32)
    sums = (grad_hidden * unit, grad_hidden, joint[:, :width], joint[:, 2 * width :])
    sums = [jnp.sum(s, axis=0, keepdims=True) for s in sums]
    split_sums(side_ref[0] == 0, sums, sums_keep, sums_send)
    grad_ref[...] = gm_ref[...] + norm_back(grad_hidden * gain, unit, inv_std)


def block_spans(a, rows, wide, paired, count):
    if paired:
        tall, wide = 2 * rows // count, wide // 2
        first, start = a // 2 * tall, a % 2 * wide
    else:
        tall = rows // count
        first, start = a * tall, 0
    return first, tall, [start + j * LANES for j in range(wide // LANES)]


def pack_kernel(paired, parts, meta_ref, *refs):
    weights = len(paired)
    ins, (keep_sums, came_sums) = refs[: 4 * weights], refs[4 * weights : 4 * weights + 2]
    outs, refs = refs[4 * weights + 2 :][: 2 * parts], refs[4 * weights + 2 + 2 * parts :]
    lefts, rights, (pk, extra) = refs[:-2:2], refs[1:-2:2], refs[-2:]
    count = pk.shape[0]
    for i, (left, right) in enumerate(zip(lefts, rights)):
        rows = left.shape[0] // 2
        for n, dst in enumerate((left, left, right, right)):
            dst[(n % 2) * rows : (n % 2 + 1) * rows] = ins[4 * i + n][...]
    extra[...] = jnp.zeros_like(extra)
    sums = keep_sums[...] + came_sums[...]
    each = sums.shape[1] // LANES
    for q in range(sums.shape[0] * each):
        extra[q // LINES, q % LINES : q % LINES + 1] = sums[
            q // each : q // each + 1, q % each * LANES : (q % each + 1) * LANES
        ]
    for k, order in enumerate(sum_orders(count, parts)):
        keep_ref, send_ref = outs[2 * k : 2 * k + 2]
        line = 0
        for left, right, pair in zip(lefts, rights, paired):
            wide = right.shape[1] // parts
            grad = dot_tn(left[...], right[:, k * wide : (k + 1) * wide]).astype(pk.dtype)
            for a in range(count):
                first, tall, starts = block_spans(a, grad.shape[0], wide, pair, count)
                for j, start in enumerate(starts):
                    pk[a, line + j * tall : line + (j + 1) * tall] = grad[
                        first : first + tall, start : start + LANES
                    ]
            line += tall * len(starts)
        for m in range(count):
            dst = keep_ref if m < count // 2 else send_ref
            a = relative_at(m, order) ^ meta_ref[1]
            dst[m % (count // 2), 0:line] = pk[a].astype(BF16)
            if k == 0:
                dst[m % (count // 2), line:] = extra[a].astype(BF16)


def unpack_kernel(paired, parts, meta_ref, *refs):
    weights = len(paired)
    near_far, refs = refs[: 2 * parts], refs[2 * parts :]
    outs, refs, (extra, sem) = refs[:weights], refs[weights:-2], refs[-2:]
    lines, scratch = refs[:-weights], refs[-weights:]
    half = near_far[0].shape[0]
    count = 2 * half
    copies = []
    for k, order in enumerate(sum_orders(count, parts)):
        for m in range(count):
            a = relative_at(m, order) ^ meta_ref[1]
            block = near_far[2 * k + m // half][m % half].astype(F32)
            line = 0
            for dst, pair in zip(scratch, paired):
                rows, wide = dst.shape[1:]
                first, tall, starts = block_spans(a, rows, wide, pair, count)
                for start in starts:
                    if pair:
                        start = pl.ds(pl.multiple_of(start, LANES), LANES)
                    else:
                        start = slice(start, start + LANES)
                    place = pl.ds(pl.multiple_of(first, 8), tall)
                    dst[k, place, start] = block[line : line + tall]
                    line += tall
            if k == 0:
                extra[a] = block[line:]
        for i, (src, dst) in enumerate(zip(scratch, outs)):
            size = src.shape[2]
            copy = pltpu.make_async_copy(
                src.at[k], dst.at[:, k * size : (k + 1) * size], sem.at[k, i]
            )
            copy.start()
            copies.append(copy)
    each = lines[0].shape[0] // LANES
    for q in range(len(lines) * each):
        lines[q // each][q % each * LANES : (q % each + 1) * LANES] = extra[
            q // LINES, q % LINES, :
        ]
    for copy in copies:
        copy.wait()


def stack_kernel(*refs):
    out_ref = refs[-1]
    row = 0
    for ref in refs[:-1]:
        line = ref[...].reshape(1, -1)
        for start in range(0, line.shape[1], out_ref.shape[1]):
            out_ref[row : row + 1] = line[:, start : start + out_ref.shape[1]]
            row += 1


SWAP = [(0, 1), (1, 0)]


def pieces(weight, group):
    if group == 2:
        return weight, lax.ppermute(weight, "fsdp", SWAP)
    full = lax.all_gather(weight, "fsdp", axis=0, tiled=True)
    half = full.shape[0] // 2
    return full[:half], full[half:]


def join_vector(vector, group, side):
    if group == 2:
        other = lax.ppermute(vector, "fsdp", SWAP)
        return jnp.where(
            side == 0,
            jnp.concatenate([vector, other], axis=1),
            jnp.concatenate([other, vector], axis=1),
        )
    return lax.all_gather(vector, "fsdp", axis=1, tiled=True)


def swap_side(part):
    return lax.ppermute(part, "fsdp", SWAP)


def rows_over_group(keep, send, right):
    left = jnp.concatenate([keep, send], axis=1)
    left = lax.all_to_all(left, "fsdp", split_axis=1, concat_axis=0, tiled=True)
    return dot_tn(left, lax.all_gather(right, "fsdp", axis=0, tiled=True))


def sums_over_group(keep, send, group):
    sums = jnp.concatenate([keep[:4], send[:4]], axis=1)
    width = sums.shape[1]
    if keep.shape[0] > 4:
        wide = jnp.concatenate([keep[4:].reshape(-1), send[4:].reshape(-1)])
        wide = wide.reshape(group, 4, width // group).swapaxes(0, 1).reshape(4, width)
        sums = jnp.concatenate([sums, wide], axis=0)
    return lax.psum_scatter(sums, "fsdp", scatter_dimension=1, tiled=True)


def swap_bit(part, bit, count):
    return lax.ppermute(part, "ctx", [(d, d ^ (1 << bit)) for d in range(count)])


def add_parts(left, right):
    return (left.astype(F32) + right.astype(F32)).astype(BF16)


class Flow:
    def __init__(self, keeps, sends, count):
        self.keeps, self.sends = list(keeps), list(sends)
        self.orders = sum_orders(count, len(self.keeps))
        self.bits = len(self.orders[0])
        self.step = 0

    def bit_row(self):
        at = self.bits - 1 - self.step if self.step < self.bits else self.step - self.bits
        return [order[at] for order in self.orders]

    def pending(self):
        parts = self.sends if self.step < self.bits else self.keeps
        row = self.bit_row()
        if len(set(row)) == 1:
            return [(jnp.concatenate(parts, axis=1), row[0])]
        return list(zip(parts, row))

    def accept(self, cames):
        if len(cames) == 1:
            sizes = [part.shape[1] for part in self.keeps]
            ends = [sum(sizes[: k + 1]) for k in range(len(sizes))]
            cames = [cames[0][:, end - size : end] for end, size in zip(ends, sizes)]
        half = cames[0].shape[0] // 2
        if self.step < self.bits - 1:
            self.sends = [add_parts(p[half:], c[half:]) for p, c in zip(self.keeps, cames)]
            self.keeps = [add_parts(p[:half], c[:half]) for p, c in zip(self.keeps, cames)]
        elif self.step == self.bits - 1:
            self.keeps = [add_parts(p, c) for p, c in zip(self.keeps, cames)]
        elif self.step == 2 * self.bits - 1:
            self.fars = cames
        else:
            self.keeps = [jnp.concatenate(pair, axis=0) for pair in zip(self.keeps, cames)]
        self.step += 1

    def over(self):
        return self.step == 2 * self.bits


def advance(flows, count):
    flows = [flow for flow in flows if not flow.over()]
    waiting = [flow.pending() for flow in flows]
    cames = lax.optimization_barrier(
        [[swap_bit(part, bit, count) for part, bit in parts] for parts in waiting]
    )
    for flow, came in zip(flows, cames):
        flow.accept(came)


def pack(pairs, paired, sums, meta, index, group, count):
    extra = sums.reshape(-1, LANES)
    extra = jnp.pad(extra, ((0, LINES * count - extra.shape[0]), (0, 0))).astype(BF16)
    extra = extra.reshape(count, LINES, LANES)
    if group == 2 and count == 16:
        args = []
        for keep, send, right in pairs:
            args += [keep, swap_side(send), right, swap_side(right)]
        size = sum(keep.shape[1] * right.shape[1] for keep, _, right in pairs)
        block = size // 3 // LANES // count
        half = count // 2
        tall = [block + LINES, block, block]
        rows = pairs[0][0].shape[0]
        parts = call(
            functools.partial(pack_kernel, paired),
            [((half, tall[k // 2], LANES), BF16) for k in range(6)],
            [((2 * rows, a.shape[1]), BF16) for a in args[::2]] + [((count, block, LANES), BF16)],
            "pack", 4 * rows * size, meta, *args, extra,
        )
        return Flow(parts[::2], parts[1::2], count)
    weights = [rows_over_group(*pair) for pair in pairs]
    return Flow(*plain_pack(weights, extra, index, count), count)


def unpack(flow, shapes, paired, sums, meta, index, group, count):
    if group == 2 and count == 16:
        near_far = [part for pair in zip(flow.keeps, flow.fars) for part in pair]
        *weights, extra = call(
            functools.partial(unpack_kernel, paired),
            [(s, F32) for s in shapes] + [((count, LINES, LANES), F32)],
            [((3, r, c // 3), F32) for r, c in shapes]
            + [pltpu.SemaphoreType.DMA((3, len(shapes)))],
            "unpack", 0, meta, *near_far, away_outs=len(shapes),
        )
    else:
        weights, extra = plain_unpack(flow.keeps, flow.fars, shapes, LINES, index, count)
    sums = extra.reshape(-1, LANES)[: sums.size // LANES].reshape(sums.shape)
    return weights, sums


def plain_pack(weights, extra, index, count, parts):
    keeps, sends = [], []
    for k, order in enumerate(sum_orders(count, parts)):
        blocks = []
        for weight in weights:
            span = weight.shape[1] // parts
            for start in range(k * span, (k + 1) * span, LANES):
                blocks.append(weight[:, start : start + LANES].astype(BF16))
        flat = jnp.concatenate(blocks, axis=0)
        flat = flat.reshape(count, -1, LANES)
        if k == 0:
            flat = jnp.concatenate([flat, extra], axis=1)
        turn = jnp.array([relative_at(m, order) for m in range(count)], jnp.int32) ^ index
        flat = jnp.take(flat, turn, axis=0)
        keeps.append(flat[: count // 2])
        sends.append(flat[count // 2 :])
    return keeps, sends


def plain_unpack(keeps, fars, shapes, index, count, parts):
    columns = [[] for _ in shapes]
    extra = None
    for k, order in enumerate(sum_orders(count, parts)):
        flat = jnp.concatenate([keeps[k], fars[k]], axis=0)
        turn = place_of(jnp.arange(count, dtype=jnp.int32) ^ index, order)
        flat = jnp.take(flat, turn, axis=0).astype(F32)
        if k == 0:
            extra = flat[:, flat.shape[1] - LINES :]
            flat = flat[:, : flat.shape[1] - LINES]
        flat = flat.reshape(-1, LANES)
        first = 0
        for i, (rows, cols) in enumerate(shapes):
            for _ in range(cols // parts // LANES):
                columns[i].append(flat[first : first + rows])
                first += rows
    return [jnp.concatenate(c, axis=1) for c in columns], extra


def pack(pairs, paired, parts, sums, meta, index, group, count):
    keep_sums, send_sums = sums
    if group == 2 and count == 16:
        args = []
        for keep, send, right in pairs:
            args += [keep, swap_side(send), right, swap_side(right)]
        size = sum(keep.shape[1] * right.shape[1] for keep, _, right in pairs)
        block = size // parts // LANES // count
        half = count // 2
        rows = pairs[0][0].shape[0]
        kind = BF16 if block % 16 == 0 else F32
        outs = [
            ((half, block + (LINES if k // 2 == 0 else 0), LANES), BF16) for k in range(2 * parts)
        ]
        flows = call(
            functools.partial(pack_kernel, paired, parts), outs,
            [((2 * rows, a.shape[1]), BF16) for a in args[::2]]
            + [((count, block, LANES), kind), ((count, LINES, LANES), F32)],
            "pack", 4 * rows * size, meta, *args, keep_sums, swap_side(send_sums),
        )
        return Flow(flows[::2], flows[1::2], count)
    extra = sums_over_group(keep_sums, send_sums, group).reshape(-1, LANES)
    extra = jnp.pad(extra, ((0, LINES * count - extra.shape[0]), (0, 0))).astype(BF16)
    extra = extra.reshape(count, LINES, LANES)
    weights = [rows_over_group(*pair) for pair in pairs]
    return Flow(*plain_pack(weights, extra, index, count, parts), count)


def unpack(flow, shapes, paired, vectors, meta, index, group, count):
    parts = len(flow.keeps)
    each = shapes[-1][0]
    if group == 2 and count == 16:
        near_far = [part for pair in zip(flow.keeps, flow.fars) for part in pair]
        outs = call(
            functools.partial(unpack_kernel, paired, parts),
            [(s, F32) for s in shapes] + [((each,), F32)] * vectors,
            [((parts, r, c // parts), F32) for r, c in shapes]
            + [((count, LINES, LANES), F32), pltpu.SemaphoreType.DMA((parts, len(shapes)))],
            "unpack", 0, meta, *near_far, away_outs=len(shapes),
        )
        return outs[: len(shapes)], outs[len(shapes) :]
    weights, extra = plain_unpack(flow.keeps, flow.fars, shapes, index, count, parts)
    return weights, list(extra.reshape(-1)[: vectors * each].reshape(vectors, each))


def body(
    block_input, out_cotangent, block_position, first_gain, first_shift, qkv_weight, query_bias,
    value_bias, output_weight, output_bias, second_gain, second_shift, expand_weight, expand_bias,
    shrink_weight, shrink_bias,
):
    count = lax.axis_size("ctx")
    group = lax.axis_size("fsdp")
    rows, width = block_input.shape[1:]
    ff = expand_weight.shape[1]
    length = count * rows
    side = lax.axis_index("fsdp") if group == 2 else jnp.int32(0)
    index = lax.axis_index("ctx")
    half = width // 2
    three = 3 * HD
    each = width // group
    meta = jnp.stack([side, index]).astype(jnp.int32)
    table = block_position[0]
    places = jnp.arange(count, dtype=jnp.int32)
    slots = jnp.sum(
        jnp.where(table[None, :] == places[:, None], places[None, :], 0), axis=1
    ).astype(jnp.int32)
    x = block_input[0]
    vectors = (
        first_gain, first_shift, query_bias, value_bias, output_bias, second_gain, second_shift,
        shrink_bias,
    )
    if group == 2:
        (mine,) = call(
            stack_kernel, [((12, each), BF16)], [], "stack", 0, *vectors, expand_bias, smem=0
        )
        mine, qkv_weight = lax.optimization_barrier((mine, qkv_weight))
        vec = mine, swap_side(mine)
    else:
        lines = lax.all_gather(jnp.stack(vectors), "fsdp", axis=1, tiled=True)
        wide = lax.all_gather(expand_bias, "fsdp", axis=0, tiled=True).reshape(2, 4, half)
        vec = [
            jnp.concatenate([lines[:, i * half : (i + 1) * half], wide[i]], axis=0)
            for i in range(2)
        ]
    qkv = pieces(qkv_weight, group)
    vec, qkv, output_weight, expand_weight, shrink_weight = lax.optimization_barrier(
        (vec, qkv, output_weight, expand_weight, shrink_weight)
    )
    mix = pieces(output_weight, group)
    expand = pieces(expand_weight, group)
    shrink = pieces(shrink_weight, group)
    size = width * ff

    hidden_a, qkv_send = call(
        project_kernel,
        [((rows, width), BF16), ((count, three, rows), BF16)],
        [], "project", 6 * rows * width * width,
        meta, x, *vec, *qkv,
    )
    qkv_here = lax.all_to_all(qkv_send, "ctx", 0, 0, tiled=True)
    att_send, log_total = call(
        attend_kernel,
        [((count, HD, rows), BF16), ((1, length), F32)],
        [((HD, length), BF16), ((length, HD), BF16), ((HD, length), BF16), ((HD, length), BF16)],
        "attend", 2 * length * length * HD,
        slots, qkv_here,
    )
    att_here = lax.all_to_all(att_send, "ctx", 0, 0, tiled=True)
    (
        result, grad_middle, grad_send, keep_sums, send_sums, cot_b, act_keep, act_out, hid_keep,
        hid_out, ge_b, att_keep, att_out, gm_b,
    ) = call(
        middle_kernel,
        [
            ((rows, width), BF16), ((rows, width), F32), ((count, HD, rows), BF16),
            ((8, half), F32), ((8, half), F32), ((rows, width), BF16), ((rows, ff // 2), BF16),
            ((rows, ff // 2), BF16), ((rows, half), BF16), ((rows, half), BF16),
            ((rows, ff), BF16), ((rows, half), BF16), ((rows, half), BF16), ((rows, width), BF16),
        ],
        [
            ((rows, ff), F32), ((rows, ff), BF16), ((rows, width), BF16), ((rows, width), BF16),
            ((rows, width), F32),
        ]
        + [(w.shape, BF16) for w in (*mix, *expand, *shrink)]
        + [pltpu.SemaphoreType.DMA((6,))],
        "middle", 8 * rows * size + 4 * rows * width * width,
        meta, att_here, x, out_cotangent[0], *vec, *mix, *expand, *shrink, away=6,
    )
    grad_here = lax.all_to_all(grad_send, "ctx", 0, 0, tiled=True)

    early_kinds = (False, True, True)
    early = pack(
        [(act_keep, act_out, cot_b), (hid_keep, hid_out, ge_b), (att_keep, att_out, gm_b)],
        early_kinds, 3, (keep_sums, send_sums), meta, index, group, count,
    )
    early.keeps, early.sends, grad_here = lax.optimization_barrier(
        (early.keeps, early.sends, grad_here)
    )
    advance([early], count)
    (dqkv_send,) = call(
        attend_back_kernel,
        [((count, three, rows), BF16)],
        [
            ((HD, length), BF16), ((length, HD), BF16), ((HD, length), BF16),
            ((length, HD), BF16), ((length, HD), BF16), ((HD, length), BF16),
            ((length, HD), BF16), ((1, length), F32), ((HD, length), F32), ((HD, length), F32),
            ((HD, length), F32),
        ],
        "attend_back", 5 * length * length * HD,
        slots, qkv_here, att_send, grad_here, log_total,
    )
    dqkv_here = lax.all_to_all(dqkv_send, "ctx", 0, 0, tiled=True)
    early.keeps, early.sends, _ = lax.optimization_barrier(
        (early.keeps, early.sends, dqkv_send)
    )
    advance([early], count)
    advance([early], count)
    input_grad, keep_sums, send_sums, gj, hida_keep, hida_out = call(
        finish_kernel,
        [
            ((rows, width), F32), ((4, half), F32), ((4, half), F32), ((rows, 3 * width), BF16),
            ((rows, half), BF16), ((rows, half), BF16),
        ],
        [((rows, width), F32)],
        "finish", 6 * rows * width * width,
        meta, dqkv_here, x, grad_middle, *vec, hidden_a, *qkv,
    )
    late = pack(
        [(hida_keep, hida_out, gj)], (False,), 2, (keep_sums, send_sums), meta, index, group,
        count,
    )
    while not early.over():
        advance([early, late], count)
    (grad_shrink, grad_expand, grad_mix), sums = unpack(
        early, ((4 * each, width), (each, ff), (each, width)), early_kinds, 8, meta, index,
        group, count,
    )
    while not late.over():
        advance([late], count)
    (grad_qkv,), late_sums = unpack(
        late, ((each, 3 * width),), (False,), 4, meta, index, group, count
    )
    return (
        result[None], input_grad[None], late_sums[0], late_sums[1], grad_qkv, late_sums[2],
        late_sums[3], grad_mix, sums[0], sums[1], sums[2], grad_expand, jnp.concatenate(sums[4:8]),
        grad_shrink, sums[3],
    )


def solution(mesh):
    block = P("fsdp", "ctx", None)
    vector, matrix = P("fsdp"), P("fsdp", None)
    return jax.shard_map(
        body,
        mesh=mesh,
        in_specs=(
            block, block, matrix, vector, vector, matrix, vector, vector, matrix, vector, vector,
            vector, matrix, vector, matrix, vector,
        ),
        out_specs=(
            block, block, vector, vector, matrix, vector, vector, matrix, vector, vector, vector,
            matrix, vector, matrix, vector,
        ),
        check_vma=False,
    )
```

```python
import functools

import jax
import jax.numpy as jnp
from jax import lax
from jax.experimental import pallas as pl
from jax.experimental.pallas import tpu as pltpu
from jax.sharding import PartitionSpec as P

H = 12
HD = 64
NORM_EPS = 1e-05
MASK_FLOOR = -1e30
GELU_COEF = 0.7978845608028654
GELU_CUBE = 0.044715
SCALE = HD ** (-0.5)
F32 = jnp.float32
BF16 = jnp.bfloat16
LANES = 128
LINES = 16
MIB = 1024 * 1024


def dot_nn(left, right):
    return lax.dot_general(left, right, (((1,), (0,)), ((), ())), preferred_element_type=F32)


def dot_nt(left, right):
    return lax.dot_general(left, right, (((1,), (1,)), ((), ())), preferred_element_type=F32)


def dot_tn(left, right):
    return lax.dot_general(left, right, (((0,), (0,)), ((), ())), preferred_element_type=F32)


def normalise(inputs):
    centred = inputs - jnp.mean(inputs, axis=-1, keepdims=True)
    inv_std = lax.rsqrt(jnp.mean(centred * centred, axis=-1, keepdims=True) + NORM_EPS)
    return centred * inv_std, inv_std


def norm_back(scaled, unit, inv_std):
    return inv_std * (
        scaled
        - jnp.mean(scaled, axis=-1, keepdims=True)
        - unit * jnp.mean(scaled * unit, axis=-1, keepdims=True)
    )


def whole_vectors(side_ref, mine_ref, theirs_ref, rows):
    mine, theirs = mine_ref[rows].astype(F32), theirs_ref[rows].astype(F32)
    first = side_ref[0] == 0
    left, right = jnp.where(first, mine, theirs), jnp.where(first, theirs, mine)
    return jnp.concatenate([left, right], axis=1)


def halves(side_ref, size):
    side = side_ref[0]
    own = pl.ds(pl.multiple_of(side * size, 128), size)
    other = pl.ds(pl.multiple_of((1 - side) * size, 128), size)
    return own, other


def call(kernel, outs, scratch, name, flops, *args, smem=1, away=0, away_outs=0):
    vmem = pl.BlockSpec(memory_space=pltpu.VMEM)
    anywhere = pl.BlockSpec(memory_space=pl.ANY)
    specs = [pl.BlockSpec(memory_space=pltpu.SMEM)] * smem
    specs += [vmem] * (len(args) - smem - away) + [anywhere] * away
    moved = sum(a.size * a.dtype.itemsize for a in args)
    return pl.pallas_call(
        kernel,
        out_shape=[jax.ShapeDtypeStruct(s, d) for s, d in outs],
        in_specs=specs,
        out_specs=[anywhere] * away_outs + [vmem] * (len(outs) - away_outs),
        scratch_shapes=[pltpu.VMEM(*s) if isinstance(s, tuple) else s for s in scratch],
        compiler_params=pltpu.CompilerParams(vmem_limit_bytes=56 * MIB),
        cost_estimate=pl.CostEstimate(flops=flops, bytes_accessed=moved, transcendentals=0),
        name=name,
    )(*args)


def bits_of(count):
    return list(range(count.bit_length() - 1))


def sum_orders(count, parts):
    turn, last = bits_of(count)[:parts], bits_of(count)[parts:]
    return [list(reversed(turn[k:] + turn[:k] + last)) for k in range(parts)]


def place_of(r, order):
    place = 0
    for s, bit in enumerate(order):
        place = place | (((r >> bit) & 1) << s)
    return place


def relative_at(place, order):
    return sum(((place >> s) & 1) << bit for s, bit in enumerate(order))


def fetch(sources, targets, sem):
    copies = [
        pltpu.make_async_copy(src, dst, sem.at[i])
        for i, (src, dst) in enumerate(zip(sources, targets))
    ]
    for copy in copies:
        copy.start()
    return copies


def project_kernel(
    side_ref, x_ref, mine_ref, theirs_ref, own_ref, other_ref, hid_ref, send_ref
):
    rows, width = x_ref.shape
    own, other = halves(side_ref, width // 2)
    unit, _ = normalise(x_ref[...].astype(F32))
    vec = whole_vectors(side_ref, mine_ref, theirs_ref, slice(0, 8))
    hid_ref[...] = (unit * vec[0:1] + vec[1:2]).astype(BF16)
    joint = dot_nn(hid_ref[:, own], own_ref[...]) + dot_nn(hid_ref[:, other], other_ref[...])
    three = (
        (joint[:, :width] + vec[2:3]).astype(BF16),
        joint[:, width : 2 * width].astype(BF16),
        (joint[:, 2 * width :] + vec[3:4]).astype(BF16),
    )
    for k, part in enumerate(three):
        turned = part.T
        for h in range(H):
            send_ref[h, k * HD : (k + 1) * HD, :] = turned[h * HD : (h + 1) * HD]
    for h in range(H, send_ref.shape[0]):
        send_ref[h] = jnp.zeros(send_ref.shape[1:], BF16)


def attend_kernel(slot_ref, in_ref, out_ref, total_ref, q_t, k_n, v_t, o_t):
    count, _, rows = in_ref.shape
    tile = 512
    for p in range(count):
        slot = slot_ref[p]
        where = slice(p * rows, (p + 1) * rows)
        q_t[:, where] = in_ref[slot, 0:HD, :] * jnp.asarray(SCALE, BF16)
        k_n[where, :] = in_ref[slot, HD : 2 * HD, :].T
        v_t[:, where] = in_ref[slot, 2 * HD : 3 * HD, :]
    length = count * rows
    below = lax.broadcasted_iota(jnp.int32, (tile, tile), 0) <= lax.broadcasted_iota(
        jnp.int32, (tile, tile), 1
    )
    for i in range(length // tile):
        front, here = slice(0, i * tile), slice(i * tile, (i + 1) * tile)
        query = q_t[:, here]
        spans = [here] + [front] * (i > 0)
        scores = [dot_nn(k_n[span, :], query) for span in spans]
        scores[0] = jnp.where(below, scores[0], MASK_FLOOR)
        best = jnp.max(scores[0], axis=0, keepdims=True)
        for part in scores[1:]:
            best = jnp.maximum(best, jnp.max(part, axis=0, keepdims=True))
        weights = [jnp.exp(part - best) for part in scores]
        total = sum(jnp.sum(part, axis=0, keepdims=True) for part in weights)
        mixed = sum(dot_nn(v_t[:, s], w.astype(BF16)) for s, w in zip(spans, weights))
        o_t[:, here] = (mixed / total).astype(BF16)
        total_ref[:, here] = best + jnp.log(total)
    for p in range(count):
        out_ref[slot_ref[p]] = o_t[:, p * rows : (p + 1) * rows]


def attend_back_kernel(
    slot_ref, in_ref, att_ref, grad_ref, total_ref, out_ref,
    q_t, q_n, k_t, k_n, v_n, g_t, g_n, delta, dq_t, dk_t, dv_t,
):
    count, _, rows = in_ref.shape
    tile = 512
    for p in range(count):
        slot = slot_ref[p]
        where = slice(p * rows, (p + 1) * rows)
        query = in_ref[slot, 0:HD, :] * jnp.asarray(SCALE, BF16)
        q_t[:, where] = query
        q_n[where, :] = query.T
        key = in_ref[slot, HD : 2 * HD, :]
        k_t[:, where] = key
        k_n[where, :] = key.T
        v_n[where, :] = in_ref[slot, 2 * HD : 3 * HD, :].T
        grad = grad_ref[slot]
        g_t[:, where] = grad
        g_n[where, :] = grad.T
        delta[:, where] = jnp.sum(
            grad.astype(F32) * att_ref[slot].astype(F32), axis=0, keepdims=True
        )
    length = count * rows
    tiles = length // tile
    below = lax.broadcasted_iota(jnp.int32, (tile, tile), 0) <= lax.broadcasted_iota(
        jnp.int32, (tile, tile), 1
    )
    dq_t[...] = jnp.zeros_like(dq_t)
    for j in range(tiles):
        here = slice(j * tile, (j + 1) * tile)

        def step(i, state, masked=False, here=here):
            key_sum, value_sum = state
            span = slice(i * tile, (i + 1) * tile)
            scores = dot_nn(k_n[here, :], q_t[:, span])
            probs = jnp.exp(scores - total_ref[:, span])
            if masked:
                probs = jnp.where(below, probs, 0.0)
            prob_grad = dot_nn(v_n[here, :], g_t[:, span])
            score_grad = (probs * (prob_grad - delta[:, span])).astype(BF16)
            value_sum = value_sum + dot_nn(probs.astype(BF16), g_n[span, :])
            key_sum = key_sum + dot_nn(score_grad, q_n[span, :])
            dq_t[:, span] = dq_t[:, span] + dot_nn(k_t[:, here], score_grad)
            return key_sum, value_sum

        zero = jnp.zeros((tile, HD), F32)
        state = step(j, (zero, zero), masked=True)
        for i in range(j + 1, tiles):
            state = step(i, state)
        dk_t[:, here] = state[0].T
        dv_t[:, here] = state[1].T
    for p in range(count):
        slot = slot_ref[p]
        where = slice(p * rows, (p + 1) * rows)
        out_ref[slot, 0:HD, :] = (dq_t[:, where] * SCALE).astype(BF16)
        out_ref[slot, HD : 2 * HD, :] = dk_t[:, where].astype(BF16)
        out_ref[slot, 2 * HD : 3 * HD, :] = dv_t[:, where].astype(BF16)


def split_sums(first, sums, keep_ref, send_ref):
    for r, line in enumerate(sums):
        half = line.shape[1] // 2
        low, high = line[:, :half], line[:, half:]
        keep_ref[r : r + 1] = jnp.where(first, low, high)
        send_ref[r : r + 1] = jnp.where(first, high, low)


def middle_kernel(
    side_ref, att_in, x_ref, cot_ref, mine_ref, theirs_ref, *refs,
):
    sources, refs = refs[:6], refs[6:]
    (
        res_ref, gm_ref, gsend_ref, sums_keep, sums_send,
        cotb_ref, act_keep, act_send, hid_keep, hid_send, ge_ref, att_keep, att_send, gmb_ref,
        wide, act_s, hid_s, att_s, narrow, *weights, sem,
    ) = refs
    mix_own, mix_other, ex_own, ex_other, sh_own, sh_other = weights
    copies = fetch(sources, weights, sem)
    rows, width = x_ref.shape
    ff = wide.shape[1]
    part = ff // 8
    own, other = halves(side_ref, width // 2)
    fown, fother = halves(side_ref, ff // 2)
    vec = whole_vectors(side_ref, mine_ref, theirs_ref, slice(0, 8))
    first = side_ref[0] == 0
    lines = [
        [ref[8 + r : 9 + r].astype(F32) for r in range(4)] for ref in (mine_ref, theirs_ref)
    ]
    ebias = jnp.concatenate(
        [jnp.where(first, a, b) for a, b in zip(*lines)]
        + [jnp.where(first, b, a) for a, b in zip(*lines)],
        axis=1,
    )
    att_s[...] = att_in[0:H].reshape(width, rows).T
    att_keep[...] = att_s[:, own]
    att_send[...] = att_s[:, other]
    copies[0].wait()
    copies[1].wait()
    middle = (
        x_ref[...].astype(F32)
        + (dot_nn(att_keep[...], mix_own[...]) + dot_nn(att_send[...], mix_other[...]))
        + vec[4:5]
    )
    unit, inv_std = normalise(middle)
    hid_s[...] = (unit * vec[5:6] + vec[6:7]).astype(BF16)
    hid_keep[...] = hid_s[:, own]
    hid_send[...] = hid_s[:, other]
    copies[2].wait()
    copies[3].wait()
    expanded = (
        dot_nn(hid_keep[...], ex_own[...])
        + dot_nn(hid_send[...], ex_other[...])
        + ebias
    )
    square = expanded * expanded
    bend = jnp.tanh(GELU_COEF * (expanded + GELU_CUBE * square * expanded))
    act_s[...] = (0.5 * expanded * (1.0 + bend)).astype(BF16)
    slope = 0.5 * (1.0 + bend) + 0.5 * expanded * (1.0 - bend * bend) * GELU_COEF * (
        1.0 + 3.0 * GELU_CUBE * square
    )
    act_keep[...] = act_s[:, fown]
    act_send[...] = act_s[:, fother]
    copies[4].wait()
    copies[5].wait()
    result = (
        middle
        + (dot_nn(act_keep[...], sh_own[...]) + dot_nn(act_send[...], sh_other[...]))
        + vec[7:8]
    )
    res_ref[...] = result.astype(BF16)
    upstream = cot_ref[...]
    cotb_ref[...] = upstream.astype(BF16)
    wide[:, fown] = dot_nt(cotb_ref[...], sh_own[...])
    wide[:, fother] = dot_nt(cotb_ref[...], sh_other[...])
    grad_expanded = wide[...] * slope
    esum = jnp.sum(grad_expanded, axis=0, keepdims=True)
    for r in range(4):
        low = esum[:, r * part : (r + 1) * part]
        high = esum[:, (4 + r) * part : (5 + r) * part]
        sums_keep[4 + r : 5 + r] = jnp.where(first, low, high)
        sums_send[4 + r : 5 + r] = jnp.where(first, high, low)
    ge_ref[...] = grad_expanded.astype(BF16)
    narrow[:, own] = dot_nt(ge_ref[...], ex_own[...])
    narrow[:, other] = dot_nt(ge_ref[...], ex_other[...])
    grad_hidden = narrow[...]
    sums = [jnp.sum(s, axis=0, keepdims=True) for s in (grad_hidden * unit, grad_hidden)]
    grad_middle = upstream + norm_back(grad_hidden * vec[5:6], unit, inv_std)
    gm_ref[...] = grad_middle
    gmb_ref[...] = grad_middle.astype(BF16)
    sums = [jnp.sum(grad_middle, axis=0, keepdims=True)] + sums
    sums += [jnp.sum(upstream, axis=0, keepdims=True)]
    split_sums(first, sums, sums_keep, sums_send)
    narrow[:, own] = dot_nt(gmb_ref[...], mix_own[...])
    narrow[:, other] = dot_nt(gmb_ref[...], mix_other[...])
    gsend_ref[0:H] = narrow[...].astype(BF16).T.reshape(H, HD, rows)
    for h in range(H, gsend_ref.shape[0]):
        gsend_ref[h] = jnp.zeros(gsend_ref.shape[1:], BF16)


def finish_kernel(
    side_ref, in_ref, x_ref, gm_ref, mine_ref, theirs_ref, hid_ref, own_ref, other_ref,
    grad_ref, sums_keep, sums_send, gj_ref, hid_keep, hid_send, narrow,
):
    rows, width = x_ref.shape
    own, other = halves(side_ref, width // 2)
    gain = whole_vectors(side_ref, mine_ref, theirs_ref, slice(0, 1))
    for k in range(3):
        gj_ref[:, k * width : (k + 1) * width] = (
            in_ref[0:H, k * HD : (k + 1) * HD, :].reshape(width, rows).T
        )
    hid_keep[...] = hid_ref[:, own]
    hid_send[...] = hid_ref[:, other]
    unit, inv_std = normalise(x_ref[...].astype(F32))
    narrow[:, own] = dot_nt(gj_ref[...], own_ref[...])
    narrow[:, other] = dot_nt(gj_ref[...], other_ref[...])
    grad_hidden = narrow[...]
    joint = gj_ref[...].astype(F32)
    sums = (grad_hidden * unit, grad_hidden, joint[:, :width], joint[:, 2 * width :])
    sums = [jnp.sum(s, axis=0, keepdims=True) for s in sums]
    split_sums(side_ref[0] == 0, sums, sums_keep, sums_send)
    grad_ref[...] = gm_ref[...] + norm_back(grad_hidden * gain, unit, inv_std)


def block_spans(a, rows, wide, paired, count):
    if paired:
        tall, wide = 2 * rows // count, wide // 2
        first, start = a // 2 * tall, a % 2 * wide
    else:
        tall = rows // count
        first, start = a * tall, 0
    return first, tall, [start + j * LANES for j in range(wide // LANES)]


def pack_kernel(paired, parts, meta_ref, *refs):
    weights = len(paired)
    ins, (keep_sums, came_sums) = refs[: 4 * weights], refs[4 * weights : 4 * weights + 2]
    outs, refs = refs[4 * weights + 2 :][: 2 * parts], refs[4 * weights + 2 + 2 * parts :]
    lefts, rights, (pk, extra) = refs[:-2:2], refs[1:-2:2], refs[-2:]
    count = pk.shape[0]
    for i, (left, right) in enumerate(zip(lefts, rights)):
        rows = left.shape[0] // 2
        for n, dst in enumerate((left, left, right, right)):
            dst[(n % 2) * rows : (n % 2 + 1) * rows] = ins[4 * i + n][...]
    extra[...] = jnp.zeros_like(extra)
    sums = keep_sums[...] + came_sums[...]
    each = sums.shape[1] // LANES
    for q in range(sums.shape[0] * each):
        extra[q // LINES, q % LINES : q % LINES + 1] = sums[
            q // each : q // each + 1, q % each * LANES : (q % each + 1) * LANES
        ]
    for k, order in enumerate(sum_orders(count, parts)):
        keep_ref, send_ref = outs[2 * k : 2 * k + 2]
        line = 0
        for left, right, pair in zip(lefts, rights, paired):
            wide = right.shape[1] // parts
            grad = dot_tn(left[...], right[:, k * wide : (k + 1) * wide]).astype(pk.dtype)
            for a in range(count):
                first, tall, starts = block_spans(a, grad.shape[0], wide, pair, count)
                for j, start in enumerate(starts):
                    pk[a, line + j * tall : line + (j + 1) * tall] = grad[
                        first : first + tall, start : start + LANES
                    ]
            line += tall * len(starts)
        for m in range(count):
            dst = keep_ref if m < count // 2 else send_ref
            a = relative_at(m, order) ^ meta_ref[1]
            dst[m % (count // 2), 0:line] = pk[a].astype(BF16)
            if k == 0:
                dst[m % (count // 2), line:] = extra[a].astype(BF16)


def unpack_kernel(paired, parts, meta_ref, *refs):
    weights = len(paired)
    near_far, refs = refs[: 2 * parts], refs[2 * parts :]
    outs, refs, (extra, sem) = refs[:weights], refs[weights:-2], refs[-2:]
    lines, scratch = refs[:-weights], refs[-weights:]
    half = near_far[0].shape[0]
    count = 2 * half
    copies = []
    for k, order in enumerate(sum_orders(count, parts)):
        for m in range(count):
            a = relative_at(m, order) ^ meta_ref[1]
            block = near_far[2 * k + m // half][m % half].astype(F32)
            line = 0
            for dst, pair in zip(scratch, paired):
                rows, wide = dst.shape[1:]
                first, tall, starts = block_spans(a, rows, wide, pair, count)
                for start in starts:
                    if pair:
                        start = pl.ds(pl.multiple_of(start, LANES), LANES)
                    else:
                        start = slice(start, start + LANES)
                    place = pl.ds(pl.multiple_of(first, 8), tall)
                    dst[k, place, start] = block[line : line + tall]
                    line += tall
            if k == 0:
                extra[a] = block[line:]
        for i, (src, dst) in enumerate(zip(scratch, outs)):
            size = src.shape[2]
            copy = pltpu.make_async_copy(
                src.at[k], dst.at[:, k * size : (k + 1) * size], sem.at[k, i]
            )
            copy.start()
            copies.append(copy)
    each = lines[0].shape[0] // LANES
    for q in range(len(lines) * each):
        lines[q // each][q % each * LANES : (q % each + 1) * LANES] = extra[
            q // LINES, q % LINES, :
        ]
    for copy in copies:
        copy.wait()


def stack_kernel(*refs):
    out_ref = refs[-1]
    row = 0
    for ref in refs[:-1]:
        line = ref[...].reshape(1, -1)
        for start in range(0, line.shape[1], out_ref.shape[1]):
            out_ref[row : row + 1] = line[:, start : start + out_ref.shape[1]]
            row += 1


SWAP = [(0, 1), (1, 0)]


def pieces(weight, group):
    if group == 2:
        return weight, lax.ppermute(weight, "fsdp", SWAP)
    full = lax.all_gather(weight, "fsdp", axis=0, tiled=True)
    half = full.shape[0] // 2
    return full[:half], full[half:]


def join_vector(vector, group, side):
    if group == 2:
        other = lax.ppermute(vector, "fsdp", SWAP)
        return jnp.where(
            side == 0,
            jnp.concatenate([vector, other], axis=1),
            jnp.concatenate([other, vector], axis=1),
        )
    return lax.all_gather(vector, "fsdp", axis=1, tiled=True)


def swap_side(part):
    return lax.ppermute(part, "fsdp", SWAP)


def rows_over_group(keep, send, right):
    left = jnp.concatenate([keep, send], axis=1)
    left = lax.all_to_all(left, "fsdp", split_axis=1, concat_axis=0, tiled=True)
    return dot_tn(left, lax.all_gather(right, "fsdp", axis=0, tiled=True))


def sums_over_group(keep, send, group):
    sums = jnp.concatenate([keep[:4], send[:4]], axis=1)
    width = sums.shape[1]
    if keep.shape[0] > 4:
        wide = jnp.concatenate([keep[4:].reshape(-1), send[4:].reshape(-1)])
        wide = wide.reshape(group, 4, width // group).swapaxes(0, 1).reshape(4, width)
        sums = jnp.concatenate([sums, wide], axis=0)
    return lax.psum_scatter(sums, "fsdp", scatter_dimension=1, tiled=True)


def swap_bit(part, bit, count):
    return lax.ppermute(part, "ctx", [(d, d ^ (1 << bit)) for d in range(count)])


def add_parts(left, right):
    return (left.astype(F32) + right.astype(F32)).astype(BF16)


class Flow:
    def __init__(self, keeps, sends, count):
        self.keeps, self.sends = list(keeps), list(sends)
        self.orders = sum_orders(count, len(self.keeps))
        self.bits = len(self.orders[0])
        self.step = 0

    def bit_row(self):
        at = self.bits - 1 - self.step if self.step < self.bits else self.step - self.bits
        return [order[at] for order in self.orders]

    def pending(self):
        parts = self.sends if self.step < self.bits else self.keeps
        row = self.bit_row()
        if len(set(row)) == 1:
            return [(jnp.concatenate(parts, axis=1), row[0])]
        return list(zip(parts, row))

    def accept(self, cames):
        if len(cames) == 1:
            sizes = [part.shape[1] for part in self.keeps]
            ends = [sum(sizes[: k + 1]) for k in range(len(sizes))]
            cames = [cames[0][:, end - size : end] for end, size in zip(ends, sizes)]
        half = cames[0].shape[0] // 2
        if self.step < self.bits - 1:
            self.sends = [add_parts(p[half:], c[half:]) for p, c in zip(self.keeps, cames)]
            self.keeps = [add_parts(p[:half], c[:half]) for p, c in zip(self.keeps, cames)]
        elif self.step == self.bits - 1:
            self.keeps = [add_parts(p, c) for p, c in zip(self.keeps, cames)]
        elif self.step == 2 * self.bits - 1:
            self.fars = cames
        else:
            self.keeps = [jnp.concatenate(pair, axis=0) for pair in zip(self.keeps, cames)]
        self.step += 1

    def over(self):
        return self.step == 2 * self.bits


def send_all(flow, count):
    return [swap_bit(part, bit, count) for part, bit in flow.pending()]


def advance(flow, count, inner=None, steps=0):
    cames = send_all(flow, count)
    for _ in range(steps - 1):
        inner.accept(lax.optimization_barrier(send_all(inner, count)))
    both = lax.optimization_barrier((cames, send_all(inner, count) if steps else []))
    flow.accept(both[0])
    if steps:
        inner.accept(both[1])


def plain_pack(weights, extra, index, count, parts):
    keeps, sends = [], []
    for k, order in enumerate(sum_orders(count, parts)):
        blocks = []
        for weight in weights:
            span = weight.shape[1] // parts
            for start in range(k * span, (k + 1) * span, LANES):
                blocks.append(weight[:, start : start + LANES].astype(BF16))
        flat = jnp.concatenate(blocks, axis=0)
        flat = flat.reshape(count, -1, LANES)
        if k == 0:
            flat = jnp.concatenate([flat, extra], axis=1)
        turn = jnp.array([relative_at(m, order) for m in range(count)], jnp.int32) ^ index
        flat = jnp.take(flat, turn, axis=0)
        keeps.append(flat[: count // 2])
        sends.append(flat[count // 2 :])
    return keeps, sends


def plain_unpack(keeps, fars, shapes, index, count, parts):
    columns = [[] for _ in shapes]
    extra = None
    for k, order in enumerate(sum_orders(count, parts)):
        flat = jnp.concatenate([keeps[k], fars[k]], axis=0)
        turn = place_of(jnp.arange(count, dtype=jnp.int32) ^ index, order)
        flat = jnp.take(flat, turn, axis=0).astype(F32)
        if k == 0:
            extra = flat[:, flat.shape[1] - LINES :]
            flat = flat[:, : flat.shape[1] - LINES]
        flat = flat.reshape(-1, LANES)
        first = 0
        for i, (rows, cols) in enumerate(shapes):
            for _ in range(cols // parts // LANES):
                columns[i].append(flat[first : first + rows])
                first += rows
    return [jnp.concatenate(c, axis=1) for c in columns], extra


def exchange(pairs, sums, group, count):
    if group != 2 or count != 16:
        return []
    args = []
    for keep, send, right in pairs:
        args += [keep, swap_side(send), right, swap_side(right)]
    return args + [sums[0], swap_side(sums[1])]


def pack(pairs, sums, args, paired, parts, meta, index, group, count):
    keep_sums, send_sums = sums
    if args:
        size = sum(keep.shape[1] * right.shape[1] for keep, _, right in pairs)
        block = size // parts // LANES // count
        half = count // 2
        rows = pairs[0][0].shape[0]
        kind = BF16 if block % 16 == 0 else F32
        outs = [
            ((half, block + (LINES if k // 2 == 0 else 0), LANES), BF16) for k in range(2 * parts)
        ]
        flows = call(
            functools.partial(pack_kernel, paired, parts), outs,
            [((2 * rows, a.shape[1]), BF16) for a in args[:-2:2]]
            + [((count, block, LANES), kind), ((count, LINES, LANES), F32)],
            "pack", 4 * rows * size, meta, *args,
        )
        return Flow(flows[::2], flows[1::2], count)
    extra = sums_over_group(keep_sums, send_sums, group).reshape(-1, LANES)
    extra = jnp.pad(extra, ((0, LINES * count - extra.shape[0]), (0, 0))).astype(BF16)
    extra = extra.reshape(count, LINES, LANES)
    weights = [rows_over_group(*pair) for pair in pairs]
    return Flow(*plain_pack(weights, extra, index, count, parts), count)


def unpack(flow, shapes, paired, vectors, meta, index, group, count):
    parts = len(flow.keeps)
    each = shapes[-1][0]
    if group == 2 and count == 16:
        near_far = [part for pair in zip(flow.keeps, flow.fars) for part in pair]
        outs = call(
            functools.partial(unpack_kernel, paired, parts),
            [(s, F32) for s in shapes] + [((each,), F32)] * vectors,
            [((parts, r, c // parts), F32) for r, c in shapes]
            + [((count, LINES, LANES), F32), pltpu.SemaphoreType.DMA((parts, len(shapes)))],
            "unpack", 0, meta, *near_far, away_outs=len(shapes),
        )
        return outs[: len(shapes)], outs[len(shapes) :]
    weights, extra = plain_unpack(flow.keeps, flow.fars, shapes, index, count, parts)
    return weights, list(extra.reshape(-1)[: vectors * each].reshape(vectors, each))


def body(
    block_input, out_cotangent, block_position, first_gain, first_shift, qkv_weight, query_bias,
    value_bias, output_weight, output_bias, second_gain, second_shift, expand_weight, expand_bias,
    shrink_weight, shrink_bias,
):
    count = lax.axis_size("ctx")
    group = lax.axis_size("fsdp")
    rows, width = block_input.shape[1:]
    ff = expand_weight.shape[1]
    length = count * rows
    side = lax.axis_index("fsdp") if group == 2 else jnp.int32(0)
    index = lax.axis_index("ctx")
    half = width // 2
    three = 3 * HD
    each = width // group
    meta = jnp.stack([side, index]).astype(jnp.int32)
    table = block_position[0]
    places = jnp.arange(count, dtype=jnp.int32)
    slots = jnp.sum(
        jnp.where(table[None, :] == places[:, None], places[None, :], 0), axis=1
    ).astype(jnp.int32)
    x = block_input[0]
    vectors = (
        first_gain, first_shift, query_bias, value_bias, output_bias, second_gain, second_shift,
        shrink_bias,
    )
    if group == 2:
        (mine,) = call(
            stack_kernel, [((12, each), BF16)], [], "stack", 0, *vectors, expand_bias, smem=0
        )
        mine, qkv_weight = lax.optimization_barrier((mine, qkv_weight))
        vec = mine, swap_side(mine)
    else:
        lines = lax.all_gather(jnp.stack(vectors), "fsdp", axis=1, tiled=True)
        wide = lax.all_gather(expand_bias, "fsdp", axis=0, tiled=True).reshape(2, 4, half)
        vec = [
            jnp.concatenate([lines[:, i * half : (i + 1) * half], wide[i]], axis=0)
            for i in range(2)
        ]
    qkv = pieces(qkv_weight, group)
    vec, qkv, output_weight, expand_weight, shrink_weight = lax.optimization_barrier(
        (vec, qkv, output_weight, expand_weight, shrink_weight)
    )
    mix = pieces(output_weight, group)
    expand = pieces(expand_weight, group)
    shrink = pieces(shrink_weight, group)
    size = width * ff

    hidden_a, qkv_send = call(
        project_kernel,
        [((rows, width), BF16), ((count, three, rows), BF16)],
        [], "project", 6 * rows * width * width,
        meta, x, *vec, *qkv,
    )
    qkv_here = lax.all_to_all(qkv_send, "ctx", 0, 0, tiled=True)
    att_send, log_total = call(
        attend_kernel,
        [((count, HD, rows), BF16), ((1, length), F32)],
        [((HD, length), BF16), ((length, HD), BF16), ((HD, length), BF16), ((HD, length), BF16)],
        "attend", 2 * length * length * HD,
        slots, qkv_here,
    )
    att_here = lax.all_to_all(att_send, "ctx", 0, 0, tiled=True)
    (
        result, grad_middle, grad_send, keep_sums, send_sums, cot_b, act_keep, act_out, hid_keep,
        hid_out, ge_b, att_keep, att_out, gm_b,
    ) = call(
        middle_kernel,
        [
            ((rows, width), BF16), ((rows, width), F32), ((count, HD, rows), BF16),
            ((8, half), F32), ((8, half), F32), ((rows, width), BF16), ((rows, ff // 2), BF16),
            ((rows, ff // 2), BF16), ((rows, half), BF16), ((rows, half), BF16),
            ((rows, ff), BF16), ((rows, half), BF16), ((rows, half), BF16), ((rows, width), BF16),
        ],
        [
            ((rows, ff), F32), ((rows, ff), BF16), ((rows, width), BF16), ((rows, width), BF16),
            ((rows, width), F32),
        ]
        + [(w.shape, BF16) for w in (*mix, *expand, *shrink)]
        + [pltpu.SemaphoreType.DMA((6,))],
        "middle", 8 * rows * size + 4 * rows * width * width,
        meta, att_here, x, out_cotangent[0], *vec, *mix, *expand, *shrink, away=6,
    )
    grad_here = lax.all_to_all(grad_send, "ctx", 0, 0, tiled=True)

    early_kinds = (False, True, True)
    pairs = [(act_keep, act_out, cot_b), (hid_keep, hid_out, ge_b), (att_keep, att_out, gm_b)]
    sums = keep_sums, send_sums
    args = exchange(pairs, sums, group, count)
    early = pack(pairs, sums, args, early_kinds, 3, meta, index, group, count)
    early.keeps, early.sends, grad_here = lax.optimization_barrier(
        (early.keeps, early.sends, grad_here)
    )
    advance(early, count)
    (dqkv_send,) = call(
        attend_back_kernel,
        [((count, three, rows), BF16)],
        [
            ((HD, length), BF16), ((length, HD), BF16), ((HD, length), BF16),
            ((length, HD), BF16), ((length, HD), BF16), ((HD, length), BF16),
            ((length, HD), BF16), ((1, length), F32), ((HD, length), F32), ((HD, length), F32),
            ((HD, length), F32),
        ],
        "attend_back", 5 * length * length * HD,
        slots, qkv_here, att_send, grad_here, log_total,
    )
    dqkv_here = lax.all_to_all(dqkv_send, "ctx", 0, 0, tiled=True)
    early.keeps, early.sends, _ = lax.optimization_barrier(
        (early.keeps, early.sends, dqkv_send)
    )
    advance(early, count)
    input_grad, keep_sums, send_sums, gj, hida_keep, hida_out = call(
        finish_kernel,
        [
            ((rows, width), F32), ((4, half), F32), ((4, half), F32), ((rows, 3 * width), BF16),
            ((rows, half), BF16), ((rows, half), BF16),
        ],
        [((rows, width), F32)],
        "finish", 6 * rows * width * width,
        meta, dqkv_here, x, grad_middle, *vec, hidden_a, *qkv,
    )
    pairs = [(hida_keep, hida_out, gj)]
    sums = keep_sums, send_sums
    args = exchange(pairs, sums, group, count)
    early.keeps, early.sends, args = lax.optimization_barrier((early.keeps, early.sends, args))
    advance(early, count)
    late = pack(pairs, sums, args, (False,), 2, meta, index, group, count)
    while not early.over():
        advance(early, count, late, 1 + (2 * early.bits - 1 > early.step >= 2 * early.bits - 3))
    (grad_shrink, grad_expand, grad_mix), sums = unpack(
        early, ((4 * each, width), (each, ff), (each, width)), early_kinds, 8, meta, index,
        group, count,
    )
    while not late.over():
        advance(late, count)
    (grad_qkv,), late_sums = unpack(
        late, ((each, 3 * width),), (False,), 4, meta, index, group, count
    )
    return (
        result[None], input_grad[None], late_sums[0], late_sums[1], grad_qkv, late_sums[2],
        late_sums[3], grad_mix, sums[0], sums[1], sums[2], grad_expand, jnp.concatenate(sums[4:8]),
        grad_shrink, sums[3],
    )


def solution(mesh):
    block = P("fsdp", "ctx", None)
    vector, matrix = P("fsdp"), P("fsdp", None)
    return jax.shard_map(
        body,
        mesh=mesh,
        in_specs=(
            block, block, matrix, vector, vector, matrix, vector, vector, matrix, vector, vector,
            vector, matrix, vector, matrix, vector,
        ),
        out_specs=(
            block, block, vector, vector, matrix, vector, vector, matrix, vector, vector, vector,
            matrix, vector, matrix, vector,
        ),
        check_vma=False,
    )
```

```python
import functools

import jax
import jax.numpy as jnp
from jax import lax
from jax.experimental import pallas as pl
from jax.experimental.pallas import tpu as pltpu
from jax.sharding import PartitionSpec as P

H = 12
HD = 64
NORM_EPS = 1e-05
MASK_FLOOR = -1e30
GELU_COEF = 0.7978845608028654
GELU_CUBE = 0.044715
SCALE = HD ** (-0.5)
F32 = jnp.float32
BF16 = jnp.bfloat16
LANES = 128
LINES = 16
MIB = 1024 * 1024


def dot_nn(left, right):
    return lax.dot_general(left, right, (((1,), (0,)), ((), ())), preferred_element_type=F32)


def dot_nt(left, right):
    return lax.dot_general(left, right, (((1,), (1,)), ((), ())), preferred_element_type=F32)


def dot_tn(left, right):
    return lax.dot_general(left, right, (((0,), (0,)), ((), ())), preferred_element_type=F32)


def normalise(inputs):
    centred = inputs - jnp.mean(inputs, axis=-1, keepdims=True)
    inv_std = lax.rsqrt(jnp.mean(centred * centred, axis=-1, keepdims=True) + NORM_EPS)
    return centred * inv_std, inv_std


def norm_back(scaled, unit, inv_std):
    return inv_std * (
        scaled
        - jnp.mean(scaled, axis=-1, keepdims=True)
        - unit * jnp.mean(scaled * unit, axis=-1, keepdims=True)
    )


def whole_vectors(side_ref, mine_ref, theirs_ref, rows):
    mine, theirs = mine_ref[rows].astype(F32), theirs_ref[rows].astype(F32)
    first = side_ref[0] == 0
    left, right = jnp.where(first, mine, theirs), jnp.where(first, theirs, mine)
    return jnp.concatenate([left, right], axis=1)


def halves(side_ref, size):
    side = side_ref[0]
    own = pl.ds(pl.multiple_of(side * size, 128), size)
    other = pl.ds(pl.multiple_of((1 - side) * size, 128), size)
    return own, other


def call(kernel, outs, scratch, name, flops, *args, smem=1, away=0, away_outs=0, limit=56):
    vmem = pl.BlockSpec(memory_space=pltpu.VMEM)
    anywhere = pl.BlockSpec(memory_space=pl.ANY)
    specs = [pl.BlockSpec(memory_space=pltpu.SMEM)] * smem
    specs += [vmem] * (len(args) - smem - away) + [anywhere] * away
    moved = sum(a.size * a.dtype.itemsize for a in args)
    return pl.pallas_call(
        kernel,
        out_shape=[jax.ShapeDtypeStruct(s, d) for s, d in outs],
        in_specs=specs,
        out_specs=[anywhere] * away_outs + [vmem] * (len(outs) - away_outs),
        scratch_shapes=[pltpu.VMEM(*s) if isinstance(s, tuple) else s for s in scratch],
        compiler_params=pltpu.CompilerParams(vmem_limit_bytes=limit * MIB),
        cost_estimate=pl.CostEstimate(flops=flops, bytes_accessed=moved, transcendentals=0),
        name=name,
    )(*args)


def bits_of(count):
    return list(range(count.bit_length() - 1))


def sum_orders(count, parts):
    turn, last = bits_of(count)[:parts], bits_of(count)[parts:]
    return [list(reversed(turn[k:] + turn[:k] + last)) for k in range(parts)]


def place_of(r, order):
    place = 0
    for s, bit in enumerate(order):
        place = place | (((r >> bit) & 1) << s)
    return place


def relative_at(place, order):
    return sum(((place >> s) & 1) << bit for s, bit in enumerate(order))


def fetch(sources, targets, sem):
    copies = [
        pltpu.make_async_copy(src, dst, sem.at[i])
        for i, (src, dst) in enumerate(zip(sources, targets))
    ]
    for copy in copies:
        copy.start()
    return copies


def project_kernel(
    side_ref, x_ref, mine_ref, theirs_ref, own_ref, other_ref, hid_ref, send_ref
):
    rows, width = x_ref.shape
    own, other = halves(side_ref, width // 2)
    unit, _ = normalise(x_ref[...].astype(F32))
    vec = whole_vectors(side_ref, mine_ref, theirs_ref, slice(0, 8))
    hid_ref[...] = (unit * vec[0:1] + vec[1:2]).astype(BF16)
    joint = dot_nn(hid_ref[:, own], own_ref[...]) + dot_nn(hid_ref[:, other], other_ref[...])
    three = (
        (joint[:, :width] + vec[2:3]).astype(BF16),
        joint[:, width : 2 * width].astype(BF16),
        (joint[:, 2 * width :] + vec[3:4]).astype(BF16),
    )
    for k, part in enumerate(three):
        turned = part.T
        for h in range(H):
            send_ref[h, k * HD : (k + 1) * HD, :] = turned[h * HD : (h + 1) * HD]
    for h in range(H, send_ref.shape[0]):
        send_ref[h] = jnp.zeros(send_ref.shape[1:], BF16)


def attend_kernel(slot_ref, in_ref, out_ref, total_ref, q_t, k_n, v_t, o_t):
    count, _, rows = in_ref.shape
    tile = 512
    for p in range(count):
        slot = slot_ref[p]
        where = slice(p * rows, (p + 1) * rows)
        q_t[:, where] = in_ref[slot, 0:HD, :] * jnp.asarray(SCALE, BF16)
        k_n[where, :] = in_ref[slot, HD : 2 * HD, :].T
        v_t[:, where] = in_ref[slot, 2 * HD : 3 * HD, :]
    length = count * rows
    below = lax.broadcasted_iota(jnp.int32, (tile, tile), 0) <= lax.broadcasted_iota(
        jnp.int32, (tile, tile), 1
    )
    for i in range(length // tile):
        front, here = slice(0, i * tile), slice(i * tile, (i + 1) * tile)
        query = q_t[:, here]
        spans = [here] + [front] * (i > 0)
        scores = [dot_nn(k_n[span, :], query) for span in spans]
        scores[0] = jnp.where(below, scores[0], MASK_FLOOR)
        best = jnp.max(scores[0], axis=0, keepdims=True)
        for part in scores[1:]:
            best = jnp.maximum(best, jnp.max(part, axis=0, keepdims=True))
        weights = [jnp.exp(part - best) for part in scores]
        total = sum(jnp.sum(part, axis=0, keepdims=True) for part in weights)
        mixed = sum(dot_nn(v_t[:, s], w.astype(BF16)) for s, w in zip(spans, weights))
        o_t[:, here] = (mixed / total).astype(BF16)
        total_ref[:, here] = best + jnp.log(total)
    for p in range(count):
        out_ref[slot_ref[p]] = o_t[:, p * rows : (p + 1) * rows]


def attend_back_kernel(
    slot_ref, in_ref, att_ref, grad_ref, total_ref, out_ref,
    q_t, q_n, k_t, k_n, v_n, g_t, g_n, delta, dq_t, dk_t, dv_t,
):
    count, _, rows = in_ref.shape
    tile = 512
    for p in range(count):
        slot = slot_ref[p]
        where = slice(p * rows, (p + 1) * rows)
        query = in_ref[slot, 0:HD, :] * jnp.asarray(SCALE, BF16)
        q_t[:, where] = query
        q_n[where, :] = query.T
        key = in_ref[slot, HD : 2 * HD, :]
        k_t[:, where] = key
        k_n[where, :] = key.T
        v_n[where, :] = in_ref[slot, 2 * HD : 3 * HD, :].T
        grad = grad_ref[slot]
        g_t[:, where] = grad
        g_n[where, :] = grad.T
        delta[:, where] = jnp.sum(
            grad.astype(F32) * att_ref[slot].astype(F32), axis=0, keepdims=True
        )
    length = count * rows
    tiles = length // tile
    below = lax.broadcasted_iota(jnp.int32, (tile, tile), 0) <= lax.broadcasted_iota(
        jnp.int32, (tile, tile), 1
    )
    dq_t[...] = jnp.zeros_like(dq_t)
    for j in range(tiles):
        here = slice(j * tile, (j + 1) * tile)

        def step(i, state, masked=False, here=here):
            key_sum, value_sum = state
            span = slice(i * tile, (i + 1) * tile)
            scores = dot_nn(k_n[here, :], q_t[:, span])
            probs = jnp.exp(scores - total_ref[:, span])
            if masked:
                probs = jnp.where(below, probs, 0.0)
            prob_grad = dot_nn(v_n[here, :], g_t[:, span])
            score_grad = (probs * (prob_grad - delta[:, span])).astype(BF16)
            value_sum = value_sum + dot_nn(probs.astype(BF16), g_n[span, :])
            key_sum = key_sum + dot_nn(score_grad, q_n[span, :])
            dq_t[:, span] = dq_t[:, span] + dot_nn(k_t[:, here], score_grad)
            return key_sum, value_sum

        zero = jnp.zeros((tile, HD), F32)
        state = step(j, (zero, zero), masked=True)
        for i in range(j + 1, tiles):
            state = step(i, state)
        dk_t[:, here] = state[0].T
        dv_t[:, here] = state[1].T
    for p in range(count):
        slot = slot_ref[p]
        where = slice(p * rows, (p + 1) * rows)
        out_ref[slot, 0:HD, :] = (dq_t[:, where] * SCALE).astype(BF16)
        out_ref[slot, HD : 2 * HD, :] = dk_t[:, where].astype(BF16)
        out_ref[slot, 2 * HD : 3 * HD, :] = dv_t[:, where].astype(BF16)


def split_sums(first, sums, keep_ref, send_ref):
    for r, line in enumerate(sums):
        half = line.shape[1] // 2
        low, high = line[:, :half], line[:, half:]
        keep_ref[r : r + 1] = jnp.where(first, low, high)
        send_ref[r : r + 1] = jnp.where(first, high, low)


def middle_kernel(
    side_ref, att_in, x_ref, cot_ref, mine_ref, theirs_ref, *refs,
):
    sources, refs = refs[:6], refs[6:]
    (
        res_ref, gm_ref, gsend_ref, sums_keep, sums_send,
        cotb_ref, act_keep, act_send, hid_keep, hid_send, ge_ref, att_keep, att_send, gmb_ref,
        wide, act_s, hid_s, att_s, narrow, *weights, sem,
    ) = refs
    mix_own, mix_other, ex_own, ex_other, sh_own, sh_other = weights
    copies = fetch(sources, weights, sem)
    rows, width = x_ref.shape
    ff = wide.shape[1]
    part = ff // 8
    own, other = halves(side_ref, width // 2)
    fown, fother = halves(side_ref, ff // 2)
    vec = whole_vectors(side_ref, mine_ref, theirs_ref, slice(0, 8))
    first = side_ref[0] == 0
    lines = [
        [ref[8 + r : 9 + r].astype(F32) for r in range(4)] for ref in (mine_ref, theirs_ref)
    ]
    ebias = jnp.concatenate(
        [jnp.where(first, a, b) for a, b in zip(*lines)]
        + [jnp.where(first, b, a) for a, b in zip(*lines)],
        axis=1,
    )
    att_s[...] = att_in[0:H].reshape(width, rows).T
    att_keep[...] = att_s[:, own]
    att_send[...] = att_s[:, other]
    copies[0].wait()
    copies[1].wait()
    middle = (
        x_ref[...].astype(F32)
        + (dot_nn(att_keep[...], mix_own[...]) + dot_nn(att_send[...], mix_other[...]))
        + vec[4:5]
    )
    unit, inv_std = normalise(middle)
    hid_s[...] = (unit * vec[5:6] + vec[6:7]).astype(BF16)
    hid_keep[...] = hid_s[:, own]
    hid_send[...] = hid_s[:, other]
    copies[2].wait()
    copies[3].wait()
    expanded = (
        dot_nn(hid_keep[...], ex_own[...])
        + dot_nn(hid_send[...], ex_other[...])
        + ebias
    )
    square = expanded * expanded
    bend = jnp.tanh(GELU_COEF * (expanded + GELU_CUBE * square * expanded))
    act_s[...] = (0.5 * expanded * (1.0 + bend)).astype(BF16)
    slope = 0.5 * (1.0 + bend) + 0.5 * expanded * (1.0 - bend * bend) * GELU_COEF * (
        1.0 + 3.0 * GELU_CUBE * square
    )
    act_keep[...] = act_s[:, fown]
    act_send[...] = act_s[:, fother]
    copies[4].wait()
    copies[5].wait()
    result = (
        middle
        + (dot_nn(act_keep[...], sh_own[...]) + dot_nn(act_send[...], sh_other[...]))
        + vec[7:8]
    )
    res_ref[...] = result.astype(BF16)
    upstream = cot_ref[...]
    cotb_ref[...] = upstream.astype(BF16)
    wide[:, fown] = dot_nt(cotb_ref[...], sh_own[...])
    wide[:, fother] = dot_nt(cotb_ref[...], sh_other[...])
    grad_expanded = wide[...] * slope
    esum = jnp.sum(grad_expanded, axis=0, keepdims=True)
    for r in range(4):
        low = esum[:, r * part : (r + 1) * part]
        high = esum[:, (4 + r) * part : (5 + r) * part]
        sums_keep[4 + r : 5 + r] = jnp.where(first, low, high)
        sums_send[4 + r : 5 + r] = jnp.where(first, high, low)
    ge_ref[...] = grad_expanded.astype(BF16)
    narrow[:, own] = dot_nt(ge_ref[...], ex_own[...])
    narrow[:, other] = dot_nt(ge_ref[...], ex_other[...])
    grad_hidden = narrow[...]
    sums = [jnp.sum(s, axis=0, keepdims=True) for s in (grad_hidden * unit, grad_hidden)]
    grad_middle = upstream + norm_back(grad_hidden * vec[5:6], unit, inv_std)
    gm_ref[...] = grad_middle
    gmb_ref[...] = grad_middle.astype(BF16)
    sums = [jnp.sum(grad_middle, axis=0, keepdims=True)] + sums
    sums += [jnp.sum(upstream, axis=0, keepdims=True)]
    split_sums(first, sums, sums_keep, sums_send)
    narrow[:, own] = dot_nt(gmb_ref[...], mix_own[...])
    narrow[:, other] = dot_nt(gmb_ref[...], mix_other[...])
    gsend_ref[0:H] = narrow[...].astype(BF16).T.reshape(H, HD, rows)
    for h in range(H, gsend_ref.shape[0]):
        gsend_ref[h] = jnp.zeros(gsend_ref.shape[1:], BF16)


def finish_kernel(
    side_ref, in_ref, x_ref, gm_ref, mine_ref, theirs_ref, hid_ref, own_ref, other_ref,
    grad_ref, sums_keep, sums_send, gj_ref, hid_keep, hid_send, narrow,
):
    rows, width = x_ref.shape
    own, other = halves(side_ref, width // 2)
    gain = whole_vectors(side_ref, mine_ref, theirs_ref, slice(0, 1))
    for k in range(3):
        gj_ref[:, k * width : (k + 1) * width] = (
            in_ref[0:H, k * HD : (k + 1) * HD, :].reshape(width, rows).T
        )
    hid_keep[...] = hid_ref[:, own]
    hid_send[...] = hid_ref[:, other]
    unit, inv_std = normalise(x_ref[...].astype(F32))
    narrow[:, own] = dot_nt(gj_ref[...], own_ref[...])
    narrow[:, other] = dot_nt(gj_ref[...], other_ref[...])
    grad_hidden = narrow[...]
    joint = gj_ref[...].astype(F32)
    sums = (grad_hidden * unit, grad_hidden, joint[:, :width], joint[:, 2 * width :])
    sums = [jnp.sum(s, axis=0, keepdims=True) for s in sums]
    split_sums(side_ref[0] == 0, sums, sums_keep, sums_send)
    grad_ref[...] = gm_ref[...] + norm_back(grad_hidden * gain, unit, inv_std)


def block_spans(a, rows, wide, paired, count):
    if paired:
        tall, wide = 2 * rows // count, wide // 2
        first, start = a // 2 * tall, a % 2 * wide
    else:
        tall = rows // count
        first, start = a * tall, 0
    return first, tall, [start + j * LANES for j in range(wide // LANES)]


def pack_kernel(paired, parts, meta_ref, *refs):
    weights = len(paired)
    ins, (keep_sums, came_sums) = refs[: 4 * weights], refs[4 * weights : 4 * weights + 2]
    outs, refs = refs[4 * weights + 2 :][: 2 * parts], refs[4 * weights + 2 + 2 * parts :]
    lefts, rights, (pk, extra) = refs[:-2:2], refs[1:-2:2], refs[-2:]
    count = pk.shape[0]
    for i, (left, right) in enumerate(zip(lefts, rights)):
        rows = left.shape[0] // 2
        for n, dst in enumerate((left, left, right, right)):
            dst[(n % 2) * rows : (n % 2 + 1) * rows] = ins[4 * i + n][...]
    extra[...] = jnp.zeros_like(extra)
    sums = keep_sums[...] + came_sums[...]
    each = sums.shape[1] // LANES
    for q in range(sums.shape[0] * each):
        extra[q // LINES, q % LINES : q % LINES + 1] = sums[
            q // each : q // each + 1, q % each * LANES : (q % each + 1) * LANES
        ]
    for k, order in enumerate(sum_orders(count, parts)):
        keep_ref, send_ref = outs[2 * k : 2 * k + 2]
        line = 0
        for left, right, pair in zip(lefts, rights, paired):
            wide = right.shape[1] // parts
            grad = dot_tn(left[...], right[:, k * wide : (k + 1) * wide]).astype(pk.dtype)
            for a in range(count):
                first, tall, starts = block_spans(a, grad.shape[0], wide, pair, count)
                for j, start in enumerate(starts):
                    pk[a, line + j * tall : line + (j + 1) * tall] = grad[
                        first : first + tall, start : start + LANES
                    ]
            line += tall * len(starts)
        for m in range(count):
            dst = keep_ref if m < count // 2 else send_ref
            a = relative_at(m, order) ^ meta_ref[1]
            dst[m % (count // 2), 0:line] = pk[a].astype(BF16)
            if k == 0:
                dst[m % (count // 2), line:] = extra[a].astype(BF16)


def unpack_kernel(paired, parts, meta_ref, *refs):
    weights = len(paired)
    near_far, refs = refs[: 2 * parts], refs[2 * parts :]
    outs, refs, (extra, sem) = refs[:weights], refs[weights:-2], refs[-2:]
    lines, scratch = refs[:-weights], refs[-weights:]
    half = near_far[0].shape[0]
    count = 2 * half
    copies = []
    for k, order in enumerate(sum_orders(count, parts)):
        for m in range(count):
            a = relative_at(m, order) ^ meta_ref[1]
            block = near_far[2 * k + m // half][m % half].astype(F32)
            line = 0
            for dst, pair in zip(scratch, paired):
                rows, wide = dst.shape[1:]
                first, tall, starts = block_spans(a, rows, wide, pair, count)
                for start in starts:
                    if pair:
                        start = pl.ds(pl.multiple_of(start, LANES), LANES)
                    else:
                        start = slice(start, start + LANES)
                    place = pl.ds(pl.multiple_of(first, 8), tall)
                    dst[k, place, start] = block[line : line + tall]
                    line += tall
            if k == 0:
                extra[a] = block[line:]
        for i, (src, dst) in enumerate(zip(scratch, outs)):
            size = src.shape[2]
            copy = pltpu.make_async_copy(
                src.at[k], dst.at[:, k * size : (k + 1) * size], sem.at[k, i]
            )
            copy.start()
            copies.append(copy)
    q = 0
    for line in lines:
        for start in range(0, line.shape[0], LANES):
            line[start : start + LANES] = extra[q // LINES, q % LINES, :]
            q += 1
    for copy in copies:
        copy.wait()


def stack_kernel(*refs):
    out_ref = refs[-1]
    row = 0
    for ref in refs[:-1]:
        line = ref[...].reshape(1, -1)
        for start in range(0, line.shape[1], out_ref.shape[1]):
            out_ref[row : row + 1] = line[:, start : start + out_ref.shape[1]]
            row += 1


SWAP = [(0, 1), (1, 0)]


def pieces(weight, group):
    if group == 2:
        return weight, lax.ppermute(weight, "fsdp", SWAP)
    full = lax.all_gather(weight, "fsdp", axis=0, tiled=True)
    half = full.shape[0] // 2
    return full[:half], full[half:]


def join_vector(vector, group, side):
    if group == 2:
        other = lax.ppermute(vector, "fsdp", SWAP)
        return jnp.where(
            side == 0,
            jnp.concatenate([vector, other], axis=1),
            jnp.concatenate([other, vector], axis=1),
        )
    return lax.all_gather(vector, "fsdp", axis=1, tiled=True)


def swap_side(part):
    return lax.ppermute(part, "fsdp", SWAP)


def rows_over_group(keep, send, right):
    left = jnp.concatenate([keep, send], axis=1)
    left = lax.all_to_all(left, "fsdp", split_axis=1, concat_axis=0, tiled=True)
    return dot_tn(left, lax.all_gather(right, "fsdp", axis=0, tiled=True))


def sums_over_group(keep, send, group):
    sums = jnp.concatenate([keep[:4], send[:4]], axis=1)
    width = sums.shape[1]
    if keep.shape[0] > 4:
        wide = jnp.concatenate([keep[4:].reshape(-1), send[4:].reshape(-1)])
        wide = wide.reshape(group, 4, width // group).swapaxes(0, 1).reshape(4, width)
        sums = jnp.concatenate([sums, wide], axis=0)
    return lax.psum_scatter(sums, "fsdp", scatter_dimension=1, tiled=True)


def swap_bit(part, bit, count):
    return lax.ppermute(part, "ctx", [(d, d ^ (1 << bit)) for d in range(count)])


def add_parts(left, right):
    return (left.astype(F32) + right.astype(F32)).astype(BF16)


class Flow:
    def __init__(self, keeps, sends, count):
        self.keeps, self.sends = list(keeps), list(sends)
        self.orders = sum_orders(count, len(self.keeps))
        self.bits = len(self.orders[0])
        self.step = 0

    def bit_row(self):
        at = self.bits - 1 - self.step if self.step < self.bits else self.step - self.bits
        return [order[at] for order in self.orders]

    def pending(self):
        parts = self.sends if self.step < self.bits else self.keeps
        row = self.bit_row()
        if len(set(row)) == 1:
            return [(jnp.concatenate(parts, axis=1), row[0])]
        return list(zip(parts, row))

    def accept(self, cames):
        if len(cames) == 1:
            sizes = [part.shape[1] for part in self.keeps]
            ends = [sum(sizes[: k + 1]) for k in range(len(sizes))]
            cames = [cames[0][:, end - size : end] for end, size in zip(ends, sizes)]
        half = cames[0].shape[0] // 2
        if self.step < self.bits - 1:
            self.sends = [add_parts(p[half:], c[half:]) for p, c in zip(self.keeps, cames)]
            self.keeps = [add_parts(p[:half], c[:half]) for p, c in zip(self.keeps, cames)]
        elif self.step == self.bits - 1:
            self.keeps = [add_parts(p, c) for p, c in zip(self.keeps, cames)]
        elif self.step == 2 * self.bits - 1:
            self.fars = cames
        else:
            self.keeps = [jnp.concatenate(pair, axis=0) for pair in zip(self.keeps, cames)]
        self.step += 1

    def over(self):
        return self.step == 2 * self.bits


def send_all(flow, count):
    return [swap_bit(part, bit, count) for part, bit in flow.pending()]


def advance(flow, count, inner=None, steps=0):
    cames = send_all(flow, count)
    for _ in range(steps - 1):
        inner.accept(lax.optimization_barrier(send_all(inner, count)))
    both = lax.optimization_barrier((cames, send_all(inner, count) if steps else []))
    flow.accept(both[0])
    if steps:
        inner.accept(both[1])


def plain_pack(weights, extra, index, count, parts):
    keeps, sends = [], []
    for k, order in enumerate(sum_orders(count, parts)):
        blocks = []
        for weight in weights:
            span = weight.shape[1] // parts
            for start in range(k * span, (k + 1) * span, LANES):
                blocks.append(weight[:, start : start + LANES].astype(BF16))
        flat = jnp.concatenate(blocks, axis=0)
        flat = flat.reshape(count, -1, LANES)
        if k == 0:
            flat = jnp.concatenate([flat, extra], axis=1)
        turn = jnp.array([relative_at(m, order) for m in range(count)], jnp.int32) ^ index
        flat = jnp.take(flat, turn, axis=0)
        keeps.append(flat[: count // 2])
        sends.append(flat[count // 2 :])
    return keeps, sends


def plain_unpack(keeps, fars, shapes, index, count, parts):
    columns = [[] for _ in shapes]
    extra = None
    for k, order in enumerate(sum_orders(count, parts)):
        flat = jnp.concatenate([keeps[k], fars[k]], axis=0)
        turn = place_of(jnp.arange(count, dtype=jnp.int32) ^ index, order)
        flat = jnp.take(flat, turn, axis=0).astype(F32)
        if k == 0:
            extra = flat[:, flat.shape[1] - LINES :]
            flat = flat[:, : flat.shape[1] - LINES]
        flat = flat.reshape(-1, LANES)
        first = 0
        for i, (rows, cols) in enumerate(shapes):
            for _ in range(cols // parts // LANES):
                columns[i].append(flat[first : first + rows])
                first += rows
    return [jnp.concatenate(c, axis=1) for c in columns], extra


def exchange(pairs, sums, group, count):
    if group != 2 or count != 16:
        return []
    args = []
    for keep, send, right in pairs:
        args += [keep, swap_side(send), right, swap_side(right)]
    return args + [sums[0], swap_side(sums[1])]


def pack(pairs, sums, args, paired, parts, meta, index, group, count):
    keep_sums, send_sums = sums
    if args:
        size = sum(keep.shape[1] * right.shape[1] for keep, _, right in pairs)
        block = size // parts // LANES // count
        half = count // 2
        rows = pairs[0][0].shape[0]
        kind = BF16 if block % 16 == 0 else F32
        outs = [
            ((half, block + (LINES if k // 2 == 0 else 0), LANES), BF16) for k in range(2 * parts)
        ]
        flows = call(
            functools.partial(pack_kernel, paired, parts), outs,
            [((2 * rows, a.shape[1]), BF16) for a in args[:-2:2]]
            + [((count, block, LANES), kind), ((count, LINES, LANES), F32)],
            "pack", 4 * rows * size, meta, *args,
        )
        return Flow(flows[::2], flows[1::2], count)
    extra = sums_over_group(keep_sums, send_sums, group).reshape(-1, LANES)
    extra = jnp.pad(extra, ((0, LINES * count - extra.shape[0]), (0, 0))).astype(BF16)
    extra = extra.reshape(count, LINES, LANES)
    weights = [rows_over_group(*pair) for pair in pairs]
    return Flow(*plain_pack(weights, extra, index, count, parts), count)


def unpack(flow, shapes, paired, vectors, meta, index, group, count):
    parts = len(flow.keeps)
    each = shapes[-1][0]
    if group == 2 and count == 16:
        near_far = [part for pair in zip(flow.keeps, flow.fars) for part in pair]
        outs = call(
            functools.partial(unpack_kernel, paired, parts),
            [(s, F32) for s in shapes] + [((n * each,), F32) for n in vectors],
            [((parts, r, c // parts), F32) for r, c in shapes]
            + [((count, LINES, LANES), F32), pltpu.SemaphoreType.DMA((parts, len(shapes)))],
            "unpack", 0, meta, *near_far, away_outs=len(shapes), limit=24,
        )
        return outs[: len(shapes)], outs[len(shapes) :]
    weights, extra = plain_unpack(flow.keeps, flow.fars, shapes, index, count, parts)
    ends = [sum(vectors[: k + 1]) * each for k in range(len(vectors))]
    flat = extra.reshape(-1)
    return weights, [flat[end - n * each : end] for end, n in zip(ends, vectors)]


def body(
    block_input, out_cotangent, block_position, first_gain, first_shift, qkv_weight, query_bias,
    value_bias, output_weight, output_bias, second_gain, second_shift, expand_weight, expand_bias,
    shrink_weight, shrink_bias,
):
    count = lax.axis_size("ctx")
    group = lax.axis_size("fsdp")
    rows, width = block_input.shape[1:]
    ff = expand_weight.shape[1]
    length = count * rows
    side = lax.axis_index("fsdp") if group == 2 else jnp.int32(0)
    index = lax.axis_index("ctx")
    half = width // 2
    three = 3 * HD
    each = width // group
    meta = jnp.stack([side, index]).astype(jnp.int32)
    table = block_position[0]
    places = jnp.arange(count, dtype=jnp.int32)
    slots = jnp.sum(
        jnp.where(table[None, :] == places[:, None], places[None, :], 0), axis=1
    ).astype(jnp.int32)
    x = block_input[0]
    vectors = (
        first_gain, first_shift, query_bias, value_bias, output_bias, second_gain, second_shift,
        shrink_bias,
    )
    if group == 2:
        (mine,) = call(
            stack_kernel, [((12, each), BF16)], [], "stack", 0, *vectors, expand_bias, smem=0
        )
        vec = mine, swap_side(mine)
    else:
        lines = lax.all_gather(jnp.stack(vectors), "fsdp", axis=1, tiled=True)
        wide = lax.all_gather(expand_bias, "fsdp", axis=0, tiled=True).reshape(2, 4, half)
        vec = [
            jnp.concatenate([lines[:, i * half : (i + 1) * half], wide[i]], axis=0)
            for i in range(2)
        ]
    qkv = pieces(qkv_weight, group)
    vec, qkv, output_weight, expand_weight, shrink_weight = lax.optimization_barrier(
        (vec, qkv, output_weight, expand_weight, shrink_weight)
    )
    mix = pieces(output_weight, group)
    expand = pieces(expand_weight, group)
    shrink = pieces(shrink_weight, group)
    size = width * ff

    hidden_a, qkv_send = call(
        project_kernel,
        [((rows, width), BF16), ((count, three, rows), BF16)],
        [], "project", 6 * rows * width * width,
        meta, x, *vec, *qkv,
    )
    qkv_here = lax.all_to_all(qkv_send, "ctx", 0, 0, tiled=True)
    att_send, log_total = call(
        attend_kernel,
        [((count, HD, rows), BF16), ((1, length), F32)],
        [((HD, length), BF16), ((length, HD), BF16), ((HD, length), BF16), ((HD, length), BF16)],
        "attend", 2 * length * length * HD,
        slots, qkv_here, limit=32,
    )
    att_here = lax.all_to_all(att_send, "ctx", 0, 0, tiled=True)
    (
        result, grad_middle, grad_send, keep_sums, send_sums, cot_b, act_keep, act_out, hid_keep,
        hid_out, ge_b, att_keep, att_out, gm_b,
    ) = call(
        middle_kernel,
        [
            ((rows, width), BF16), ((rows, width), F32), ((count, HD, rows), BF16),
            ((8, half), F32), ((8, half), F32), ((rows, width), BF16), ((rows, ff // 2), BF16),
            ((rows, ff // 2), BF16), ((rows, half), BF16), ((rows, half), BF16),
            ((rows, ff), BF16), ((rows, half), BF16), ((rows, half), BF16), ((rows, width), BF16),
        ],
        [
            ((rows, ff), F32), ((rows, ff), BF16), ((rows, width), BF16), ((rows, width), BF16),
            ((rows, width), F32),
        ]
        + [(w.shape, BF16) for w in (*mix, *expand, *shrink)]
        + [pltpu.SemaphoreType.DMA((6,))],
        "middle", 8 * rows * size + 4 * rows * width * width,
        meta, att_here, x, out_cotangent[0], *vec, *mix, *expand, *shrink, away=6,
    )
    grad_here = lax.all_to_all(grad_send, "ctx", 0, 0, tiled=True)

    early_kinds = (False, True, True)
    pairs = [(act_keep, act_out, cot_b), (hid_keep, hid_out, ge_b), (att_keep, att_out, gm_b)]
    sums = keep_sums, send_sums
    args = exchange(pairs, sums, group, count)
    early = pack(pairs, sums, args, early_kinds, 3, meta, index, group, count)
    early.keeps, early.sends, grad_here = lax.optimization_barrier(
        (early.keeps, early.sends, grad_here)
    )
    advance(early, count)
    (dqkv_send,) = call(
        attend_back_kernel,
        [((count, three, rows), BF16)],
        [
            ((HD, length), BF16), ((length, HD), BF16), ((HD, length), BF16),
            ((length, HD), BF16), ((length, HD), BF16), ((HD, length), BF16),
            ((length, HD), BF16), ((1, length), F32), ((HD, length), F32), ((HD, length), F32),
            ((HD, length), F32),
        ],
        "attend_back", 5 * length * length * HD,
        slots, qkv_here, att_send, grad_here, log_total, limit=32,
    )
    dqkv_here = lax.all_to_all(dqkv_send, "ctx", 0, 0, tiled=True)
    early.keeps, early.sends, _ = lax.optimization_barrier(
        (early.keeps, early.sends, dqkv_send)
    )
    advance(early, count)
    input_grad, keep_sums, send_sums, gj, hida_keep, hida_out = call(
        finish_kernel,
        [
            ((rows, width), F32), ((4, half), F32), ((4, half), F32), ((rows, 3 * width), BF16),
            ((rows, half), BF16), ((rows, half), BF16),
        ],
        [((rows, width), F32)],
        "finish", 6 * rows * width * width,
        meta, dqkv_here, x, grad_middle, *vec, hidden_a, *qkv,
    )
    pairs = [(hida_keep, hida_out, gj)]
    sums = keep_sums, send_sums
    args = exchange(pairs, sums, group, count)
    early.keeps, early.sends, args = lax.optimization_barrier((early.keeps, early.sends, args))
    advance(early, count)
    late = pack(pairs, sums, args, (False,), 2, meta, index, group, count)
    while not early.over():
        advance(early, count, late, 1 + (2 * early.bits - 1 > early.step >= 2 * early.bits - 3))
    (grad_shrink, grad_expand, grad_mix), sums = unpack(
        early, ((4 * each, width), (each, ff), (each, width)), early_kinds, (1, 1, 1, 1, 4), meta, index,
        group, count,
    )
    while not late.over():
        advance(late, count)
    (grad_qkv,), late_sums = unpack(
        late, ((each, 3 * width),), (False,), (1,) * 4, meta, index, group, count
    )
    return (
        result[None], input_grad[None], late_sums[0], late_sums[1], grad_qkv, late_sums[2],
        late_sums[3], grad_mix, sums[0], sums[1], sums[2], grad_expand, sums[4],
        grad_shrink, sums[3],
    )


def solution(mesh):
    block = P("fsdp", "ctx", None)
    vector, matrix = P("fsdp"), P("fsdp", None)
    return jax.shard_map(
        body,
        mesh=mesh,
        in_specs=(
            block, block, matrix, vector, vector, matrix, vector, vector, matrix, vector, vector,
            vector, matrix, vector, matrix, vector,
        ),
        out_specs=(
            block, block, vector, vector, matrix, vector, vector, matrix, vector, vector, vector,
            matrix, vector, matrix, vector,
        ),
        check_vma=False,
    )
```

```python
import functools

import jax
import jax.numpy as jnp
from jax import lax
from jax.experimental import pallas as pl
from jax.experimental.pallas import tpu as pltpu
from jax.sharding import PartitionSpec as P

H = 12
HD = 64
NORM_EPS = 1e-05
MASK_FLOOR = -1e30
GELU_COEF = 0.7978845608028654
GELU_CUBE = 0.044715
SCALE = HD ** (-0.5)
F32 = jnp.float32
BF16 = jnp.bfloat16
LANES = 128
LINES = 16
MIB = 1024 * 1024


def dot_nn(left, right):
    return lax.dot_general(left, right, (((1,), (0,)), ((), ())), preferred_element_type=F32)


def dot_nt(left, right):
    return lax.dot_general(left, right, (((1,), (1,)), ((), ())), preferred_element_type=F32)


def dot_tn(left, right):
    return lax.dot_general(left, right, (((0,), (0,)), ((), ())), preferred_element_type=F32)


def normalise(inputs):
    centred = inputs - jnp.mean(inputs, axis=-1, keepdims=True)
    inv_std = lax.rsqrt(jnp.mean(centred * centred, axis=-1, keepdims=True) + NORM_EPS)
    return centred * inv_std, inv_std


def norm_back(scaled, unit, inv_std):
    return inv_std * (
        scaled
        - jnp.mean(scaled, axis=-1, keepdims=True)
        - unit * jnp.mean(scaled * unit, axis=-1, keepdims=True)
    )


def whole_vectors(side_ref, mine_ref, theirs_ref, rows):
    mine, theirs = mine_ref[rows].astype(F32), theirs_ref[rows].astype(F32)
    first = side_ref[0] == 0
    left, right = jnp.where(first, mine, theirs), jnp.where(first, theirs, mine)
    return jnp.concatenate([left, right], axis=1)


def halves(side_ref, size):
    side = side_ref[0]
    own = pl.ds(pl.multiple_of(side * size, 128), size)
    other = pl.ds(pl.multiple_of((1 - side) * size, 128), size)
    return own, other


def call(kernel, outs, scratch, name, flops, *args, smem=1, away=0, away_outs=0, limit=56):
    vmem = pl.BlockSpec(memory_space=pltpu.VMEM)
    anywhere = pl.BlockSpec(memory_space=pl.ANY)
    specs = [pl.BlockSpec(memory_space=pltpu.SMEM)] * smem
    specs += [vmem] * (len(args) - smem - away) + [anywhere] * away
    moved = sum(a.size * a.dtype.itemsize for a in args)
    return pl.pallas_call(
        kernel,
        out_shape=[jax.ShapeDtypeStruct(s, d) for s, d in outs],
        in_specs=specs,
        out_specs=[anywhere] * away_outs + [vmem] * (len(outs) - away_outs),
        scratch_shapes=[pltpu.VMEM(*s) if isinstance(s, tuple) else s for s in scratch],
        compiler_params=pltpu.CompilerParams(vmem_limit_bytes=limit * MIB),
        cost_estimate=pl.CostEstimate(flops=flops, bytes_accessed=moved, transcendentals=0),
        name=name,
    )(*args)


def bits_of(count):
    return list(range(count.bit_length() - 1))


def sum_orders(count, parts):
    turn, last = bits_of(count)[:parts], bits_of(count)[parts:]
    return [list(reversed(turn[k:] + turn[:k] + last)) for k in range(parts)]


def place_of(r, order):
    place = 0
    for s, bit in enumerate(order):
        place = place | (((r >> bit) & 1) << s)
    return place


def relative_at(place, order):
    return sum(((place >> s) & 1) << bit for s, bit in enumerate(order))


def fetch(sources, targets, sem):
    copies = [
        pltpu.make_async_copy(src, dst, sem.at[i])
        for i, (src, dst) in enumerate(zip(sources, targets))
    ]
    for copy in copies:
        copy.start()
    return copies


def project_kernel(
    side_ref, x_ref, mine_ref, theirs_ref, own_ref, other_ref, hid_ref, send_ref
):
    rows, width = x_ref.shape
    own, other = halves(side_ref, width // 2)
    unit, _ = normalise(x_ref[...].astype(F32))
    vec = whole_vectors(side_ref, mine_ref, theirs_ref, slice(0, 8))
    hid_ref[...] = (unit * vec[0:1] + vec[1:2]).astype(BF16)
    joint = dot_nn(hid_ref[:, own], own_ref[...]) + dot_nn(hid_ref[:, other], other_ref[...])
    three = (
        (joint[:, :width] + vec[2:3]).astype(BF16),
        joint[:, width : 2 * width].astype(BF16),
        (joint[:, 2 * width :] + vec[3:4]).astype(BF16),
    )
    for k, part in enumerate(three):
        turned = part.T
        for h in range(H):
            send_ref[h, k * HD : (k + 1) * HD, :] = turned[h * HD : (h + 1) * HD]
    for h in range(H, send_ref.shape[0]):
        send_ref[h] = jnp.zeros(send_ref.shape[1:], BF16)


def attend_kernel(slot_ref, in_ref, out_ref, total_ref, q_t, k_n, v_t, o_t):
    count, _, rows = in_ref.shape
    tile = 512
    for p in range(count):
        slot = slot_ref[p]
        where = slice(p * rows, (p + 1) * rows)
        q_t[:, where] = in_ref[slot, 0:HD, :] * jnp.asarray(SCALE, BF16)
        k_n[where, :] = in_ref[slot, HD : 2 * HD, :].T
        v_t[:, where] = in_ref[slot, 2 * HD : 3 * HD, :]
    length = count * rows
    below = lax.broadcasted_iota(jnp.int32, (tile, tile), 0) <= lax.broadcasted_iota(
        jnp.int32, (tile, tile), 1
    )
    for i in range(length // tile):
        front, here = slice(0, i * tile), slice(i * tile, (i + 1) * tile)
        query = q_t[:, here]
        spans = [here] + [front] * (i > 0)
        scores = [dot_nn(k_n[span, :], query) for span in spans]
        scores[0] = jnp.where(below, scores[0], MASK_FLOOR)
        best = jnp.max(scores[0], axis=0, keepdims=True)
        for part in scores[1:]:
            best = jnp.maximum(best, jnp.max(part, axis=0, keepdims=True))
        weights = [jnp.exp(part - best) for part in scores]
        total = sum(jnp.sum(part, axis=0, keepdims=True) for part in weights)
        mixed = sum(dot_nn(v_t[:, s], w.astype(BF16)) for s, w in zip(spans, weights))
        o_t[:, here] = (mixed / total).astype(BF16)
        total_ref[:, here] = best + jnp.log(total)
    for p in range(count):
        out_ref[slot_ref[p]] = o_t[:, p * rows : (p + 1) * rows]


def attend_back_kernel(
    slot_ref, in_ref, att_ref, grad_ref, total_ref, out_ref,
    q_t, q_n, k_t, k_n, v_n, g_t, g_n, delta, dq_t, dk_t, dv_t,
):
    count, _, rows = in_ref.shape
    tile = 512
    for p in range(count):
        slot = slot_ref[p]
        where = slice(p * rows, (p + 1) * rows)
        query = in_ref[slot, 0:HD, :] * jnp.asarray(SCALE, BF16)
        q_t[:, where] = query
        q_n[where, :] = query.T
        key = in_ref[slot, HD : 2 * HD, :]
        k_t[:, where] = key
        k_n[where, :] = key.T
        v_n[where, :] = in_ref[slot, 2 * HD : 3 * HD, :].T
        grad = grad_ref[slot]
        g_t[:, where] = grad
        g_n[where, :] = grad.T
        delta[:, where] = jnp.sum(
            grad.astype(F32) * att_ref[slot].astype(F32), axis=0, keepdims=True
        )
    length = count * rows
    tiles = length // tile
    below = lax.broadcasted_iota(jnp.int32, (tile, tile), 0) <= lax.broadcasted_iota(
        jnp.int32, (tile, tile), 1
    )
    dq_t[...] = jnp.zeros_like(dq_t)
    for j in range(tiles):
        here = slice(j * tile, (j + 1) * tile)

        def step(i, state, masked=False, here=here):
            key_sum, value_sum = state
            span = slice(i * tile, (i + 1) * tile)
            scores = dot_nn(k_n[here, :], q_t[:, span])
            probs = jnp.exp(scores - total_ref[:, span])
            if masked:
                probs = jnp.where(below, probs, 0.0)
            prob_grad = dot_nn(v_n[here, :], g_t[:, span])
            score_grad = (probs * (prob_grad - delta[:, span])).astype(BF16)
            value_sum = value_sum + dot_nn(probs.astype(BF16), g_n[span, :])
            key_sum = key_sum + dot_nn(score_grad, q_n[span, :])
            dq_t[:, span] = dq_t[:, span] + dot_nn(k_t[:, here], score_grad)
            return key_sum, value_sum

        zero = jnp.zeros((tile, HD), F32)
        state = step(j, (zero, zero), masked=True)
        for i in range(j + 1, tiles):
            state = step(i, state)
        dk_t[:, here] = state[0].T
        dv_t[:, here] = state[1].T
    for p in range(count):
        slot = slot_ref[p]
        where = slice(p * rows, (p + 1) * rows)
        out_ref[slot, 0:HD, :] = (dq_t[:, where] * SCALE).astype(BF16)
        out_ref[slot, HD : 2 * HD, :] = dk_t[:, where].astype(BF16)
        out_ref[slot, 2 * HD : 3 * HD, :] = dv_t[:, where].astype(BF16)


def split_sums(first, sums, keep_ref, send_ref):
    for r, line in enumerate(sums):
        half = line.shape[1] // 2
        low, high = line[:, :half], line[:, half:]
        keep_ref[r : r + 1] = jnp.where(first, low, high)
        send_ref[r : r + 1] = jnp.where(first, high, low)


def middle_kernel(
    side_ref, att_in, x_ref, cot_ref, mine_ref, theirs_ref, *refs,
):
    sources, refs = refs[:6], refs[6:]
    (
        res_ref, gm_ref, gsend_ref, sums_keep, sums_send,
        cotb_ref, act_keep, act_send, hid_keep, hid_send, ge_ref, att_keep, att_send, gmb_ref,
        wide, act_s, hid_s, att_s, narrow, *weights, sem,
    ) = refs
    mix_own, mix_other, ex_own, ex_other, sh_own, sh_other = weights
    copies = fetch(sources, weights, sem)
    rows, width = x_ref.shape
    ff = wide.shape[1]
    part = ff // 8
    own, other = halves(side_ref, width // 2)
    fown, fother = halves(side_ref, ff // 2)
    vec = whole_vectors(side_ref, mine_ref, theirs_ref, slice(0, 8))
    first = side_ref[0] == 0
    lines = [
        [ref[8 + r : 9 + r].astype(F32) for r in range(4)] for ref in (mine_ref, theirs_ref)
    ]
    ebias = jnp.concatenate(
        [jnp.where(first, a, b) for a, b in zip(*lines)]
        + [jnp.where(first, b, a) for a, b in zip(*lines)],
        axis=1,
    )
    att_s[...] = att_in[0:H].reshape(width, rows).T
    att_keep[...] = att_s[:, own]
    att_send[...] = att_s[:, other]
    copies[0].wait()
    copies[1].wait()
    middle = (
        x_ref[...].astype(F32)
        + (dot_nn(att_keep[...], mix_own[...]) + dot_nn(att_send[...], mix_other[...]))
        + vec[4:5]
    )
    unit, inv_std = normalise(middle)
    hid_s[...] = (unit * vec[5:6] + vec[6:7]).astype(BF16)
    hid_keep[...] = hid_s[:, own]
    hid_send[...] = hid_s[:, other]
    copies[2].wait()
    copies[3].wait()
    expanded = (
        dot_nn(hid_keep[...], ex_own[...])
        + dot_nn(hid_send[...], ex_other[...])
        + ebias
    )
    square = expanded * expanded
    bend = jnp.tanh(GELU_COEF * (expanded + GELU_CUBE * square * expanded))
    act_s[...] = (0.5 * expanded * (1.0 + bend)).astype(BF16)
    slope = 0.5 * (1.0 + bend) + 0.5 * expanded * (1.0 - bend * bend) * GELU_COEF * (
        1.0 + 3.0 * GELU_CUBE * square
    )
    act_keep[...] = act_s[:, fown]
    act_send[...] = act_s[:, fother]
    copies[4].wait()
    copies[5].wait()
    result = (
        middle
        + (dot_nn(act_keep[...], sh_own[...]) + dot_nn(act_send[...], sh_other[...]))
        + vec[7:8]
    )
    res_ref[...] = result.astype(BF16)
    upstream = cot_ref[...]
    cotb_ref[...] = upstream.astype(BF16)
    wide[:, fown] = dot_nt(cotb_ref[...], sh_own[...])
    wide[:, fother] = dot_nt(cotb_ref[...], sh_other[...])
    grad_expanded = wide[...] * slope
    esum = jnp.sum(grad_expanded, axis=0, keepdims=True)
    for r in range(4):
        low = esum[:, r * part : (r + 1) * part]
        high = esum[:, (4 + r) * part : (5 + r) * part]
        sums_keep[4 + r : 5 + r] = jnp.where(first, low, high)
        sums_send[4 + r : 5 + r] = jnp.where(first, high, low)
    ge_ref[...] = grad_expanded.astype(BF16)
    narrow[:, own] = dot_nt(ge_ref[...], ex_own[...])
    narrow[:, other] = dot_nt(ge_ref[...], ex_other[...])
    grad_hidden = narrow[...]
    sums = [jnp.sum(s, axis=0, keepdims=True) for s in (grad_hidden * unit, grad_hidden)]
    grad_middle = upstream + norm_back(grad_hidden * vec[5:6], unit, inv_std)
    gm_ref[...] = grad_middle
    gmb_ref[...] = grad_middle.astype(BF16)
    sums = [jnp.sum(grad_middle, axis=0, keepdims=True)] + sums
    sums += [jnp.sum(upstream, axis=0, keepdims=True)]
    split_sums(first, sums, sums_keep, sums_send)
    narrow[:, own] = dot_nt(gmb_ref[...], mix_own[...])
    narrow[:, other] = dot_nt(gmb_ref[...], mix_other[...])
    gsend_ref[0:H] = narrow[...].astype(BF16).T.reshape(H, HD, rows)
    for h in range(H, gsend_ref.shape[0]):
        gsend_ref[h] = jnp.zeros(gsend_ref.shape[1:], BF16)


def finish_kernel(
    side_ref, in_ref, x_ref, gm_ref, mine_ref, theirs_ref, hid_ref, own_ref, other_ref,
    grad_ref, sums_keep, sums_send, gj_ref, hid_keep, hid_send, narrow,
):
    rows, width = x_ref.shape
    own, other = halves(side_ref, width // 2)
    gain = whole_vectors(side_ref, mine_ref, theirs_ref, slice(0, 1))
    for k in range(3):
        gj_ref[:, k * width : (k + 1) * width] = (
            in_ref[0:H, k * HD : (k + 1) * HD, :].reshape(width, rows).T
        )
    hid_keep[...] = hid_ref[:, own]
    hid_send[...] = hid_ref[:, other]
    unit, inv_std = normalise(x_ref[...].astype(F32))
    narrow[:, own] = dot_nt(gj_ref[...], own_ref[...])
    narrow[:, other] = dot_nt(gj_ref[...], other_ref[...])
    grad_hidden = narrow[...]
    joint = gj_ref[...].astype(F32)
    sums = (grad_hidden * unit, grad_hidden, joint[:, :width], joint[:, 2 * width :])
    sums = [jnp.sum(s, axis=0, keepdims=True) for s in sums]
    split_sums(side_ref[0] == 0, sums, sums_keep, sums_send)
    grad_ref[...] = gm_ref[...] + norm_back(grad_hidden * gain, unit, inv_std)


def block_spans(a, rows, wide, paired, count):
    if paired:
        tall, wide = 2 * rows // count, wide // 2
        first, start = a // 2 * tall, a % 2 * wide
    else:
        tall = rows // count
        first, start = a * tall, 0
    return first, tall, [start + j * LANES for j in range(wide // LANES)]


def pack_kernel(paired, parts, meta_ref, *refs):
    weights = len(paired)
    ins, (keep_sums, came_sums) = refs[: 4 * weights], refs[4 * weights : 4 * weights + 2]
    outs, refs = refs[4 * weights + 2 :][: 2 * parts], refs[4 * weights + 2 + 2 * parts :]
    lefts, rights, (pk, extra) = refs[:-2:2], refs[1:-2:2], refs[-2:]
    count = pk.shape[0]
    for i, (left, right) in enumerate(zip(lefts, rights)):
        rows = left.shape[0] // 2
        for n, dst in enumerate((left, left, right, right)):
            dst[(n % 2) * rows : (n % 2 + 1) * rows] = ins[4 * i + n][...]
    extra[...] = jnp.zeros_like(extra)
    sums = keep_sums[...] + came_sums[...]
    each = sums.shape[1] // LANES
    for q in range(sums.shape[0] * each):
        extra[q // LINES, q % LINES : q % LINES + 1] = sums[
            q // each : q // each + 1, q % each * LANES : (q % each + 1) * LANES
        ]
    for k, order in enumerate(sum_orders(count, parts)):
        keep_ref, send_ref = outs[2 * k : 2 * k + 2]
        line = 0
        for left, right, pair in zip(lefts, rights, paired):
            wide = right.shape[1] // parts
            grad = dot_tn(left[...], right[:, k * wide : (k + 1) * wide]).astype(pk.dtype)
            for a in range(count):
                first, tall, starts = block_spans(a, grad.shape[0], wide, pair, count)
                for j, start in enumerate(starts):
                    pk[a, line + j * tall : line + (j + 1) * tall] = grad[
                        first : first + tall, start : start + LANES
                    ]
            line += tall * len(starts)
        for m in range(count):
            dst = keep_ref if m < count // 2 else send_ref
            a = relative_at(m, order) ^ meta_ref[1]
            dst[m % (count // 2), 0:line] = pk[a].astype(BF16)
            if k == 0:
                dst[m % (count // 2), line:] = extra[a].astype(BF16)


def unpack_kernel(paired, parts, meta_ref, *refs):
    weights = len(paired)
    near_far, refs = refs[: 2 * parts], refs[2 * parts :]
    outs, refs, (extra, sem) = refs[:weights], refs[weights:-2], refs[-2:]
    lines, scratch = refs[:-weights], refs[-weights:]
    half = near_far[0].shape[0]
    count = 2 * half
    copies = []
    for k, order in enumerate(sum_orders(count, parts)):
        for m in range(count):
            a = relative_at(m, order) ^ meta_ref[1]
            block = near_far[2 * k + m // half][m % half].astype(F32)
            line = 0
            for dst, pair in zip(scratch, paired):
                rows, wide = dst.shape[1:]
                first, tall, starts = block_spans(a, rows, wide, pair, count)
                for start in starts:
                    if pair:
                        start = pl.ds(pl.multiple_of(start, LANES), LANES)
                    else:
                        start = slice(start, start + LANES)
                    place = pl.ds(pl.multiple_of(first, 8), tall)
                    dst[k, place, start] = block[line : line + tall]
                    line += tall
            if k == 0:
                extra[a] = block[line:]
        for i, (src, dst) in enumerate(zip(scratch, outs)):
            size = src.shape[2]
            copy = pltpu.make_async_copy(
                src.at[k], dst.at[:, k * size : (k + 1) * size], sem.at[k, i]
            )
            copy.start()
            copies.append(copy)
    q = 0
    for line in lines:
        for start in range(0, line.shape[0], LANES):
            line[start : start + LANES] = extra[q // LINES, q % LINES, :]
            q += 1
    for copy in copies:
        copy.wait()


def stack_kernel(*refs):
    out_ref = refs[-1]
    row = 0
    for ref in refs[:-1]:
        line = ref[...].reshape(1, -1)
        for start in range(0, line.shape[1], out_ref.shape[1]):
            out_ref[row : row + 1] = line[:, start : start + out_ref.shape[1]]
            row += 1


SWAP = [(0, 1), (1, 0)]


def pieces(weight, group):
    if group == 2:
        return weight, lax.ppermute(weight, "fsdp", SWAP)
    full = lax.all_gather(weight, "fsdp", axis=0, tiled=True)
    half = full.shape[0] // 2
    return full[:half], full[half:]


def join_vector(vector, group, side):
    if group == 2:
        other = lax.ppermute(vector, "fsdp", SWAP)
        return jnp.where(
            side == 0,
            jnp.concatenate([vector, other], axis=1),
            jnp.concatenate([other, vector], axis=1),
        )
    return lax.all_gather(vector, "fsdp", axis=1, tiled=True)


def swap_side(part):
    return lax.ppermute(part, "fsdp", SWAP)


def rows_over_group(keep, send, right):
    left = jnp.concatenate([keep, send], axis=1)
    left = lax.all_to_all(left, "fsdp", split_axis=1, concat_axis=0, tiled=True)
    return dot_tn(left, lax.all_gather(right, "fsdp", axis=0, tiled=True))


def sums_over_group(keep, send, group):
    sums = jnp.concatenate([keep[:4], send[:4]], axis=1)
    width = sums.shape[1]
    if keep.shape[0] > 4:
        wide = jnp.concatenate([keep[4:].reshape(-1), send[4:].reshape(-1)])
        wide = wide.reshape(group, 4, width // group).swapaxes(0, 1).reshape(4, width)
        sums = jnp.concatenate([sums, wide], axis=0)
    return lax.psum_scatter(sums, "fsdp", scatter_dimension=1, tiled=True)


def swap_bit(part, bit, count):
    return lax.ppermute(part, "ctx", [(d, d ^ (1 << bit)) for d in range(count)])


def add_parts(left, right):
    return (left.astype(F32) + right.astype(F32)).astype(BF16)


class Flow:
    def __init__(self, keeps, sends, count):
        self.keeps, self.sends = list(keeps), list(sends)
        self.orders = sum_orders(count, len(self.keeps))
        self.bits = len(self.orders[0])
        self.step = 0

    def bit_row(self):
        at = self.bits - 1 - self.step if self.step < self.bits else self.step - self.bits
        return [order[at] for order in self.orders]

    def pending(self):
        parts = self.sends if self.step < self.bits else self.keeps
        row = self.bit_row()
        if len(set(row)) == 1:
            return [(jnp.concatenate(parts, axis=1), row[0])]
        return list(zip(parts, row))

    def accept(self, cames):
        if len(cames) == 1:
            sizes = [part.shape[1] for part in self.keeps]
            ends = [sum(sizes[: k + 1]) for k in range(len(sizes))]
            cames = [cames[0][:, end - size : end] for end, size in zip(ends, sizes)]
        half = cames[0].shape[0] // 2
        if self.step < self.bits - 1:
            self.sends = [add_parts(p[half:], c[half:]) for p, c in zip(self.keeps, cames)]
            self.keeps = [add_parts(p[:half], c[:half]) for p, c in zip(self.keeps, cames)]
        elif self.step == self.bits - 1:
            self.keeps = [add_parts(p, c) for p, c in zip(self.keeps, cames)]
        elif self.step == 2 * self.bits - 1:
            self.fars = cames
        else:
            self.keeps = [jnp.concatenate(pair, axis=0) for pair in zip(self.keeps, cames)]
        self.step += 1

    def over(self):
        return self.step == 2 * self.bits


def send_all(flow, count):
    return [swap_bit(part, bit, count) for part, bit in flow.pending()]


def advance(flow, count, inner=None, steps=0):
    cames = send_all(flow, count)
    for _ in range(steps - 1):
        inner.accept(lax.optimization_barrier(send_all(inner, count)))
    both = lax.optimization_barrier((cames, send_all(inner, count) if steps else []))
    flow.accept(both[0])
    if steps:
        inner.accept(both[1])


def plain_pack(weights, extra, index, count, parts):
    keeps, sends = [], []
    for k, order in enumerate(sum_orders(count, parts)):
        blocks = []
        for weight in weights:
            span = weight.shape[1] // parts
            for start in range(k * span, (k + 1) * span, LANES):
                blocks.append(weight[:, start : start + LANES].astype(BF16))
        flat = jnp.concatenate(blocks, axis=0)
        flat = flat.reshape(count, -1, LANES)
        if k == 0:
            flat = jnp.concatenate([flat, extra], axis=1)
        turn = jnp.array([relative_at(m, order) for m in range(count)], jnp.int32) ^ index
        flat = jnp.take(flat, turn, axis=0)
        keeps.append(flat[: count // 2])
        sends.append(flat[count // 2 :])
    return keeps, sends


def plain_unpack(keeps, fars, shapes, index, count, parts):
    columns = [[] for _ in shapes]
    extra = None
    for k, order in enumerate(sum_orders(count, parts)):
        flat = jnp.concatenate([keeps[k], fars[k]], axis=0)
        turn = place_of(jnp.arange(count, dtype=jnp.int32) ^ index, order)
        flat = jnp.take(flat, turn, axis=0).astype(F32)
        if k == 0:
            extra = flat[:, flat.shape[1] - LINES :]
            flat = flat[:, : flat.shape[1] - LINES]
        flat = flat.reshape(-1, LANES)
        first = 0
        for i, (rows, cols) in enumerate(shapes):
            for _ in range(cols // parts // LANES):
                columns[i].append(flat[first : first + rows])
                first += rows
    return [jnp.concatenate(c, axis=1) for c in columns], extra


def exchange(pairs, sums, group, count):
    if group != 2 or count != 16:
        return []
    args = []
    for keep, send, right in pairs:
        args += [keep, swap_side(send), right, swap_side(right)]
    return args + [sums[0], swap_side(sums[1])]


def pack(pairs, sums, args, paired, parts, meta, index, group, count):
    keep_sums, send_sums = sums
    if args:
        size = sum(keep.shape[1] * right.shape[1] for keep, _, right in pairs)
        block = size // parts // LANES // count
        half = count // 2
        rows = pairs[0][0].shape[0]
        kind = BF16 if block % 16 == 0 else F32
        outs = [
            ((half, block + (LINES if k // 2 == 0 else 0), LANES), BF16) for k in range(2 * parts)
        ]
        flows = call(
            functools.partial(pack_kernel, paired, parts), outs,
            [((2 * rows, a.shape[1]), BF16) for a in args[:-2:2]]
            + [((count, block, LANES), kind), ((count, LINES, LANES), F32)],
            "pack", 4 * rows * size, meta, *args, limit=24 if parts == 2 else 56,
        )
        return Flow(flows[::2], flows[1::2], count)
    extra = sums_over_group(keep_sums, send_sums, group).reshape(-1, LANES)
    extra = jnp.pad(extra, ((0, LINES * count - extra.shape[0]), (0, 0))).astype(BF16)
    extra = extra.reshape(count, LINES, LANES)
    weights = [rows_over_group(*pair) for pair in pairs]
    return Flow(*plain_pack(weights, extra, index, count, parts), count)


def unpack(flow, shapes, paired, vectors, meta, index, group, count):
    parts = len(flow.keeps)
    each = shapes[-1][0]
    if group == 2 and count == 16:
        near_far = [part for pair in zip(flow.keeps, flow.fars) for part in pair]
        outs = call(
            functools.partial(unpack_kernel, paired, parts),
            [(s, F32) for s in shapes] + [((n * each,), F32) for n in vectors],
            [((parts, r, c // parts), F32) for r, c in shapes]
            + [((count, LINES, LANES), F32), pltpu.SemaphoreType.DMA((parts, len(shapes)))],
            "unpack", 0, meta, *near_far, away_outs=len(shapes), limit=24,
        )
        return outs[: len(shapes)], outs[len(shapes) :]
    weights, extra = plain_unpack(flow.keeps, flow.fars, shapes, index, count, parts)
    ends = [sum(vectors[: k + 1]) * each for k in range(len(vectors))]
    flat = extra.reshape(-1)
    return weights, [flat[end - n * each : end] for end, n in zip(ends, vectors)]


def body(
    block_input, out_cotangent, block_position, first_gain, first_shift, qkv_weight, query_bias,
    value_bias, output_weight, output_bias, second_gain, second_shift, expand_weight, expand_bias,
    shrink_weight, shrink_bias,
):
    count = lax.axis_size("ctx")
    group = lax.axis_size("fsdp")
    rows, width = block_input.shape[1:]
    ff = expand_weight.shape[1]
    length = count * rows
    side = lax.axis_index("fsdp") if group == 2 else jnp.int32(0)
    index = lax.axis_index("ctx")
    half = width // 2
    three = 3 * HD
    each = width // group
    meta = jnp.stack([side, index]).astype(jnp.int32)
    table = block_position[0]
    places = jnp.arange(count, dtype=jnp.int32)
    slots = jnp.sum(
        jnp.where(table[None, :] == places[:, None], places[None, :], 0), axis=1
    ).astype(jnp.int32)
    x = block_input[0]
    vectors = (
        first_gain, first_shift, query_bias, value_bias, output_bias, second_gain, second_shift,
        shrink_bias,
    )
    if group == 2:
        (mine,) = call(
            stack_kernel, [((12, each), BF16)], [], "stack", 0, *vectors, expand_bias, smem=0
        )
        vec = mine, swap_side(mine)
    else:
        lines = lax.all_gather(jnp.stack(vectors), "fsdp", axis=1, tiled=True)
        wide = lax.all_gather(expand_bias, "fsdp", axis=0, tiled=True).reshape(2, 4, half)
        vec = [
            jnp.concatenate([lines[:, i * half : (i + 1) * half], wide[i]], axis=0)
            for i in range(2)
        ]
    qkv = pieces(qkv_weight, group)
    vec, qkv, output_weight, expand_weight, shrink_weight = lax.optimization_barrier(
        (vec, qkv, output_weight, expand_weight, shrink_weight)
    )
    mix = pieces(output_weight, group)
    expand = pieces(expand_weight, group)
    shrink = pieces(shrink_weight, group)
    size = width * ff

    hidden_a, qkv_send = call(
        project_kernel,
        [((rows, width), BF16), ((count, three, rows), BF16)],
        [], "project", 6 * rows * width * width,
        meta, x, *vec, *qkv,
    )
    qkv_here = lax.all_to_all(qkv_send, "ctx", 0, 0, tiled=True)
    att_send, log_total = call(
        attend_kernel,
        [((count, HD, rows), BF16), ((1, length), F32)],
        [((HD, length), BF16), ((length, HD), BF16), ((HD, length), BF16), ((HD, length), BF16)],
        "attend", 2 * length * length * HD,
        slots, qkv_here, limit=32,
    )
    att_here = lax.all_to_all(att_send, "ctx", 0, 0, tiled=True)
    (
        result, grad_middle, grad_send, keep_sums, send_sums, cot_b, act_keep, act_out, hid_keep,
        hid_out, ge_b, att_keep, att_out, gm_b,
    ) = call(
        middle_kernel,
        [
            ((rows, width), BF16), ((rows, width), F32), ((count, HD, rows), BF16),
            ((8, half), F32), ((8, half), F32), ((rows, width), BF16), ((rows, ff // 2), BF16),
            ((rows, ff // 2), BF16), ((rows, half), BF16), ((rows, half), BF16),
            ((rows, ff), BF16), ((rows, half), BF16), ((rows, half), BF16), ((rows, width), BF16),
        ],
        [
            ((rows, ff), F32), ((rows, ff), BF16), ((rows, width), BF16), ((rows, width), BF16),
            ((rows, width), F32),
        ]
        + [(w.shape, BF16) for w in (*mix, *expand, *shrink)]
        + [pltpu.SemaphoreType.DMA((6,))],
        "middle", 8 * rows * size + 4 * rows * width * width,
        meta, att_here, x, out_cotangent[0], *vec, *mix, *expand, *shrink, away=6,
    )
    grad_here = lax.all_to_all(grad_send, "ctx", 0, 0, tiled=True)

    early_kinds = (False, True, True)
    pairs = [(act_keep, act_out, cot_b), (hid_keep, hid_out, ge_b), (att_keep, att_out, gm_b)]
    sums = keep_sums, send_sums
    args = exchange(pairs, sums, group, count)
    early = pack(pairs, sums, args, early_kinds, 3, meta, index, group, count)
    early.keeps, early.sends, grad_here = lax.optimization_barrier(
        (early.keeps, early.sends, grad_here)
    )
    advance(early, count)
    (dqkv_send,) = call(
        attend_back_kernel,
        [((count, three, rows), BF16)],
        [
            ((HD, length), BF16), ((length, HD), BF16), ((HD, length), BF16),
            ((length, HD), BF16), ((length, HD), BF16), ((HD, length), BF16),
            ((length, HD), BF16), ((1, length), F32), ((HD, length), F32), ((HD, length), F32),
            ((HD, length), F32),
        ],
        "attend_back", 5 * length * length * HD,
        slots, qkv_here, att_send, grad_here, log_total, limit=32,
    )
    dqkv_here = lax.all_to_all(dqkv_send, "ctx", 0, 0, tiled=True)
    early.keeps, early.sends, _ = lax.optimization_barrier(
        (early.keeps, early.sends, dqkv_send)
    )
    advance(early, count)
    input_grad, keep_sums, send_sums, gj, hida_keep, hida_out = call(
        finish_kernel,
        [
            ((rows, width), F32), ((4, half), F32), ((4, half), F32), ((rows, 3 * width), BF16),
            ((rows, half), BF16), ((rows, half), BF16),
        ],
        [((rows, width), F32)],
        "finish", 6 * rows * width * width,
        meta, dqkv_here, x, grad_middle, *vec, hidden_a, *qkv,
    )
    pairs = [(hida_keep, hida_out, gj)]
    sums = keep_sums, send_sums
    args = exchange(pairs, sums, group, count)
    early.keeps, early.sends, args = lax.optimization_barrier((early.keeps, early.sends, args))
    advance(early, count)
    late = pack(pairs, sums, args, (False,), 2, meta, index, group, count)
    while not early.over():
        advance(early, count, late, 1 + (2 * early.bits - 2 > early.step >= 2 * early.bits - 4))
    (grad_shrink, grad_expand, grad_mix), sums = unpack(
        early, ((4 * each, width), (each, ff), (each, width)), early_kinds, (1, 1, 1, 1, 4), meta, index,
        group, count,
    )
    while not late.over():
        advance(late, count)
    (grad_qkv,), late_sums = unpack(
        late, ((each, 3 * width),), (False,), (1,) * 4, meta, index, group, count
    )
    return (
        result[None], input_grad[None], late_sums[0], late_sums[1], grad_qkv, late_sums[2],
        late_sums[3], grad_mix, sums[0], sums[1], sums[2], grad_expand, sums[4],
        grad_shrink, sums[3],
    )


def solution(mesh):
    block = P("fsdp", "ctx", None)
    vector, matrix = P("fsdp"), P("fsdp", None)
    return jax.shard_map(
        body,
        mesh=mesh,
        in_specs=(
            block, block, matrix, vector, vector, matrix, vector, vector, matrix, vector, vector,
            vector, matrix, vector, matrix, vector,
        ),
        out_specs=(
            block, block, vector, vector, matrix, vector, vector, matrix, vector, vector, vector,
            matrix, vector, matrix, vector,
        ),
        check_vma=False,
    )
```
